32 devices in a mesh: tm: 4 (over x, core), cell: 8 (over z, y).
Axes of the slice: x: 2, y: 2, z: 4, core: 2. Of those that a mesh axis runs over, the one named last changes fastest.
Arguments:
- sensitivity: bfloat16 [2048, 4, 4096], P(None, 'tm', 'cell'), may hold values from -0.1875 to 0.1875
- duals: bfloat16 [2048, 128], P(('tm', 'cell')), may hold values from -6 to 6
- time_cov: float32 [4, 4], replicated, may hold values from 0.05 to 0.5
- cell_coords: int32 [2, 4096], P(None, 'cell'), may hold values from 0 to 127, as said below
- obs_time: int32 [2048], replicated, may hold values from 0 to 3
- obs_owner: int32 [2048], replicated, may hold values from 0 to 2047, each once
Outputs:
- product: float32 [2048, 128], P(('tm', 'cell'))
The draws below stay inside these ranges and needn't reach their ends.
Inputs may be any that keep to these rules, and one draw needn't show every extreme that they name: `cell_coords`: every cell has its own grid position; rows lie below 32 and columns below 128. `obs_owner`: every observation stands in exactly one slot.
All inputs are finite; a program needn't handle non-finite values.
Results may differ from the reference program's by a relative error of at most 0.0049.
Values may be sent and summed in bfloat16 or wider, within the bound.
A program may use at most 64 MiB of HBM per device.

```python
import jax
import jax.numpy as jnp
from jax import lax

OBS = 2048
REALS = 128
GRID_COLS = 128
LSCALE = 4
TIMES = 4
CELLS = 4096


def draw_cell_coords(key, part):
    placed = jax.random.permutation(jax.random.fold_in(key, 17), CELLS).astype(jnp.int32)
    return jnp.stack([placed // GRID_COLS, placed % GRID_COLS]).astype(jnp.int32)


def plant(drawn, stream_key, low, largest):
    longest = drawn.shape.index(max(drawn.shape))
    spots = []
    for shift in (0, 1):
        where = [jax.random.randint(jax.random.fold_in(stream_key, axis), (), 0, length) for axis, length in enumerate(drawn.shape)]
        where[longest] = (where[longest] + shift) % drawn.shape[longest]
        spots.append(tuple(where))
    return drawn.at[spots[0]].set(low).at[spots[1]].set(largest)


def raised(array, stream_key, source, target, blocks, factor):
    owner, partner = [(jnp.arange(array.shape[axis_at]) // (array.shape[axis_at] // blocks)).reshape([-1 if axis == axis_at else 1 for axis in range(array.ndim)]) for axis_at in (source, target)]
    chosen = jax.random.permutation(stream_key, blocks)[partner]
    strong = (owner == chosen) | (owner == (partner + blocks // 2) % blocks)
    return jnp.where(strong, factor * array, array)


def levels(own_key, shape, cuts, least, high):
    def one(dim, parts):
        draws = jax.random.uniform(jax.random.fold_in(jax.random.fold_in(own_key, 6), dim), (parts,), jnp.float32, least / len(cuts), high / len(cuts))
        return jnp.repeat(jnp.exp(draws), shape[dim] // parts).reshape((-1,) + (1,) * (len(shape) - dim - 1))

    gain = one(*cuts[0])
    for cut in cuts[1:]:
        gain = gain * one(*cut)
    return gain


def normal_values(stream_key, shape, deviation, limit, cuts=(), kind=jnp.bfloat16):
    drawn = jax.random.normal(stream_key, shape, jnp.float32) * deviation
    if len(cuts) > 0:
        drawn = levels(stream_key, shape, cuts, -0.22, 0.18) * drawn
    return jnp.clip(drawn, min=-limit, max=limit).astype(kind)


def gaussian_with(key, dims, scale, reach, shards, heavy, kind=jnp.bfloat16):
    array = scale * jax.random.normal(key, dims, jnp.float32)
    if shards:
        array = array * levels(key, dims, shards, -0.22, 0.18)
    return jnp.clip(raised(array, jax.random.fold_in(key, 3), *heavy), -reach, reach).astype(kind)


def setup_inputs(seed: int = 0) -> dict:
    splits = jax.random.split(jax.random.key(seed), 7)
    return {
        "sensitivity": gaussian_with(splits[0], (OBS, TIMES, CELLS), OBS ** -0.5, 0.1875, ((1, 4), (2, 8)), (2, 0, 8, 2.0)),
        "duals": normal_values(splits[1], (OBS, REALS), 1.0, 6.0, ((0, 32),)),
        "time_cov": jnp.clip(jax.random.uniform(splits[2], (TIMES, TIMES), jnp.float32, 0.05, 0.5), 0.05, 0.5),
        "cell_coords": draw_cell_coords(jax.random.fold_in(splits[6], 71), 0),
        "obs_time": plant(jax.random.randint(splits[4], (OBS,), 0, TIMES), jax.random.fold_in(splits[4], 1), 0, TIMES - 1).astype(jnp.int32),
        "obs_owner": jax.random.permutation(splits[5], OBS).astype(jnp.int32),
    }


def covariance(left_coords, right_coords):
    row_gap = (left_coords[0][:, None] - right_coords[0][None, :]).astype(jnp.float32)
    col_gap = (left_coords[1][:, None] - right_coords[1][None, :]).astype(jnp.float32)
    distance = jnp.sqrt(row_gap * row_gap + col_gap * col_gap)
    return (jnp.exp(-distance / LSCALE) / (8.0 * LSCALE)).astype(jnp.bfloat16)

def reference(sensitivity, duals, time_cov, cell_coords, obs_time, obs_owner):
    time_index = jnp.arange(TIMES, dtype=jnp.int32)
    live = time_index[None, :, None] <= obs_time[:, None, None]
    masked = jnp.where(live, sensitivity, jnp.zeros((), jnp.bfloat16))
    flattened = masked.reshape(OBS, TIMES * CELLS)
    adjoint = jnp.dot(flattened.T, duals, preferred_element_type=jnp.float32).astype(jnp.bfloat16)
    adjoint_f = adjoint.reshape(TIMES, CELLS, REALS).astype(jnp.float32)
    mixed = jnp.einsum('st,tcr->scr', time_cov, adjoint_f, precision=lax.Precision.HIGHEST).astype(jnp.bfloat16)
    columns = mixed.transpose(1, 0, 2).reshape(CELLS, TIMES * REALS)
    width = min(512, CELLS)
    starts = jnp.arange(0, CELLS, width, dtype=jnp.int32)

    def row_block(offset):
        left_coords = lax.dynamic_slice_in_dim(cell_coords, offset, width, 1)
        kernel = covariance(left_coords, cell_coords)
        return jnp.dot(kernel, columns, preferred_element_type=jnp.float32).astype(jnp.bfloat16)
    weighted = lax.map(row_block, starts).reshape(CELLS, TIMES, REALS)
    weighted_flat = weighted.transpose(1, 0, 2).reshape(TIMES * CELLS, REALS)
    forward = jnp.dot(flattened, weighted_flat, preferred_element_type=jnp.float32)
    return forward[obs_owner]
```

```python
import functools

import jax
import jax.numpy as jnp
from jax import lax
from jax.experimental import pallas as pl
from jax.experimental.pallas import tpu as pltpu
from jax.sharding import PartitionSpec as P

LSCALE = 4
LANES = 128
HALVES = 2
PICK_ROWS = 256
QUARTERS = 4
FILL = (0, 3, 3, 1, 1)
MESH = pl.DeviceIdType.MESH
BF16 = jnp.bfloat16
F32 = jnp.float32


def remote(src, dst, sems, index, device):
    send, recv = sems
    return pltpu.make_async_remote_copy(
        src_ref=src, dst_ref=dst, send_sem=send.at[index], recv_sem=recv.at[index],
        device_id=device, device_id_type=MESH,
    )


def column_of(row):
    return jnp.broadcast_to(row, (LANES, row.shape[1])).T


def ring_kernel(cfg, sens_hbm, duals_ref, cov_ref, coords_ref, time_ref, owner_ref, out_ref, *s):
    n_hi, n_cell, gather, scatter = cfg
    n_tm = 2 * n_hi
    (sens, full, coords_all, mask_t, picked, row_b, col_b, own_b, ids, cov_k, adj, held, acc,
     core_out, core_in, x_out, x_in, total, cell_out, cell_in, local_sem, *pairs) = s
    co, ac, ax, ap, bx, bp, ring_r, ring_l, dp, dx, dc = zip(pairs[0::2], pairs[1::2])
    obs, cells = sens.shape
    rows = duals_ref.shape[0]
    half = cells // HALVES
    quarter = cells // QUARTERS

    tm = lax.axis_index("tm")
    cell = lax.axis_index("cell")
    hi, core = tm // 2, tm % 2
    partner = (hi * 2 + (1 - core), cell)

    def hi_at(q):
        return lax.rem(hi + q + n_hi, n_hi)

    def x_peer(q):
        return (hi_at(q) * 2 + core, cell)

    def cell_at(k):
        return lax.rem(cell + k + n_cell, n_cell)

    load = pltpu.make_async_copy(sens_hbm, sens, local_sem)
    load.start()

    barrier = pltpu.get_barrier_semaphore()
    peers = [(tm, cell_at(k)) for k in range(1, n_cell)] + [x_peer(q) for q in range(1, n_hi)] + [partner]
    for peer in peers:
        pl.semaphore_signal(barrier, inc=1, device_id=peer, device_id_type=MESH)
    coords_all[cell] = coords_ref[...]
    row_b[...] = column_of(coords_ref[0:1, :].astype(F32))
    col_b[...] = column_of(coords_ref[1:2, :].astype(F32))
    own_b[...] = column_of(owner_ref[...].astype(F32))
    live = tm <= time_ref[...]
    ids[...] = jnp.where(live, lax.broadcasted_iota(jnp.int32, (1, obs), 1), -1).astype(F32)

    def covariance_block(c):
        @pl.loop(0, cells // LANES)
        def _(j):
            lanes = pl.ds(pl.multiple_of(j * LANES, LANES), LANES)
            row_gap = row_b[...] - coords_all[c, 0:1, lanes].astype(F32)
            col_gap = col_b[...] - coords_all[c, 1:2, lanes].astype(F32)
            distance = jnp.sqrt(row_gap * row_gap + col_gap * col_gap)
            cov_k[c, :, lanes] = (jnp.exp(-distance / LSCALE) / (8.0 * LSCALE)).astype(BF16)

    def pick(i):
        at = slice(i * PICK_ROWS, (i + 1) * PICK_ROWS)
        owned = own_b[at, :]
        hot = [
            jnp.where(owned == ids[:, j * LANES:(j + 1) * LANES], 1.0, 0.0).astype(BF16)
            for j in range(obs // LANES)
        ]
        picked[at, :] = jnp.dot(
            jnp.concatenate(hot, axis=1), sens[...], preferred_element_type=F32
        ).astype(BF16)

    fillers = [functools.partial(pick, i) for i in range(obs // PICK_ROWS)]

    def fill(count):
        for _ in range(count):
            if fillers:
                fillers.pop(0)()

    covariance_block(cell)
    load.wait()

    @pl.loop(0, obs // PICK_ROWS)
    def _(i):
        at = pl.ds(pl.multiple_of(i * PICK_ROWS, PICK_ROWS), PICK_ROWS)
        alive = jnp.where(ids[:, at] >= 0.0, 1.0, 0.0).astype(BF16)
        mask_t[:, at] = sens[at, :].T * alive

    fill(FILL[0])
    pl.semaphore_wait(barrier, len(peers))

    sent = []

    def go(copy):
        copy.start()
        sent.append(copy)
        return copy

    co_copies = {}
    for k in range(1, n_cell):
        co_copies[k] = go(remote(coords_ref, coords_all.at[cell], co, k, (tm, cell_at(k))))

    def block(t, c):
        return full.at[t * n_cell + c]

    cell_copies, x_copies, core_copies = {}, {}, {}

    def forward_x(src, k):
        for q in range(1, n_hi):
            x_copies[q, k] = go(remote(src, block(tm, cell_at(-k)), ax, q * n_cell + k, x_peer(q)))

    def forward_core(src, q, k):
        dst = block(hi_at(-q) * 2 + core, cell_at(-k))
        core_copies[q, k] = go(remote(src, dst, ap, q * n_cell + k, partner))

    if gather:
        for k in range(1, n_cell):
            cell_copies[k] = go(remote(duals_ref, block(tm, cell), ac, k, (tm, cell_at(k))))
        forward_x(duals_ref, 0)
        forward_core(duals_ref, 0, 0)
        full[tm * n_cell + cell] = duals_ref[...]

    fill(FILL[1])
    for k in range(1, n_cell):
        if gather:
            cell_copies[k].wait_recv()
            src = block(tm, cell_at(-k))
            forward_x(src, k)
            forward_core(src, 0, k)
    fill(FILL[2])
    if gather:
        for k in range(n_cell):
            for q in range(1, n_hi):
                x_copies[q, k].wait_recv()
                forward_core(block(hi_at(-q) * 2 + core, cell_at(-k)), q, k)
    for k in range(1, n_cell):
        co_copies[k].wait_recv()
    if gather:
        for k in range(n_cell):
            for q in range(n_hi):
                core_copies[q, k].wait_recv()

    bx_copies, bp_copies = {}, {}
    for h in range(HALVES):
        at = slice(h * half, (h + 1) * half)
        everything = full[...].reshape(obs, LANES) if gather else duals_ref[...]
        adj[tm, at, :] = jnp.dot(mask_t[at, :], everything, preferred_element_type=F32).astype(BF16)
        here = adj.at[tm, at]
        for q in range(1, n_hi):
            bx_copies[q, h] = go(remote(here, here, bx, q * HALVES + h, x_peer(q)))
        bp_copies[0, h] = go(remote(here, here, bp, h, partner))

    fill(FILL[3])
    for h in range(HALVES):
        for q in range(1, n_hi):
            bx_copies[q, h].wait_recv()
            got = adj.at[hi_at(-q) * 2 + core, h * half:(h + 1) * half]
            bp_copies[q, h] = go(remote(got, got, bp, q * HALVES + h, partner))
    fill(FILL[4])

    major = cell // 2
    place = jnp.where(cell % 2 == 0, major, n_cell - 1 - major)

    def cell_on(k):
        p = lax.rem(place + k + n_cell, n_cell)
        return jnp.where(p < n_cell // 2, p * 2, (n_cell - 1 - p) * 2 + 1)

    steps = n_cell // 2
    ring = {}

    def carries(way, step, h):
        return step < steps or (step == steps and (h < QUARTERS // 2) == (way > 0))

    def ring_send(way, step, h):
        if carries(way, step, h):
            part = held.at[cell_on(-way * (step - 1)), h * quarter:(h + 1) * quarter]
            sems = ring_r if way > 0 else ring_l
            ring[way, step, h] = go(remote(part, part, sems, step * QUARTERS + h, (tm, cell_on(way))))

    per_half = QUARTERS // HALVES
    for h in range(HALVES):
        at = slice(h * half, (h + 1) * half)
        for q in range(n_hi):
            bp_copies[q, h].wait_recv()
        mixed = cov_ref[tm, 0] * adj[0, at, :].astype(F32)
        for t in range(1, n_tm):
            mixed += cov_ref[tm, t] * adj[t, at, :].astype(F32)
        held[cell, at, :] = mixed.astype(BF16)
        for piece in range(h * per_half, (h + 1) * per_half):
            ring_send(1, 1, piece)
            ring_send(-1, 1, piece)

    def spread(c):
        return jnp.dot(cov_k[c], held[c], preferred_element_type=F32)

    def blocks(step):
        return [cell_on(-step), cell_on(step)] if step < steps else [cell_on(step)]

    acc[...] = spread(cell)
    for c in blocks(1):
        covariance_block(c)
    for step in range(1, steps + 1):
        for h in range(QUARTERS):
            for way in (1, -1):
                if carries(way, step, h):
                    ring[way, step, h].wait_recv()
                    ring_send(way, step + 1, h)
            if step < steps and h < len(blocks(step + 1)):
                covariance_block(blocks(step + 1)[h])
        for c in blocks(step):
            acc[...] += spread(c)
    fill(len(fillers))

    weighted = acc[...].astype(BF16)
    if scatter:
        span = rows * n_cell

        def product(t):
            at = pl.ds(pl.multiple_of(t * span, span), span)
            return jnp.dot(picked[at, :], weighted, preferred_element_type=F32)

        dp_copies, dx_copies, dc_copies = {}, {}, {}
        order = [*range(1, n_hi), 0]
        for q in order:
            core_out[q] = product(hi_at(q) * 2 + (1 - core)).astype(BF16)
            dp_copies[q] = go(remote(core_out.at[q], core_in.at[q], dp, q, partner))
        far = sorted(range(n_cell), key=lambda k: -min(k, n_cell - k))
        for q in order:
            summed = product(hi_at(q) * 2 + core)
            dp_copies[q].wait_recv()
            total[...] = (summed + core_in[q].astype(F32)).reshape(n_cell, rows, LANES)
            if q:
                for k in far:
                    c = cell_at(k)
                    x_out[q, c] = total[c].astype(BF16)
                    dx_copies[q, k] = go(remote(x_out.at[q, c], x_in.at[q, c], dx, q * n_cell + k, x_peer(q)))
        for k in far:
            c = cell_at(k)
            block_sum = total[c]
            for q in range(1, n_hi):
                dx_copies[q, k].wait_recv()
                block_sum += x_in[q, c].astype(F32)
            if k:
                cell_out[c] = block_sum.astype(BF16)
                dc_copies[k] = go(remote(cell_out.at[c], cell_in.at[k], dc, k, (tm, c)))
        result = block_sum
        for k in range(1, n_cell):
            dc_copies[k].wait_recv()
            result += cell_in[k].astype(F32)
        out_ref[...] = result
    else:
        for i in range(obs // PICK_ROWS):
            at = slice(i * PICK_ROWS, (i + 1) * PICK_ROWS)
            out_ref[at, :] = jnp.dot(picked[at, :], weighted, preferred_element_type=F32)

    for copy in sent:
        copy.wait_send()


def ring_program(n_tm, n_cell, sensitivity, duals, time_cov, cell_coords, obs_time, obs_owner):
    obs, _, cells = sensitivity.shape
    rows, reals = duals.shape
    n_hi = n_tm // 2
    inside = rows % 16 == 0
    if not inside:
        duals = lax.all_gather(duals, ("tm", "cell"), axis=0, tiled=True)
    span = rows * n_cell if inside else 16
    part = rows if inside else 16
    vmem = pl.BlockSpec(memory_space=pltpu.VMEM)

    def pair(count):
        return [pltpu.SemaphoreType.DMA((count,)), pltpu.SemaphoreType.DMA((count,))]

    steps = n_cell // 2 + 1
    out_rows = rows if inside else obs
    out = pl.pallas_call(
        functools.partial(ring_kernel, (n_hi, n_cell, inside, inside)),
        out_shape=jax.ShapeDtypeStruct((out_rows, reals), F32),
        in_specs=[
            pl.BlockSpec(memory_space=pl.ANY), vmem, pl.BlockSpec(memory_space=pltpu.SMEM), vmem, vmem, vmem,
        ],
        out_specs=vmem,
        scratch_shapes=[
            pltpu.VMEM((obs, cells), BF16),
            pltpu.VMEM((n_tm * n_cell if inside else 1, part, reals), BF16),
            pltpu.VMEM((n_cell, 2, cells), jnp.int32),
            pltpu.VMEM((cells, obs), BF16),
            pltpu.VMEM((obs, cells), BF16),
            pltpu.VMEM((cells, LANES), F32),
            pltpu.VMEM((cells, LANES), F32),
            pltpu.VMEM((obs, LANES), F32),
            pltpu.VMEM((1, obs), F32),
            pltpu.VMEM((n_cell, cells, cells), BF16),
            pltpu.VMEM((n_tm, cells, reals), BF16),
            pltpu.VMEM((n_cell, cells, reals), BF16),
            pltpu.VMEM((cells, reals), F32),
            pltpu.VMEM((n_hi, span, reals), BF16),
            pltpu.VMEM((n_hi, span, reals), BF16),
            pltpu.VMEM((n_hi, n_cell, part, reals), BF16),
            pltpu.VMEM((n_hi, n_cell, part, reals), BF16),
            pltpu.VMEM((n_cell, part, reals), F32),
            pltpu.VMEM((n_cell, part, reals), BF16),
            pltpu.VMEM((n_cell, part, reals), BF16),
            pltpu.SemaphoreType.DMA,
            *pair(n_cell), *pair(n_cell), *pair(n_hi * n_cell), *pair(n_hi * n_cell),
            *pair(n_hi * HALVES), *pair(n_hi * HALVES),
            *pair(steps * QUARTERS), *pair(steps * QUARTERS),
            *pair(n_hi), *pair(n_hi * n_cell), *pair(n_cell),
        ],
        compiler_params=pltpu.CompilerParams(
            collective_id=0, has_side_effects=True, vmem_limit_bytes=62 * 1024 * 1024
        ),
    )(
        sensitivity.reshape(obs, cells), duals, time_cov, cell_coords,
        obs_time.reshape(1, obs), obs_owner.reshape(1, obs),
    )
    if inside:
        return out
    return lax.psum_scatter(out, ("tm", "cell"), scatter_dimension=0, tiled=True)


GROUP = 4
PAD = GROUP - 1
TILE = 16


def field_kernel(cfg, sens_hbm, duals_ref, cov_ref, coords_ref, time_ref, owner_ref, out_ref, *s):
    n_hi, n_cell = cfg
    n_tm = 2 * n_hi
    (sens, full, coords_all, mask_t, picked, own_b, ids, toeplitz, hot_t, hot, halves, stage, tiles, fields, mixed,
     placed, grid, acc, back, outs, returned, weighted, core_out, core_in, x_out, x_in, total, cell_out, cell_in,
     local_sem, *pairs) = s
    co, ac, ax, ap, ea, eb, dp, dx, dc = zip(pairs[0::2], pairs[1::2])
    obs, cells = sens.shape
    rows = duals_ref.shape[0]
    blocks = cells // LANES
    grid_rows = n_cell * cells // LANES
    duos = grid_rows // 2
    wide = 2 * LANES

    tm = lax.axis_index("tm")
    cell = lax.axis_index("cell")
    hi, core = tm // 2, tm % 2
    partner = (hi * 2 + (1 - core), cell)
    me = tm * n_cell + cell

    def hi_at(q):
        return lax.rem(hi + q + n_hi, n_hi)

    def x_peer(q):
        return (hi_at(q) * 2 + core, cell)

    def cell_at(k):
        return lax.rem(cell + k + n_cell, n_cell)

    def tm_at(a):
        return lax.rem(tm + a + n_tm, n_tm)

    load = pltpu.make_async_copy(sens_hbm, sens, local_sem)
    load.start()

    barrier = pltpu.get_barrier_semaphore()
    peers = [(tm, cell_at(k)) for k in range(1, n_cell)] + [x_peer(q) for q in range(1, n_hi)] + [partner]
    for peer in peers:
        pl.semaphore_signal(barrier, inc=1, device_id=peer, device_id_type=MESH)
    coords_all[cell] = coords_ref[...]
    own_b[...] = column_of(owner_ref[...].astype(F32))
    live = tm <= time_ref[...]
    ids[...] = jnp.where(live, lax.broadcasted_iota(jnp.int32, (1, obs), 1), -1).astype(F32)

    col_gap = (
        lax.broadcasted_iota(jnp.int32, (LANES, LANES), 0) - lax.broadcasted_iota(jnp.int32, (LANES, LANES), 1)
    ).astype(F32)
    col_gap = col_gap * col_gap
    grid[...] = jnp.zeros_like(grid)

    @pl.loop(0, grid_rows)
    def _(gap):
        row_gap = gap.astype(F32)
        distance = jnp.sqrt(row_gap * row_gap + col_gap)
        block = (jnp.exp(-distance / LSCALE) / (8.0 * LSCALE)).astype(BF16)
        toeplitz[grid_rows - 1 - gap] = block
        toeplitz[grid_rows - 1 + gap] = block

    load.wait()

    @pl.loop(0, obs // PICK_ROWS)
    def _(i):
        at = pl.ds(pl.multiple_of(i * PICK_ROWS, PICK_ROWS), PICK_ROWS)
        alive = jnp.where(ids[:, at] >= 0.0, 1.0, 0.0).astype(BF16)
        mask_t[:, at] = sens[at, :].T * alive

    def pick(i):
        at = slice(i * PICK_ROWS, (i + 1) * PICK_ROWS)
        owned = own_b[at, :]
        hits = [
            jnp.where(owned == ids[:, j * LANES:(j + 1) * LANES], 1.0, 0.0).astype(BF16)
            for j in range(obs // LANES)
        ]
        picked[at, :] = jnp.dot(
            jnp.concatenate(hits, axis=1), sens[...], preferred_element_type=F32
        ).astype(BF16)

    fillers = [functools.partial(pick, i) for i in range(obs // PICK_ROWS)]

    def fill(count):
        for _ in range(count):
            if fillers:
                fillers.pop(0)()

    fill(PLAN[0])
    pl.semaphore_wait(barrier, len(peers))

    sent = []

    def go(copy):
        copy.start()
        sent.append(copy)
        return copy

    def block_of(t, c):
        return full.at[t * n_cell + c]

    co_copies, cell_copies, x_copies, core_copies = {}, {}, {}, {}

    def forward_x(src, k):
        for q in range(1, n_hi):
            x_copies[q, k] = go(remote(src, block_of(tm, cell_at(-k)), ax, q * n_cell + k, x_peer(q)))

    def forward_core(src, q, k):
        dst = block_of(hi_at(-q) * 2 + core, cell_at(-k))
        core_copies[q, k] = go(remote(src, dst, ap, q * n_cell + k, partner))

    for k in range(1, n_cell):
        cell_copies[k] = go(remote(duals_ref, block_of(tm, cell), ac, k, (tm, cell_at(k))))
    forward_x(duals_ref, 0)
    forward_core(duals_ref, 0, 0)
    for k in range(1, n_cell):
        co_copies[k] = go(remote(coords_ref, coords_all.at[cell], co, k, (tm, cell_at(k))))
    full[me] = duals_ref[...]

    fill(PLAN[1])
    for k in range(1, n_cell):
        cell_copies[k].wait_recv()
        src = block_of(tm, cell_at(-k))
        forward_x(src, k)
        forward_core(src, 0, k)
    fill(PLAN[2])
    for k in range(n_cell):
        for q in range(1, n_hi):
            x_copies[q, k].wait_recv()
            forward_core(block_of(hi_at(-q) * 2 + core, cell_at(-k)), q, k)
    for k in range(n_cell):
        for q in range(n_hi):
            core_copies[q, k].wait_recv()

    reals = duals_ref.shape[1]
    adjoint = jnp.dot(mask_t[...], full[...].reshape(obs, reals), preferred_element_type=F32)
    for b in range(blocks):
        stage[pl.ds(b, reals, stride=blocks), :] = adjoint[b * LANES:(b + 1) * LANES, :].T
    tiles[...] = stage[...].astype(BF16).reshape(tiles.shape)

    shifts = [(a, k) for k in sorted(range(n_cell), key=lambda k: -min(k, n_cell - k)) for a in range(n_tm)]
    ea_copies = {}
    for a, k in shifts:
        if (a, k) != (0, 0):
            peer = (tm_at(a), cell_at(k))
            ea_copies[a, k] = go(
                remote(tiles.at[peer[0] * n_cell + peer[1]], fields.at[me], ea, a * n_cell + k, peer)
            )
    fields[me] = tiles[me]

    for k in range(1, n_cell):
        co_copies[k].wait_recv()
    for k in range(n_cell):
        code = (coords_all[k, 0:1, :] & 1) * LANES + coords_all[k, 1:2, :]
        spots = lax.broadcasted_iota(jnp.int32, (wide, cells), 0)
        ones = jnp.where(spots == code, 1.0, 0.0).astype(BF16)
        hot_t[k] = ones
        hot[k] = ones.T
        halves[k] = coords_all[k, 0:1, :] >> 1
    fill(PLAN[3])

    for copy in ea_copies.values():
        copy.wait_recv()
    for k in range(n_cell):
        got = [fields[t * n_cell + k].astype(F32) for t in range(n_tm)]
        for t in range(n_tm):
            blend = cov_ref[t, 0] * got[0]
            for u in range(1, n_tm):
                blend += cov_ref[t, u] * got[u]
            mixed[k, t * TILE:(t + 1) * TILE, :] = blend
        for b in range(blocks):
            lanes = slice(b * LANES, (b + 1) * LANES)
            x = mixed[k, pl.ds(b, TILE, stride=blocks), :]
            for d in range(duos):
                placed[k, d * TILE:(d + 1) * TILE, lanes] = jnp.where(halves[k, 0:1, lanes] == d, x, 0.0).astype(BF16)
    on_grid = jnp.dot(placed[0], hot[0], preferred_element_type=F32)
    for k in range(1, n_cell):
        on_grid += jnp.dot(placed[k], hot[k], preferred_element_type=F32)
    grid[PAD * TILE:(PAD + duos) * TILE, :] = on_grid.astype(BF16)

    def covariance(m):
        at = grid_rows - 1 - 2 * m
        left = toeplitz[at:at + 2].reshape(wide, LANES)
        right = toeplitz[at - 1:at + 1].reshape(wide, LANES)
        return jnp.concatenate([left, right], axis=1)

    spans = [list(range(m, min(m + GROUP, duos))) for m in range(1 - duos, duos, GROUP)]
    spans.sort(key=lambda span: 0 not in span)
    for span in spans:
        low, high = max(0, span[0]), min(duos, duos + span[-1])
        count = (high - low) * TILE
        lhs = jnp.concatenate(
            [grid[(PAD + low - m) * TILE:(PAD + low - m) * TILE + count, :] for m in span], axis=1
        )
        rhs = jnp.concatenate([covariance(m) for m in span], axis=0)
        term = jnp.dot(lhs, rhs, preferred_element_type=F32)
        at = slice(low * TILE, high * TILE)
        if 0 in span:
            acc[at, :] = term
        else:
            acc[at, :] += term

    smooth = acc[...].astype(BF16)
    eb_copies = {}
    for k in sorted(range(n_cell), key=lambda k: -min(k, n_cell - k)):
        c = cell_at(k)
        spread = jnp.dot(smooth, hot_t[c], preferred_element_type=F32)
        for b in range(blocks):
            lanes = slice(b * LANES, (b + 1) * LANES)
            half = halves[c, 0:1, lanes]
            found = spread[0:TILE, lanes]
            for d in range(1, duos):
                found = jnp.where(half == d, spread[d * TILE:(d + 1) * TILE, lanes], found)
            back[k, pl.ds(b, TILE, stride=blocks), :] = found
        for t in range(n_tm):
            outs[t * n_cell + c] = back[k, t * TILE:(t + 1) * TILE, :].astype(BF16)
        for a in range(n_tm):
            if (a, k) != (0, 0):
                peer = (tm_at(a), c)
                eb_copies[a, k] = go(
                    remote(outs.at[peer[0] * n_cell + c], returned.at[me], eb, a * n_cell + k, peer)
                )
    returned[me] = outs[me]
    fill(len(fillers))
    for copy in eb_copies.values():
        copy.wait_recv()
    stage[...] = returned[...].reshape(stage.shape).astype(F32)
    for b in range(blocks):
        weighted[b * LANES:(b + 1) * LANES, :] = stage[pl.ds(b, reals, stride=blocks), :].T.astype(BF16)

    span = rows * n_cell

    def product(t):
        at = pl.ds(pl.multiple_of(t * span, span), span)
        return jnp.dot(picked[at, :], weighted[...], preferred_element_type=F32)

    dp_copies, dx_copies, dc_copies = {}, {}, {}
    order = [*range(1, n_hi), 0]
    for q in order:
        core_out[q] = product(hi_at(q) * 2 + (1 - core)).astype(BF16)
        dp_copies[q] = go(remote(core_out.at[q], core_in.at[q], dp, q, partner))
    far = sorted(range(n_cell), key=lambda k: -min(k, n_cell - k))
    for q in order:
        summed = product(hi_at(q) * 2 + core)
        dp_copies[q].wait_recv()
        total[...] = (summed + core_in[q].astype(F32)).reshape(n_cell, rows, LANES)
        if q:
            for k in far:
                c = cell_at(k)
                x_out[q, c] = total[c].astype(BF16)
                dx_copies[q, k] = go(remote(x_out.at[q, c], x_in.at[q, c], dx, q * n_cell + k, x_peer(q)))
    for k in far:
        c = cell_at(k)
        block_sum = total[c]
        for q in range(1, n_hi):
            dx_copies[q, k].wait_recv()
            block_sum += x_in[q, c].astype(F32)
        if k:
            cell_out[c] = block_sum.astype(BF16)
            dc_copies[k] = go(remote(cell_out.at[c], cell_in.at[k], dc, k, (tm, c)))
    result = block_sum
    for k in range(1, n_cell):
        dc_copies[k].wait_recv()
        result += cell_in[k].astype(F32)
    out_ref[...] = result

    for copy in sent:
        copy.wait_send()


PLAN = (0, 3, 3, 1)


def field_program(n_tm, n_cell, sensitivity, duals, time_cov, cell_coords, obs_time, obs_owner):
    obs, _, cells = sensitivity.shape
    rows, reals = duals.shape
    n_hi = n_tm // 2
    devices = n_tm * n_cell
    blocks = cells // LANES
    grid_rows = n_cell * cells // LANES
    duos = grid_rows // 2
    span = rows * n_cell
    vmem = pl.BlockSpec(memory_space=pltpu.VMEM)

    def pair(count):
        return [pltpu.SemaphoreType.DMA((count,)), pltpu.SemaphoreType.DMA((count,))]

    return pl.pallas_call(
        functools.partial(field_kernel, (n_hi, n_cell)),
        out_shape=jax.ShapeDtypeStruct((rows, reals), F32),
        in_specs=[
            pl.BlockSpec(memory_space=pl.ANY), vmem, pl.BlockSpec(memory_space=pltpu.SMEM), vmem, vmem, vmem,
        ],
        out_specs=vmem,
        scratch_shapes=[
            pltpu.VMEM((obs, cells), BF16),
            pltpu.VMEM((devices, rows, reals), BF16),
            pltpu.VMEM((n_cell, 2, cells), jnp.int32),
            pltpu.VMEM((cells, obs), BF16),
            pltpu.VMEM((obs, cells), BF16),
            pltpu.VMEM((obs, LANES), F32),
            pltpu.VMEM((1, obs), F32),
            pltpu.VMEM((2 * grid_rows - 1, LANES, LANES), BF16),
            pltpu.VMEM((n_cell, 2 * LANES, cells), BF16),
            pltpu.VMEM((n_cell, cells, 2 * LANES), BF16),
            pltpu.VMEM((n_cell, 1, cells), jnp.int32),
            pltpu.VMEM((reals * blocks, LANES), F32),
            pltpu.VMEM((devices, TILE, LANES), BF16),
            pltpu.VMEM((devices, TILE, LANES), BF16),
            pltpu.VMEM((n_cell, n_tm * TILE, LANES), F32),
            pltpu.VMEM((n_cell, duos * TILE, cells), BF16),
            pltpu.VMEM(((duos + 2 * PAD) * TILE, 2 * LANES), BF16),
            pltpu.VMEM((duos * TILE, 2 * LANES), F32),
            pltpu.VMEM((n_cell, n_tm * TILE, LANES), F32),
            pltpu.VMEM((devices, TILE, LANES), BF16),
            pltpu.VMEM((devices, TILE, LANES), BF16),
            pltpu.VMEM((cells, reals), BF16),
            pltpu.VMEM((n_hi, span, reals), BF16),
            pltpu.VMEM((n_hi, span, reals), BF16),
            pltpu.VMEM((n_hi, n_cell, rows, reals), BF16),
            pltpu.VMEM((n_hi, n_cell, rows, reals), BF16),
            pltpu.VMEM((n_cell, rows, reals), F32),
            pltpu.VMEM((n_cell, rows, reals), BF16),
            pltpu.VMEM((n_cell, rows, reals), BF16),
            pltpu.SemaphoreType.DMA,
            *pair(n_cell), *pair(n_cell), *pair(n_hi * n_cell), *pair(n_hi * n_cell),
            *pair(devices), *pair(devices),
            *pair(n_hi), *pair(n_hi * n_cell), *pair(n_cell),
        ],
        compiler_params=pltpu.CompilerParams(
            collective_id=0, has_side_effects=True, vmem_limit_bytes=62 * 1024 * 1024
        ),
    )(
        sensitivity.reshape(obs, cells), duals, time_cov, cell_coords,
        obs_time.reshape(1, obs), obs_owner.reshape(1, obs),
    )


def per_device(n_tm, n_cell, sensitivity, duals, *rest):
    cells = sensitivity.shape[2]
    rows, reals = duals.shape
    devices = n_tm * n_cell
    per = reals // devices
    fits = (
        rows % TILE == 0 and reals == LANES and cells % LANES == 0 and reals % devices == 0
        and per * (cells // LANES) == TILE and per * n_tm == TILE and (n_cell * cells) % (2 * LANES) == 0
    )
    program = field_program if fits else ring_program
    return program(n_tm, n_cell, sensitivity, duals, *rest)


def solution(mesh):
    in_specs = (P(None, "tm", "cell"), P(("tm", "cell"), None), P(), P(None, "cell"), P(), P())
    out_specs = P(("tm", "cell"), None)
    return jax.shard_map(
        functools.partial(per_device, mesh.shape["tm"], mesh.shape["cell"]),
        mesh=mesh, in_specs=in_specs, out_specs=out_specs, check_vma=False,
    )
```

```python
import functools

import jax
import jax.numpy as jnp
from jax import lax
from jax.experimental import pallas as pl
from jax.experimental.pallas import tpu as pltpu
from jax.sharding import PartitionSpec as P

LSCALE = 4
LANES = 128
HALVES = 2
PICK_ROWS = 256
QUARTERS = 4
FILL = (0, 3, 3, 1, 1)
MESH = pl.DeviceIdType.MESH
BF16 = jnp.bfloat16
F32 = jnp.float32


def remote(src, dst, sems, index, device):
    send, recv = sems
    return pltpu.make_async_remote_copy(
        src_ref=src, dst_ref=dst, send_sem=send.at[index], recv_sem=recv.at[index],
        device_id=device, device_id_type=MESH,
    )


def column_of(row):
    return jnp.broadcast_to(row, (LANES, row.shape[1])).T


def ring_kernel(cfg, sens_hbm, duals_ref, cov_ref, coords_ref, time_ref, owner_ref, out_ref, *s):
    n_hi, n_cell, gather, scatter = cfg
    n_tm = 2 * n_hi
    (sens, full, coords_all, mask_t, picked, row_b, col_b, own_b, ids, cov_k, adj, held, acc,
     core_out, core_in, x_out, x_in, total, cell_out, cell_in, local_sem, *pairs) = s
    co, ac, ax, ap, bx, bp, ring_r, ring_l, dp, dx, dc = zip(pairs[0::2], pairs[1::2])
    obs, cells = sens.shape
    rows = duals_ref.shape[0]
    half = cells // HALVES
    quarter = cells // QUARTERS

    tm = lax.axis_index("tm")
    cell = lax.axis_index("cell")
    hi, core = tm // 2, tm % 2
    partner = (hi * 2 + (1 - core), cell)

    def hi_at(q):
        return lax.rem(hi + q + n_hi, n_hi)

    def x_peer(q):
        return (hi_at(q) * 2 + core, cell)

    def cell_at(k):
        return lax.rem(cell + k + n_cell, n_cell)

    load = pltpu.make_async_copy(sens_hbm, sens, local_sem)
    load.start()

    barrier = pltpu.get_barrier_semaphore()
    peers = [(tm, cell_at(k)) for k in range(1, n_cell)] + [x_peer(q) for q in range(1, n_hi)] + [partner]
    for peer in peers:
        pl.semaphore_signal(barrier, inc=1, device_id=peer, device_id_type=MESH)
    coords_all[cell] = coords_ref[...]
    row_b[...] = column_of(coords_ref[0:1, :].astype(F32))
    col_b[...] = column_of(coords_ref[1:2, :].astype(F32))
    own_b[...] = column_of(owner_ref[...].astype(F32))
    live = tm <= time_ref[...]
    ids[...] = jnp.where(live, lax.broadcasted_iota(jnp.int32, (1, obs), 1), -1).astype(F32)

    def covariance_block(c):
        @pl.loop(0, cells // LANES)
        def _(j):
            lanes = pl.ds(pl.multiple_of(j * LANES, LANES), LANES)
            row_gap = row_b[...] - coords_all[c, 0:1, lanes].astype(F32)
            col_gap = col_b[...] - coords_all[c, 1:2, lanes].astype(F32)
            distance = jnp.sqrt(row_gap * row_gap + col_gap * col_gap)
            cov_k[c, :, lanes] = (jnp.exp(-distance / LSCALE) / (8.0 * LSCALE)).astype(BF16)

    def pick(i):
        at = slice(i * PICK_ROWS, (i + 1) * PICK_ROWS)
        owned = own_b[at, :]
        hot = [
            jnp.where(owned == ids[:, j * LANES:(j + 1) * LANES], 1.0, 0.0).astype(BF16)
            for j in range(obs // LANES)
        ]
        picked[at, :] = jnp.dot(
            jnp.concatenate(hot, axis=1), sens[...], preferred_element_type=F32
        ).astype(BF16)

    fillers = [functools.partial(pick, i) for i in range(obs // PICK_ROWS)]

    def fill(count):
        for _ in range(count):
            if fillers:
                fillers.pop(0)()

    covariance_block(cell)
    load.wait()

    @pl.loop(0, obs // PICK_ROWS)
    def _(i):
        at = pl.ds(pl.multiple_of(i * PICK_ROWS, PICK_ROWS), PICK_ROWS)
        alive = jnp.where(ids[:, at] >= 0.0, 1.0, 0.0).astype(BF16)
        mask_t[:, at] = sens[at, :].T * alive

    fill(FILL[0])
    pl.semaphore_wait(barrier, len(peers))

    sent = []

    def go(copy):
        copy.start()
        sent.append(copy)
        return copy

    co_copies = {}
    for k in range(1, n_cell):
        co_copies[k] = go(remote(coords_ref, coords_all.at[cell], co, k, (tm, cell_at(k))))

    def block(t, c):
        return full.at[t * n_cell + c]

    cell_copies, x_copies, core_copies = {}, {}, {}

    def forward_x(src, k):
        for q in range(1, n_hi):
            x_copies[q, k] = go(remote(src, block(tm, cell_at(-k)), ax, q * n_cell + k, x_peer(q)))

    def forward_core(src, q, k):
        dst = block(hi_at(-q) * 2 + core, cell_at(-k))
        core_copies[q, k] = go(remote(src, dst, ap, q * n_cell + k, partner))

    if gather:
        for k in range(1, n_cell):
            cell_copies[k] = go(remote(duals_ref, block(tm, cell), ac, k, (tm, cell_at(k))))
        forward_x(duals_ref, 0)
        forward_core(duals_ref, 0, 0)
        full[tm * n_cell + cell] = duals_ref[...]

    fill(FILL[1])
    for k in range(1, n_cell):
        if gather:
            cell_copies[k].wait_recv()
            src = block(tm, cell_at(-k))
            forward_x(src, k)
            forward_core(src, 0, k)
    fill(FILL[2])
    if gather:
        for k in range(n_cell):
            for q in range(1, n_hi):
                x_copies[q, k].wait_recv()
                forward_core(block(hi_at(-q) * 2 + core, cell_at(-k)), q, k)
    for k in range(1, n_cell):
        co_copies[k].wait_recv()
    if gather:
        for k in range(n_cell):
            for q in range(n_hi):
                core_copies[q, k].wait_recv()

    bx_copies, bp_copies = {}, {}
    for h in range(HALVES):
        at = slice(h * half, (h + 1) * half)
        everything = full[...].reshape(obs, LANES) if gather else duals_ref[...]
        adj[tm, at, :] = jnp.dot(mask_t[at, :], everything, preferred_element_type=F32).astype(BF16)
        here = adj.at[tm, at]
        for q in range(1, n_hi):
            bx_copies[q, h] = go(remote(here, here, bx, q * HALVES + h, x_peer(q)))
        bp_copies[0, h] = go(remote(here, here, bp, h, partner))

    fill(FILL[3])
    for h in range(HALVES):
        for q in range(1, n_hi):
            bx_copies[q, h].wait_recv()
            got = adj.at[hi_at(-q) * 2 + core, h * half:(h + 1) * half]
            bp_copies[q, h] = go(remote(got, got, bp, q * HALVES + h, partner))
    fill(FILL[4])

    major = cell // 2
    place = jnp.where(cell % 2 == 0, major, n_cell - 1 - major)

    def cell_on(k):
        p = lax.rem(place + k + n_cell, n_cell)
        return jnp.where(p < n_cell // 2, p * 2, (n_cell - 1 - p) * 2 + 1)

    steps = n_cell // 2
    ring = {}

    def carries(way, step, h):
        return step < steps or (step == steps and (h < QUARTERS // 2) == (way > 0))

    def ring_send(way, step, h):
        if carries(way, step, h):
            part = held.at[cell_on(-way * (step - 1)), h * quarter:(h + 1) * quarter]
            sems = ring_r if way > 0 else ring_l
            ring[way, step, h] = go(remote(part, part, sems, step * QUARTERS + h, (tm, cell_on(way))))

    per_half = QUARTERS // HALVES
    for h in range(HALVES):
        at = slice(h * half, (h + 1) * half)
        for q in range(n_hi):
            bp_copies[q, h].wait_recv()
        mixed = cov_ref[tm, 0] * adj[0, at, :].astype(F32)
        for t in range(1, n_tm):
            mixed += cov_ref[tm, t] * adj[t, at, :].astype(F32)
        held[cell, at, :] = mixed.astype(BF16)
        for piece in range(h * per_half, (h + 1) * per_half):
            ring_send(1, 1, piece)
            ring_send(-1, 1, piece)

    def spread(c):
        return jnp.dot(cov_k[c], held[c], preferred_element_type=F32)

    def blocks(step):
        return [cell_on(-step), cell_on(step)] if step < steps else [cell_on(step)]

    acc[...] = spread(cell)
    for c in blocks(1):
        covariance_block(c)
    for step in range(1, steps + 1):
        for h in range(QUARTERS):
            for way in (1, -1):
                if carries(way, step, h):
                    ring[way, step, h].wait_recv()
                    ring_send(way, step + 1, h)
            if step < steps and h < len(blocks(step + 1)):
                covariance_block(blocks(step + 1)[h])
        for c in blocks(step):
            acc[...] += spread(c)
    fill(len(fillers))

    weighted = acc[...].astype(BF16)
    if scatter:
        span = rows * n_cell

        def product(t):
            at = pl.ds(pl.multiple_of(t * span, span), span)
            return jnp.dot(picked[at, :], weighted, preferred_element_type=F32)

        dp_copies, dx_copies, dc_copies = {}, {}, {}
        order = [*range(1, n_hi), 0]
        for q in order:
            core_out[q] = product(hi_at(q) * 2 + (1 - core)).astype(BF16)
            dp_copies[q] = go(remote(core_out.at[q], core_in.at[q], dp, q, partner))
        far = sorted(range(n_cell), key=lambda k: -min(k, n_cell - k))
        for q in order:
            summed = product(hi_at(q) * 2 + core)
            dp_copies[q].wait_recv()
            total[...] = (summed + core_in[q].astype(F32)).reshape(n_cell, rows, LANES)
            if q:
                for k in far:
                    c = cell_at(k)
                    x_out[q, c] = total[c].astype(BF16)
                    dx_copies[q, k] = go(remote(x_out.at[q, c], x_in.at[q, c], dx, q * n_cell + k, x_peer(q)))
        for k in far:
            c = cell_at(k)
            block_sum = total[c]
            for q in range(1, n_hi):
                dx_copies[q, k].wait_recv()
                block_sum += x_in[q, c].astype(F32)
            if k:
                cell_out[c] = block_sum.astype(BF16)
                dc_copies[k] = go(remote(cell_out.at[c], cell_in.at[k], dc, k, (tm, c)))
        result = block_sum
        for k in range(1, n_cell):
            dc_copies[k].wait_recv()
            result += cell_in[k].astype(F32)
        out_ref[...] = result
    else:
        for i in range(obs // PICK_ROWS):
            at = slice(i * PICK_ROWS, (i + 1) * PICK_ROWS)
            out_ref[at, :] = jnp.dot(picked[at, :], weighted, preferred_element_type=F32)

    for copy in sent:
        copy.wait_send()


def ring_program(n_tm, n_cell, sensitivity, duals, time_cov, cell_coords, obs_time, obs_owner):
    obs, _, cells = sensitivity.shape
    rows, reals = duals.shape
    n_hi = n_tm // 2
    inside = rows % 16 == 0
    if not inside:
        duals = lax.all_gather(duals, ("tm", "cell"), axis=0, tiled=True)
    span = rows * n_cell if inside else 16
    part = rows if inside else 16
    vmem = pl.BlockSpec(memory_space=pltpu.VMEM)

    def pair(count):
        return [pltpu.SemaphoreType.DMA((count,)), pltpu.SemaphoreType.DMA((count,))]

    steps = n_cell // 2 + 1
    out_rows = rows if inside else obs
    out = pl.pallas_call(
        functools.partial(ring_kernel, (n_hi, n_cell, inside, inside)),
        out_shape=jax.ShapeDtypeStruct((out_rows, reals), F32),
        in_specs=[
            pl.BlockSpec(memory_space=pl.ANY), vmem, pl.BlockSpec(memory_space=pltpu.SMEM), vmem, vmem, vmem,
        ],
        out_specs=vmem,
        scratch_shapes=[
            pltpu.VMEM((obs, cells), BF16),
            pltpu.VMEM((n_tm * n_cell if inside else 1, part, reals), BF16),
            pltpu.VMEM((n_cell, 2, cells), jnp.int32),
            pltpu.VMEM((cells, obs), BF16),
            pltpu.VMEM((obs, cells), BF16),
            pltpu.VMEM((cells, LANES), F32),
            pltpu.VMEM((cells, LANES), F32),
            pltpu.VMEM((obs, LANES), F32),
            pltpu.VMEM((1, obs), F32),
            pltpu.VMEM((n_cell, cells, cells), BF16),
            pltpu.VMEM((n_tm, cells, reals), BF16),
            pltpu.VMEM((n_cell, cells, reals), BF16),
            pltpu.VMEM((cells, reals), F32),
            pltpu.VMEM((n_hi, span, reals), BF16),
            pltpu.VMEM((n_hi, span, reals), BF16),
            pltpu.VMEM((n_hi, n_cell, part, reals), BF16),
            pltpu.VMEM((n_hi, n_cell, part, reals), BF16),
            pltpu.VMEM((n_cell, part, reals), F32),
            pltpu.VMEM((n_cell, part, reals), BF16),
            pltpu.VMEM((n_cell, part, reals), BF16),
            pltpu.SemaphoreType.DMA,
            *pair(n_cell), *pair(n_cell), *pair(n_hi * n_cell), *pair(n_hi * n_cell),
            *pair(n_hi * HALVES), *pair(n_hi * HALVES),
            *pair(steps * QUARTERS), *pair(steps * QUARTERS),
            *pair(n_hi), *pair(n_hi * n_cell), *pair(n_cell),
        ],
        compiler_params=pltpu.CompilerParams(
            collective_id=0, has_side_effects=True, vmem_limit_bytes=62 * 1024 * 1024
        ),
    )(
        sensitivity.reshape(obs, cells), duals, time_cov, cell_coords,
        obs_time.reshape(1, obs), obs_owner.reshape(1, obs),
    )
    if inside:
        return out
    return lax.psum_scatter(out, ("tm", "cell"), scatter_dimension=0, tiled=True)


GROUP = 4
PAD = GROUP - 1
TILE = 16


def field_kernel(
    cfg, sens_hbm, duals_hbm, cov_hbm, coords_hbm, time_hbm, owner_hbm, out_ref, *s
):
    n_hi, n_cell = cfg
    n_tm, n_z = 2 * n_hi, n_cell // 2
    (sens, duals_ref, cov_ref, coords_ref, time_ref, owner_ref, full, coords_all, mask_t, picked, own_b, ids,
     toeplitz, hot_t, hot, halves, stage, tiles, fields, mixed, placed, grid, acc, back, outs, returned, weighted,
     core_out, core_in, plane_out, plane_in, sums, z_out, z_in, local_sems, *pairs) = s
    cz, cy, az, ap, ac, ea, eb, dp, dx, dz = zip(pairs[0::2], pairs[1::2])
    obs, cells = sens.shape
    rows, reals = duals_ref.shape
    blocks = cells // LANES
    grid_rows = n_cell * cells // LANES
    duos = grid_rows // 2
    wide = 2 * LANES

    tm = lax.axis_index("tm")
    cell = lax.axis_index("cell")
    hi, core = tm // 2, tm % 2
    z, y = cell // 2, cell % 2
    partner = (hi * 2 + (1 - core), cell)
    me = tm * n_cell + cell
    plane = [(dx_, dy_) for dx_ in range(n_hi) for dy_ in range(2)]

    def cell_at(k):
        return lax.rem(cell + k + n_cell, n_cell)

    def tm_at(a):
        return lax.rem(tm + a + n_tm, n_tm)

    def z_at(k):
        return lax.rem(z + k + n_z, n_z)

    def tm_in(shift):
        return lax.rem(hi + shift[0], n_hi) * 2 + core

    def y_in(shift):
        return lax.rem(y + shift[1], 2)

    def z_peer(k):
        return (tm, z_at(k) * 2 + y)

    def plane_peer(shift):
        return (tm_in(shift), z * 2 + y_in(shift))

    barrier = pltpu.get_barrier_semaphore()
    peers = [z_peer(k) for k in range(1, n_z)] + [plane_peer(shift) for shift in plane[1:]] + [partner]
    for peer in peers:
        pl.semaphore_signal(barrier, inc=1, device_id=peer, device_id_type=MESH)

    loads = [
        pltpu.make_async_copy(src, dst, local_sems.at[i])
        for i, (src, dst) in enumerate([
            (duals_hbm, duals_ref), (coords_hbm, coords_ref), (time_hbm, time_ref), (owner_hbm, owner_ref),
            (cov_hbm, cov_ref), (sens_hbm, sens),
        ])
    ]
    for load in loads:
        load.start()
    loads[0].wait()
    loads[1].wait()
    pl.semaphore_wait(barrier, len(peers))

    sent = []

    def go(copy):
        copy.start()
        sent.append(copy)
        return copy

    def block_of(shift, k):
        return full.at[tm_in(shift) * n_cell + z_at(-k) * 2 + y_in(shift)]

    az_copies, ap_copies, ac_copies, cz_copies, cy_copies = {}, {}, {}, {}, {}

    def forward_plane(src, k):
        for j, shift in enumerate(plane):
            if j:
                ap_copies[j, k] = go(remote(src, block_of((0, 0), k), ap, j * n_z + k, plane_peer(shift)))

    def forward_core(src, j, k):
        ac_copies[j, k] = go(remote(src, block_of(plane[j], k), ac, j * n_z + k, partner))

    for k in range(1, n_z):
        az_copies[k] = go(remote(duals_ref, block_of((0, 0), 0), az, k, z_peer(k)))
    forward_plane(duals_ref, 0)
    forward_core(duals_ref, 0, 0)
    for k in range(1, n_z):
        cz_copies[k] = go(remote(coords_ref, coords_all.at[cell], cz, k, z_peer(k)))
    cy_copies[0] = go(remote(coords_ref, coords_all.at[cell], cy, 0, plane_peer((0, 1))))
    full[me] = duals_ref[...]
    coords_all[cell] = coords_ref[...]

    loads[2].wait()
    loads[3].wait()
    own_b[...] = column_of(owner_ref[...].astype(F32))
    live = tm <= time_ref[...]
    ids[...] = jnp.where(live, lax.broadcasted_iota(jnp.int32, (1, obs), 1), -1).astype(F32)
    loads[4].wait()
    loads[5].wait()

    @pl.loop(0, obs // PICK_ROWS)
    def _(i):
        at = pl.ds(pl.multiple_of(i * PICK_ROWS, PICK_ROWS), PICK_ROWS)
        alive = jnp.where(ids[:, at] >= 0.0, 1.0, 0.0).astype(BF16)
        mask_t[:, at] = sens[at, :].T * alive

    def pick(i):
        at = slice(i * PICK_ROWS, (i + 1) * PICK_ROWS)
        owned = own_b[at, :]
        hits = [
            jnp.where(owned == ids[:, j * LANES:(j + 1) * LANES], 1.0, 0.0).astype(BF16)
            for j in range(obs // LANES)
        ]
        picked[at, :] = jnp.dot(
            jnp.concatenate(hits, axis=1), sens[...], preferred_element_type=F32
        ).astype(BF16)

    fillers = [functools.partial(pick, i) for i in range(obs // PICK_ROWS)]

    def fill(count):
        for _ in range(count):
            if fillers:
                fillers.pop(0)()

    fill(PLAN[0])
    for k in range(1, n_z):
        az_copies[k].wait_recv()
        src = block_of((0, 0), k)
        forward_plane(src, k)
        forward_core(src, 0, k)
    for k in range(1, n_z):
        cz_copies[k].wait_recv()
        got = coords_all.at[z_at(-k) * 2 + y]
        cy_copies[k] = go(remote(got, got, cy, k, plane_peer((0, 1))))

    col_gap = (
        lax.broadcasted_iota(jnp.int32, (LANES, LANES), 0) - lax.broadcasted_iota(jnp.int32, (LANES, LANES), 1)
    ).astype(F32)
    col_gap = col_gap * col_gap
    grid[...] = jnp.zeros_like(grid)

    @pl.loop(0, grid_rows)
    def _(gap):
        row_gap = gap.astype(F32)
        distance = jnp.sqrt(row_gap * row_gap + col_gap)
        block = (jnp.exp(-distance / LSCALE) / (8.0 * LSCALE)).astype(BF16)
        toeplitz[grid_rows - 1 - gap] = block
        toeplitz[grid_rows - 1 + gap] = block

    fill(PLAN[1])
    for k in range(n_z):
        for j in range(1, len(plane)):
            ap_copies[j, k].wait_recv()
            forward_core(block_of(plane[j], k), j, k)
    fill(PLAN[2])
    for k in range(n_z):
        for j in range(len(plane)):
            ac_copies[j, k].wait_recv()

    adjoint = jnp.dot(mask_t[...], full[...].reshape(obs, reals), preferred_element_type=F32)
    for b in range(blocks):
        stage[pl.ds(b, reals, stride=blocks), :] = adjoint[b * LANES:(b + 1) * LANES, :].T
    tiles[...] = stage[...].astype(BF16).reshape(tiles.shape)

    shifts = [(a, k) for k in sorted(range(n_cell), key=lambda k: -min(k, n_cell - k)) for a in range(n_tm)]
    ea_copies = {}
    for a, k in shifts:
        if (a, k) != (0, 0):
            peer = (tm_at(a), cell_at(k))
            ea_copies[a, k] = go(
                remote(tiles.at[peer[0] * n_cell + peer[1]], fields.at[me], ea, a * n_cell + k, peer)
            )
    fields[me] = tiles[me]

    for k in range(n_z):
        cy_copies[k].wait_recv()
    for k in range(n_cell):
        code = (coords_all[k, 0:1, :] & 1) * LANES + coords_all[k, 1:2, :]
        spots = lax.broadcasted_iota(jnp.int32, (wide, cells), 0)
        ones = jnp.where(spots == code, 1.0, 0.0).astype(BF16)
        hot_t[k] = ones
        hot[k] = ones.T
        halves[k] = coords_all[k, 0:1, :] >> 1
    fill(PLAN[3])

    for copy in ea_copies.values():
        copy.wait_recv()
    for k in range(n_cell):
        got = [fields[t * n_cell + k].astype(F32) for t in range(n_tm)]
        for t in range(n_tm):
            blend = cov_ref[t, 0] * got[0]
            for u in range(1, n_tm):
                blend += cov_ref[t, u] * got[u]
            mixed[k, t * TILE:(t + 1) * TILE, :] = blend
        for b in range(blocks):
            lanes = slice(b * LANES, (b + 1) * LANES)
            x = mixed[k, pl.ds(b, TILE, stride=blocks), :]
            for d in range(duos):
                placed[k, d * TILE:(d + 1) * TILE, lanes] = jnp.where(halves[k, 0:1, lanes] == d, x, 0.0).astype(BF16)
    on_grid = jnp.dot(placed[0], hot[0], preferred_element_type=F32)
    for k in range(1, n_cell):
        on_grid += jnp.dot(placed[k], hot[k], preferred_element_type=F32)
    grid[PAD * TILE:(PAD + duos) * TILE, :] = on_grid.astype(BF16)

    def covariance(m):
        at = grid_rows - 1 - 2 * m
        left = toeplitz[at:at + 2].reshape(wide, LANES)
        right = toeplitz[at - 1:at + 1].reshape(wide, LANES)
        return jnp.concatenate([left, right], axis=1)

    spans = [list(range(m, min(m + GROUP, duos))) for m in range(1 - duos, duos, GROUP)]
    spans.sort(key=lambda span: 0 not in span)
    for span in spans:
        low, high = max(0, span[0]), min(duos, duos + span[-1])
        count = (high - low) * TILE
        lhs = jnp.concatenate(
            [grid[(PAD + low - m) * TILE:(PAD + low - m) * TILE + count, :] for m in span], axis=1
        )
        rhs = jnp.concatenate([covariance(m) for m in span], axis=0)
        term = jnp.dot(lhs, rhs, preferred_element_type=F32)
        at = slice(low * TILE, high * TILE)
        if 0 in span:
            acc[at, :] = term
        else:
            acc[at, :] += term

    smooth = acc[...].astype(BF16)
    eb_copies = {}
    for k in sorted(range(n_cell), key=lambda k: -min(k, n_cell - k)):
        c = cell_at(k)
        spread = jnp.dot(smooth, hot_t[c], preferred_element_type=F32)
        for b in range(blocks):
            lanes = slice(b * LANES, (b + 1) * LANES)
            half = halves[c, 0:1, lanes]
            found = spread[0:TILE, lanes]
            for d in range(1, duos):
                found = jnp.where(half == d, spread[d * TILE:(d + 1) * TILE, lanes], found)
            back[k, pl.ds(b, TILE, stride=blocks), :] = found
        for t in range(n_tm):
            outs[t * n_cell + c] = back[k, t * TILE:(t + 1) * TILE, :].astype(BF16)
        for a in range(n_tm):
            if (a, k) != (0, 0):
                peer = (tm_at(a), c)
                eb_copies[a, k] = go(
                    remote(outs.at[peer[0] * n_cell + c], returned.at[me], eb, a * n_cell + k, peer)
                )
    returned[me] = outs[me]
    fill(len(fillers))
    for copy in eb_copies.values():
        copy.wait_recv()
    stage[...] = returned[...].reshape(stage.shape).astype(F32)
    for b in range(blocks):
        weighted[b * LANES:(b + 1) * LANES, :] = stage[pl.ds(b, reals, stride=blocks), :].T.astype(BF16)

    deep = 2 * rows

    def product(t, d):
        at = pl.ds(pl.multiple_of((t * n_cell + 2 * d) * rows, deep), deep)
        return jnp.dot(picked[at, :], weighted[...], preferred_element_type=F32).reshape(2, rows, reals)

    dp_copies, dx_copies = {}, {}
    for d in range(n_z):
        for h in range(n_hi):
            core_out[d, h] = product(h * 2 + (1 - core), d).astype(BF16)
        dp_copies[d] = go(remote(core_out.at[d], core_in.at[d], dp, d, partner))
    for d in range(n_z):
        terms = [product(h * 2 + core, d) for h in range(n_hi)]
        dp_copies[d].wait_recv()
        for h in range(n_hi):
            total = terms[h] + core_in[d, h].astype(F32)
            plane_out[d, h] = total.astype(BF16)
            sums[d, h] = total
        for j, shift in enumerate(plane):
            if j:
                src = plane_out.at[d, lax.rem(hi + shift[0], n_hi), y_in(shift)]
                dx_copies[j, d] = go(
                    remote(src, plane_in.at[d, j], dx, j * n_z + d, plane_peer(shift))
                )

    def z_copy(d, at):
        return remote(z_out.at[d], z_in.at[at], dz, at, (tm, d * 2 + y))

    for d in range(n_z):
        part = sums[d, hi, y]
        for j in range(1, len(plane)):
            dx_copies[j, d].wait_recv()
            part += plane_in[d, j].astype(F32)
        sums[d, 0, 0] = part
        z_out[d] = part.astype(BF16)

        @pl.when(z != d)
        def _():
            z_copy(d, z).start()

    result = sums[z, 0, 0]
    for k in range(1, n_z):
        z_copy(z_at(k), z_at(k)).wait_recv()
        result += z_in[z_at(k)].astype(F32)
    out_ref[...] = result

    for copy in sent:
        copy.wait_send()
    for d in range(n_z):
        @pl.when(z != d)
        def _():
            z_copy(d, z).wait_send()


PLAN = (1, 3, 2, 1)


def field_program(n_tm, n_cell, sensitivity, duals, time_cov, cell_coords, obs_time, obs_owner):
    obs, _, cells = sensitivity.shape
    rows, reals = duals.shape
    n_hi = n_tm // 2
    devices = n_tm * n_cell
    blocks = cells // LANES
    grid_rows = n_cell * cells // LANES
    duos = grid_rows // 2
    n_z = n_cell // 2

    def pair(count):
        return [pltpu.SemaphoreType.DMA((count,)), pltpu.SemaphoreType.DMA((count,))]

    return pl.pallas_call(
        functools.partial(field_kernel, (n_hi, n_cell)),
        out_shape=jax.ShapeDtypeStruct((rows, reals), F32),
        in_specs=[pl.BlockSpec(memory_space=pl.ANY)] * 6,
        out_specs=pl.BlockSpec(memory_space=pltpu.VMEM),
        scratch_shapes=[
            pltpu.VMEM((obs, cells), BF16),
            pltpu.VMEM((rows, reals), BF16),
            pltpu.SMEM((n_tm, n_tm), F32),
            pltpu.VMEM((2, cells), jnp.int32),
            pltpu.VMEM((1, obs), jnp.int32),
            pltpu.VMEM((1, obs), jnp.int32),
            pltpu.VMEM((devices, rows, reals), BF16),
            pltpu.VMEM((n_cell, 2, cells), jnp.int32),
            pltpu.VMEM((cells, obs), BF16),
            pltpu.VMEM((obs, cells), BF16),
            pltpu.VMEM((obs, LANES), F32),
            pltpu.VMEM((1, obs), F32),
            pltpu.VMEM((2 * grid_rows - 1, LANES, LANES), BF16),
            pltpu.VMEM((n_cell, 2 * LANES, cells), BF16),
            pltpu.VMEM((n_cell, cells, 2 * LANES), BF16),
            pltpu.VMEM((n_cell, 1, cells), jnp.int32),
            pltpu.VMEM((reals * blocks, LANES), F32),
            pltpu.VMEM((devices, TILE, LANES), BF16),
            pltpu.VMEM((devices, TILE, LANES), BF16),
            pltpu.VMEM((n_cell, n_tm * TILE, LANES), F32),
            pltpu.VMEM((n_cell, duos * TILE, cells), BF16),
            pltpu.VMEM(((duos + 2 * PAD) * TILE, 2 * LANES), BF16),
            pltpu.VMEM((duos * TILE, 2 * LANES), F32),
            pltpu.VMEM((n_cell, n_tm * TILE, LANES), F32),
            pltpu.VMEM((devices, TILE, LANES), BF16),
            pltpu.VMEM((devices, TILE, LANES), BF16),
            pltpu.VMEM((cells, reals), BF16),
            pltpu.VMEM((n_z, n_hi, 2, rows, reals), BF16),
            pltpu.VMEM((n_z, n_hi, 2, rows, reals), BF16),
            pltpu.VMEM((n_z, n_hi, 2, rows, reals), BF16),
            pltpu.VMEM((n_z, 2 * n_hi, rows, reals), BF16),
            pltpu.VMEM((n_z, n_hi, 2, rows, reals), F32),
            pltpu.VMEM((n_z, rows, reals), BF16),
            pltpu.VMEM((n_z, rows, reals), BF16),
            pltpu.SemaphoreType.DMA((6,)),
            *pair(n_z), *pair(n_z), *pair(n_z), *pair(2 * n_hi * n_z), *pair(2 * n_hi * n_z),
            *pair(devices), *pair(devices),
            *pair(n_z), *pair(2 * n_hi * n_z), *pair(n_z),
        ],
        compiler_params=pltpu.CompilerParams(
            collective_id=0, has_side_effects=True, vmem_limit_bytes=62 * 1024 * 1024
        ),
    )(
        sensitivity.reshape(obs, cells), duals, time_cov, cell_coords,
        obs_time.reshape(1, obs), obs_owner.reshape(1, obs),
    )


def per_device(n_tm, n_cell, sensitivity, duals, *rest):
    cells = sensitivity.shape[2]
    rows, reals = duals.shape
    devices = n_tm * n_cell
    per = reals // devices
    fits = (
        n_tm == 4 and n_cell % 2 == 0 and rows % TILE == 0 and reals == LANES and cells % LANES == 0 and reals % devices == 0
        and per * (cells // LANES) == TILE and per * n_tm == TILE and (n_cell * cells) % (2 * LANES) == 0
    )
    program = field_program if fits else ring_program
    return program(n_tm, n_cell, sensitivity, duals, *rest)


def solution(mesh):
    in_specs = (P(None, "tm", "cell"), P(("tm", "cell"), None), P(), P(None, "cell"), P(), P())
    out_specs = P(("tm", "cell"), None)
    return jax.shard_map(
        functools.partial(per_device, mesh.shape["tm"], mesh.shape["cell"]),
        mesh=mesh, in_specs=in_specs, out_specs=out_specs, check_vma=False,
    )
```

```python
import functools

import jax
import jax.numpy as jnp
from jax import lax
from jax.experimental import pallas as pl
from jax.experimental.pallas import tpu as pltpu
from jax.sharding import PartitionSpec as P

LSCALE = 4
LANES = 128
HALVES = 2
PICK_ROWS = 256
QUARTERS = 4
FILL = (0, 3, 3, 1, 1)
MESH = pl.DeviceIdType.MESH
BF16 = jnp.bfloat16
F32 = jnp.float32


def remote(src, dst, sems, index, device):
    send, recv = sems
    return pltpu.make_async_remote_copy(
        src_ref=src, dst_ref=dst, send_sem=send.at[index], recv_sem=recv.at[index],
        device_id=device, device_id_type=MESH,
    )


def column_of(row):
    return jnp.broadcast_to(row, (LANES, row.shape[1])).T


def ring_kernel(cfg, sens_hbm, duals_ref, cov_ref, coords_ref, time_ref, owner_ref, out_ref, *s):
    n_hi, n_cell, gather, scatter = cfg
    n_tm = 2 * n_hi
    (sens, full, coords_all, mask_t, picked, row_b, col_b, own_b, ids, cov_k, adj, held, acc,
     core_out, core_in, x_out, x_in, total, cell_out, cell_in, local_sem, *pairs) = s
    co, ac, ax, ap, bx, bp, ring_r, ring_l, dp, dx, dc = zip(pairs[0::2], pairs[1::2])
    obs, cells = sens.shape
    rows = duals_ref.shape[0]
    half = cells // HALVES
    quarter = cells // QUARTERS

    tm = lax.axis_index("tm")
    cell = lax.axis_index("cell")
    hi, core = tm // 2, tm % 2
    partner = (hi * 2 + (1 - core), cell)

    def hi_at(q):
        return lax.rem(hi + q + n_hi, n_hi)

    def x_peer(q):
        return (hi_at(q) * 2 + core, cell)

    def cell_at(k):
        return lax.rem(cell + k + n_cell, n_cell)

    load = pltpu.make_async_copy(sens_hbm, sens, local_sem)
    load.start()

    barrier = pltpu.get_barrier_semaphore()
    peers = [(tm, cell_at(k)) for k in range(1, n_cell)] + [x_peer(q) for q in range(1, n_hi)] + [partner]
    for peer in peers:
        pl.semaphore_signal(barrier, inc=1, device_id=peer, device_id_type=MESH)
    coords_all[cell] = coords_ref[...]
    row_b[...] = column_of(coords_ref[0:1, :].astype(F32))
    col_b[...] = column_of(coords_ref[1:2, :].astype(F32))
    own_b[...] = column_of(owner_ref[...].astype(F32))
    live = tm <= time_ref[...]
    ids[...] = jnp.where(live, lax.broadcasted_iota(jnp.int32, (1, obs), 1), -1).astype(F32)

    def covariance_block(c):
        @pl.loop(0, cells // LANES)
        def _(j):
            lanes = pl.ds(pl.multiple_of(j * LANES, LANES), LANES)
            row_gap = row_b[...] - coords_all[c, 0:1, lanes].astype(F32)
            col_gap = col_b[...] - coords_all[c, 1:2, lanes].astype(F32)
            distance = jnp.sqrt(row_gap * row_gap + col_gap * col_gap)
            cov_k[c, :, lanes] = (jnp.exp(-distance / LSCALE) / (8.0 * LSCALE)).astype(BF16)

    def pick(i):
        at = slice(i * PICK_ROWS, (i + 1) * PICK_ROWS)
        owned = own_b[at, :]
        hot = [
            jnp.where(owned == ids[:, j * LANES:(j + 1) * LANES], 1.0, 0.0).astype(BF16)
            for j in range(obs // LANES)
        ]
        picked[at, :] = jnp.dot(
            jnp.concatenate(hot, axis=1), sens[...], preferred_element_type=F32
        ).astype(BF16)

    fillers = [functools.partial(pick, i) for i in range(obs // PICK_ROWS)]

    def fill(count):
        for _ in range(count):
            if fillers:
                fillers.pop(0)()

    covariance_block(cell)
    load.wait()

    @pl.loop(0, obs // PICK_ROWS)
    def _(i):
        at = pl.ds(pl.multiple_of(i * PICK_ROWS, PICK_ROWS), PICK_ROWS)
        alive = jnp.where(ids[:, at] >= 0.0, 1.0, 0.0).astype(BF16)
        mask_t[:, at] = sens[at, :].T * alive

    fill(FILL[0])
    pl.semaphore_wait(barrier, len(peers))

    sent = []

    def go(copy):
        copy.start()
        sent.append(copy)
        return copy

    co_copies = {}
    for k in range(1, n_cell):
        co_copies[k] = go(remote(coords_ref, coords_all.at[cell], co, k, (tm, cell_at(k))))

    def block(t, c):
        return full.at[t * n_cell + c]

    cell_copies, x_copies, core_copies = {}, {}, {}

    def forward_x(src, k):
        for q in range(1, n_hi):
            x_copies[q, k] = go(remote(src, block(tm, cell_at(-k)), ax, q * n_cell + k, x_peer(q)))

    def forward_core(src, q, k):
        dst = block(hi_at(-q) * 2 + core, cell_at(-k))
        core_copies[q, k] = go(remote(src, dst, ap, q * n_cell + k, partner))

    if gather:
        for k in range(1, n_cell):
            cell_copies[k] = go(remote(duals_ref, block(tm, cell), ac, k, (tm, cell_at(k))))
        forward_x(duals_ref, 0)
        forward_core(duals_ref, 0, 0)
        full[tm * n_cell + cell] = duals_ref[...]

    fill(FILL[1])
    for k in range(1, n_cell):
        if gather:
            cell_copies[k].wait_recv()
            src = block(tm, cell_at(-k))
            forward_x(src, k)
            forward_core(src, 0, k)
    fill(FILL[2])
    if gather:
        for k in range(n_cell):
            for q in range(1, n_hi):
                x_copies[q, k].wait_recv()
                forward_core(block(hi_at(-q) * 2 + core, cell_at(-k)), q, k)
    for k in range(1, n_cell):
        co_copies[k].wait_recv()
    if gather:
        for k in range(n_cell):
            for q in range(n_hi):
                core_copies[q, k].wait_recv()

    bx_copies, bp_copies = {}, {}
    for h in range(HALVES):
        at = slice(h * half, (h + 1) * half)
        everything = full[...].reshape(obs, LANES) if gather else duals_ref[...]
        adj[tm, at, :] = jnp.dot(mask_t[at, :], everything, preferred_element_type=F32).astype(BF16)
        here = adj.at[tm, at]
        for q in range(1, n_hi):
            bx_copies[q, h] = go(remote(here, here, bx, q * HALVES + h, x_peer(q)))
        bp_copies[0, h] = go(remote(here, here, bp, h, partner))

    fill(FILL[3])
    for h in range(HALVES):
        for q in range(1, n_hi):
            bx_copies[q, h].wait_recv()
            got = adj.at[hi_at(-q) * 2 + core, h * half:(h + 1) * half]
            bp_copies[q, h] = go(remote(got, got, bp, q * HALVES + h, partner))
    fill(FILL[4])

    major = cell // 2
    place = jnp.where(cell % 2 == 0, major, n_cell - 1 - major)

    def cell_on(k):
        p = lax.rem(place + k + n_cell, n_cell)
        return jnp.where(p < n_cell // 2, p * 2, (n_cell - 1 - p) * 2 + 1)

    steps = n_cell // 2
    ring = {}

    def carries(way, step, h):
        return step < steps or (step == steps and (h < QUARTERS // 2) == (way > 0))

    def ring_send(way, step, h):
        if carries(way, step, h):
            part = held.at[cell_on(-way * (step - 1)), h * quarter:(h + 1) * quarter]
            sems = ring_r if way > 0 else ring_l
            ring[way, step, h] = go(remote(part, part, sems, step * QUARTERS + h, (tm, cell_on(way))))

    per_half = QUARTERS // HALVES
    for h in range(HALVES):
        at = slice(h * half, (h + 1) * half)
        for q in range(n_hi):
            bp_copies[q, h].wait_recv()
        mixed = cov_ref[tm, 0] * adj[0, at, :].astype(F32)
        for t in range(1, n_tm):
            mixed += cov_ref[tm, t] * adj[t, at, :].astype(F32)
        held[cell, at, :] = mixed.astype(BF16)
        for piece in range(h * per_half, (h + 1) * per_half):
            ring_send(1, 1, piece)
            ring_send(-1, 1, piece)

    def spread(c):
        return jnp.dot(cov_k[c], held[c], preferred_element_type=F32)

    def blocks(step):
        return [cell_on(-step), cell_on(step)] if step < steps else [cell_on(step)]

    acc[...] = spread(cell)
    for c in blocks(1):
        covariance_block(c)
    for step in range(1, steps + 1):
        for h in range(QUARTERS):
            for way in (1, -1):
                if carries(way, step, h):
                    ring[way, step, h].wait_recv()
                    ring_send(way, step + 1, h)
            if step < steps and h < len(blocks(step + 1)):
                covariance_block(blocks(step + 1)[h])
        for c in blocks(step):
            acc[...] += spread(c)
    fill(len(fillers))

    weighted = acc[...].astype(BF16)
    if scatter:
        span = rows * n_cell

        def product(t):
            at = pl.ds(pl.multiple_of(t * span, span), span)
            return jnp.dot(picked[at, :], weighted, preferred_element_type=F32)

        dp_copies, dx_copies, dc_copies = {}, {}, {}
        order = [*range(1, n_hi), 0]
        for q in order:
            core_out[q] = product(hi_at(q) * 2 + (1 - core)).astype(BF16)
            dp_copies[q] = go(remote(core_out.at[q], core_in.at[q], dp, q, partner))
        far = sorted(range(n_cell), key=lambda k: -min(k, n_cell - k))
        for q in order:
            summed = product(hi_at(q) * 2 + core)
            dp_copies[q].wait_recv()
            total[...] = (summed + core_in[q].astype(F32)).reshape(n_cell, rows, LANES)
            if q:
                for k in far:
                    c = cell_at(k)
                    x_out[q, c] = total[c].astype(BF16)
                    dx_copies[q, k] = go(remote(x_out.at[q, c], x_in.at[q, c], dx, q * n_cell + k, x_peer(q)))
        for k in far:
            c = cell_at(k)
            block_sum = total[c]
            for q in range(1, n_hi):
                dx_copies[q, k].wait_recv()
                block_sum += x_in[q, c].astype(F32)
            if k:
                cell_out[c] = block_sum.astype(BF16)
                dc_copies[k] = go(remote(cell_out.at[c], cell_in.at[k], dc, k, (tm, c)))
        result = block_sum
        for k in range(1, n_cell):
            dc_copies[k].wait_recv()
            result += cell_in[k].astype(F32)
        out_ref[...] = result
    else:
        for i in range(obs // PICK_ROWS):
            at = slice(i * PICK_ROWS, (i + 1) * PICK_ROWS)
            out_ref[at, :] = jnp.dot(picked[at, :], weighted, preferred_element_type=F32)

    for copy in sent:
        copy.wait_send()


def ring_program(n_tm, n_cell, sensitivity, duals, time_cov, cell_coords, obs_time, obs_owner):
    obs, _, cells = sensitivity.shape
    rows, reals = duals.shape
    n_hi = n_tm // 2
    inside = rows % 16 == 0
    if not inside:
        duals = lax.all_gather(duals, ("tm", "cell"), axis=0, tiled=True)
    span = rows * n_cell if inside else 16
    part = rows if inside else 16
    vmem = pl.BlockSpec(memory_space=pltpu.VMEM)

    def pair(count):
        return [pltpu.SemaphoreType.DMA((count,)), pltpu.SemaphoreType.DMA((count,))]

    steps = n_cell // 2 + 1
    out_rows = rows if inside else obs
    out = pl.pallas_call(
        functools.partial(ring_kernel, (n_hi, n_cell, inside, inside)),
        out_shape=jax.ShapeDtypeStruct((out_rows, reals), F32),
        in_specs=[
            pl.BlockSpec(memory_space=pl.ANY), vmem, pl.BlockSpec(memory_space=pltpu.SMEM), vmem, vmem, vmem,
        ],
        out_specs=vmem,
        scratch_shapes=[
            pltpu.VMEM((obs, cells), BF16),
            pltpu.VMEM((n_tm * n_cell if inside else 1, part, reals), BF16),
            pltpu.VMEM((n_cell, 2, cells), jnp.int32),
            pltpu.VMEM((cells, obs), BF16),
            pltpu.VMEM((obs, cells), BF16),
            pltpu.VMEM((cells, LANES), F32),
            pltpu.VMEM((cells, LANES), F32),
            pltpu.VMEM((obs, LANES), F32),
            pltpu.VMEM((1, obs), F32),
            pltpu.VMEM((n_cell, cells, cells), BF16),
            pltpu.VMEM((n_tm, cells, reals), BF16),
            pltpu.VMEM((n_cell, cells, reals), BF16),
            pltpu.VMEM((cells, reals), F32),
            pltpu.VMEM((n_hi, span, reals), BF16),
            pltpu.VMEM((n_hi, span, reals), BF16),
            pltpu.VMEM((n_hi, n_cell, part, reals), BF16),
            pltpu.VMEM((n_hi, n_cell, part, reals), BF16),
            pltpu.VMEM((n_cell, part, reals), F32),
            pltpu.VMEM((n_cell, part, reals), BF16),
            pltpu.VMEM((n_cell, part, reals), BF16),
            pltpu.SemaphoreType.DMA,
            *pair(n_cell), *pair(n_cell), *pair(n_hi * n_cell), *pair(n_hi * n_cell),
            *pair(n_hi * HALVES), *pair(n_hi * HALVES),
            *pair(steps * QUARTERS), *pair(steps * QUARTERS),
            *pair(n_hi), *pair(n_hi * n_cell), *pair(n_cell),
        ],
        compiler_params=pltpu.CompilerParams(
            collective_id=0, has_side_effects=True, vmem_limit_bytes=62 * 1024 * 1024
        ),
    )(
        sensitivity.reshape(obs, cells), duals, time_cov, cell_coords,
        obs_time.reshape(1, obs), obs_owner.reshape(1, obs),
    )
    if inside:
        return out
    return lax.psum_scatter(out, ("tm", "cell"), scatter_dimension=0, tiled=True)


GROUP = 4
PAD = GROUP - 1
TILE = 16


def field_kernel(
    cfg, sens_hbm, duals_hbm, cov_hbm, coords_hbm, time_hbm, owner_hbm, out_ref, *s
):
    n_hi, n_cell = cfg
    n_tm, n_z = 2 * n_hi, n_cell // 2
    (sens, duals_ref, cov_ref, coords_ref, time_ref, owner_ref, full, coords_all, mask_t, picked, own_b, ids,
     toeplitz, hot_t, hot, halves, stage, tiles, fields, mixed, placed, grid, acc, back, outs, returned, weighted,
     core_out, core_in, plane_out, plane_in, sums, z_out, z_in, local_sems, *pairs) = s
    cz, cy, az, ap, ac, ea, eb, dp, dx, dz = zip(pairs[0::2], pairs[1::2])
    obs, cells = sens.shape
    rows, reals = duals_ref.shape
    blocks = cells // LANES
    grid_rows = n_cell * cells // LANES
    duos = grid_rows // 2
    wide = 2 * LANES

    tm = lax.axis_index("tm")
    cell = lax.axis_index("cell")
    hi, core = tm // 2, tm % 2
    z, y = cell // 2, cell % 2
    partner = (hi * 2 + (1 - core), cell)
    me = tm * n_cell + cell
    plane = [(dx_, dy_) for dx_ in range(n_hi) for dy_ in range(2)]

    def cell_at(k):
        return lax.rem(cell + k + n_cell, n_cell)

    def tm_at(a):
        return lax.rem(tm + a + n_tm, n_tm)

    def z_at(k):
        return lax.rem(z + k + n_z, n_z)

    def tm_in(shift):
        return lax.rem(hi + shift[0], n_hi) * 2 + core

    def y_in(shift):
        return lax.rem(y + shift[1], 2)

    def z_peer(k):
        return (tm, z_at(k) * 2 + y)

    def plane_peer(shift):
        return (tm_in(shift), z * 2 + y_in(shift))

    barrier = pltpu.get_barrier_semaphore()
    peers = [z_peer(k) for k in range(1, n_z)] + [plane_peer(shift) for shift in plane[1:]] + [partner]
    for peer in peers:
        pl.semaphore_signal(barrier, inc=1, device_id=peer, device_id_type=MESH)

    loads = [
        pltpu.make_async_copy(src, dst, local_sems.at[i])
        for i, (src, dst) in enumerate([
            (duals_hbm, duals_ref), (coords_hbm, coords_ref), (time_hbm, time_ref), (owner_hbm, owner_ref),
            (cov_hbm, cov_ref), (sens_hbm, sens),
        ])
    ]
    for load in loads:
        load.start()
    loads[0].wait()
    loads[1].wait()
    pl.semaphore_wait(barrier, len(peers))

    sent = []

    def go(copy):
        copy.start()
        sent.append(copy)
        return copy

    def block_of(shift, k):
        return full.at[tm_in(shift) * n_cell + z_at(-k) * 2 + y_in(shift)]

    az_copies, ap_copies, ac_copies, cz_copies, cy_copies = {}, {}, {}, {}, {}

    def forward_plane(src, k):
        for j, shift in enumerate(plane):
            if j:
                ap_copies[j, k] = go(remote(src, block_of((0, 0), k), ap, j * n_z + k, plane_peer(shift)))

    def forward_core(src, j, k):
        ac_copies[j, k] = go(remote(src, block_of(plane[j], k), ac, j * n_z + k, partner))

    for k in range(1, n_z):
        az_copies[k] = go(remote(duals_ref, block_of((0, 0), 0), az, k, z_peer(k)))
    forward_plane(duals_ref, 0)
    forward_core(duals_ref, 0, 0)
    for k in range(1, n_z):
        cz_copies[k] = go(remote(coords_ref, coords_all.at[cell], cz, k, z_peer(k)))
    cy_copies[0] = go(remote(coords_ref, coords_all.at[cell], cy, 0, plane_peer((0, 1))))
    full[me] = duals_ref[...]
    coords_all[cell] = coords_ref[...]

    loads[2].wait()
    loads[3].wait()
    own_b[...] = column_of(owner_ref[...].astype(F32))
    live = tm <= time_ref[...]
    ids[...] = jnp.where(live, lax.broadcasted_iota(jnp.int32, (1, obs), 1), -1).astype(F32)
    loads[4].wait()
    loads[5].wait()

    @pl.loop(0, obs // PICK_ROWS)
    def _(i):
        at = pl.ds(pl.multiple_of(i * PICK_ROWS, PICK_ROWS), PICK_ROWS)
        alive = jnp.where(ids[:, at] >= 0.0, 1.0, 0.0).astype(BF16)
        mask_t[:, at] = sens[at, :].T * alive

    def pick(i):
        at = slice(i * PICK_ROWS, (i + 1) * PICK_ROWS)
        owned = own_b[at, :]
        hits = [
            jnp.where(owned == ids[:, j * LANES:(j + 1) * LANES], 1.0, 0.0).astype(BF16)
            for j in range(obs // LANES)
        ]
        picked[at, :] = jnp.dot(
            jnp.concatenate(hits, axis=1), sens[...], preferred_element_type=F32
        ).astype(BF16)

    fillers = [functools.partial(pick, i) for i in range(obs // PICK_ROWS)]

    def fill(count):
        for _ in range(count):
            if fillers:
                fillers.pop(0)()

    fill(PLAN[0])
    for k in range(1, n_z):
        az_copies[k].wait_recv()
        src = block_of((0, 0), k)
        forward_plane(src, k)
        forward_core(src, 0, k)
    for k in range(1, n_z):
        cz_copies[k].wait_recv()
        got = coords_all.at[z_at(-k) * 2 + y]
        cy_copies[k] = go(remote(got, got, cy, k, plane_peer((0, 1))))

    fill(PLAN[1])
    for k in range(n_z):
        for j in range(1, len(plane)):
            ap_copies[j, k].wait_recv()
            forward_core(block_of(plane[j], k), j, k)
    fill(PLAN[2])
    for k in range(n_z):
        for j in range(len(plane)):
            ac_copies[j, k].wait_recv()

    adjoint = jnp.dot(mask_t[...], full[...].reshape(obs, reals), preferred_element_type=F32)
    for b in range(blocks):
        stage[pl.ds(b, reals, stride=blocks), :] = adjoint[b * LANES:(b + 1) * LANES, :].T
    tiles[...] = stage[...].astype(BF16).reshape(tiles.shape)

    shifts = [(a, k) for k in sorted(range(n_cell), key=lambda k: -min(k, n_cell - k)) for a in range(n_tm)]
    ea_copies = {}
    for a, k in shifts:
        if (a, k) != (0, 0):
            peer = (tm_at(a), cell_at(k))
            ea_copies[a, k] = go(
                remote(tiles.at[peer[0] * n_cell + peer[1]], fields.at[me], ea, a * n_cell + k, peer)
            )
    fields[me] = tiles[me]

    for k in range(n_z):
        cy_copies[k].wait_recv()
    for k in range(n_cell):
        code = (coords_all[k, 0:1, :] & 1) * LANES + coords_all[k, 1:2, :]
        spots = lax.broadcasted_iota(jnp.int32, (wide, cells), 0)
        ones = jnp.where(spots == code, 1.0, 0.0).astype(BF16)
        hot_t[k] = ones
        hot[k] = ones.T
        halves[k] = coords_all[k, 0:1, :] >> 1
    col_gap = (
        lax.broadcasted_iota(jnp.int32, (LANES, LANES), 0) - lax.broadcasted_iota(jnp.int32, (LANES, LANES), 1)
    ).astype(F32)
    col_gap = col_gap * col_gap
    grid[...] = jnp.zeros_like(grid)

    @pl.loop(0, grid_rows)
    def _(gap):
        row_gap = gap.astype(F32)
        distance = jnp.sqrt(row_gap * row_gap + col_gap)
        block = (jnp.exp(-distance / LSCALE) / (8.0 * LSCALE)).astype(BF16)
        toeplitz[grid_rows - 1 - gap] = block
        toeplitz[grid_rows - 1 + gap] = block

    fill(PLAN[3])

    for copy in ea_copies.values():
        copy.wait_recv()
    for k in range(n_cell):
        got = [fields[t * n_cell + k].astype(F32) for t in range(n_tm)]
        for t in range(n_tm):
            blend = cov_ref[t, 0] * got[0]
            for u in range(1, n_tm):
                blend += cov_ref[t, u] * got[u]
            mixed[k, t * TILE:(t + 1) * TILE, :] = blend
        for b in range(blocks):
            lanes = slice(b * LANES, (b + 1) * LANES)
            x = mixed[k, pl.ds(b, TILE, stride=blocks), :]
            for d in range(duos):
                placed[k, d * TILE:(d + 1) * TILE, lanes] = jnp.where(halves[k, 0:1, lanes] == d, x, 0.0).astype(BF16)
    on_grid = jnp.dot(placed[0], hot[0], preferred_element_type=F32)
    for k in range(1, n_cell):
        on_grid += jnp.dot(placed[k], hot[k], preferred_element_type=F32)
    grid[PAD * TILE:(PAD + duos) * TILE, :] = on_grid.astype(BF16)

    def covariance(m):
        at = grid_rows - 1 - 2 * m
        left = toeplitz[at:at + 2].reshape(wide, LANES)
        right = toeplitz[at - 1:at + 1].reshape(wide, LANES)
        return jnp.concatenate([left, right], axis=1)

    spans = [list(range(m, min(m + GROUP, duos))) for m in range(1 - duos, duos, GROUP)]
    spans.sort(key=lambda span: 0 not in span)
    for span in spans:
        low, high = max(0, span[0]), min(duos, duos + span[-1])
        count = (high - low) * TILE
        lhs = jnp.concatenate(
            [grid[(PAD + low - m) * TILE:(PAD + low - m) * TILE + count, :] for m in span], axis=1
        )
        rhs = jnp.concatenate([covariance(m) for m in span], axis=0)
        term = jnp.dot(lhs, rhs, preferred_element_type=F32)
        at = slice(low * TILE, high * TILE)
        if 0 in span:
            acc[at, :] = term
        else:
            acc[at, :] += term

    smooth = acc[...].astype(BF16)
    eb_copies = {}
    for k in sorted(range(n_cell), key=lambda k: -min(k, n_cell - k)):
        c = cell_at(k)
        spread = jnp.dot(smooth, hot_t[c], preferred_element_type=F32)
        for b in range(blocks):
            lanes = slice(b * LANES, (b + 1) * LANES)
            half = halves[c, 0:1, lanes]
            found = spread[0:TILE, lanes]
            for d in range(1, duos):
                found = jnp.where(half == d, spread[d * TILE:(d + 1) * TILE, lanes], found)
            back[k, pl.ds(b, TILE, stride=blocks), :] = found
        for t in range(n_tm):
            outs[t * n_cell + c] = back[k, t * TILE:(t + 1) * TILE, :].astype(BF16)
        for a in range(n_tm):
            if (a, k) != (0, 0):
                peer = (tm_at(a), c)
                eb_copies[a, k] = go(
                    remote(outs.at[peer[0] * n_cell + c], returned.at[me], eb, a * n_cell + k, peer)
                )
    returned[me] = outs[me]
    fill(len(fillers))
    for copy in eb_copies.values():
        copy.wait_recv()
    stage[...] = returned[...].reshape(stage.shape).astype(F32)
    for b in range(blocks):
        weighted[b * LANES:(b + 1) * LANES, :] = stage[pl.ds(b, reals, stride=blocks), :].T.astype(BF16)

    deep = 2 * rows

    def product(t, d):
        at = pl.ds(pl.multiple_of((t * n_cell + 2 * d) * rows, deep), deep)
        return jnp.dot(picked[at, :], weighted[...], preferred_element_type=F32).reshape(2, rows, reals)

    dp_copies, dx_copies = {}, {}
    for d in range(n_z):
        for h in range(n_hi):
            core_out[d, h] = product(h * 2 + (1 - core), d).astype(BF16)
        dp_copies[d] = go(remote(core_out.at[d], core_in.at[d], dp, d, partner))
    for d in range(n_z):
        terms = [product(h * 2 + core, d) for h in range(n_hi)]
        dp_copies[d].wait_recv()
        for h in range(n_hi):
            total = terms[h] + core_in[d, h].astype(F32)
            plane_out[d, h] = total.astype(BF16)
            sums[d, h] = total
        if d == 1:
            @pl.when(core == 1)
            def _():
                for j in (1,):
                    dx_copies[j, 0].wait_recv()

        for j, shift in enumerate(plane):
            if j:
                src = plane_out.at[d, lax.rem(hi + shift[0], n_hi), y_in(shift)]
                dx_copies[j, d] = go(
                    remote(src, plane_in.at[d, j], dx, j * n_z + d, plane_peer(shift))
                )

    def z_copy(d, at):
        return remote(z_out.at[d], z_in.at[at], dz, at, (tm, d * 2 + y))

    for d in range(n_z):
        part = sums[d, hi, y]
        if d == 0:
            @pl.when(core == 0)
            def _():
                for j in (1,):
                    dx_copies[j, d].wait_recv()

        for j in range(1, len(plane)):
            if d != 0 or j not in (1,):
                dx_copies[j, d].wait_recv()
            part += plane_in[d, j].astype(F32)
        sums[d, 0, 0] = part
        z_out[d] = part.astype(BF16)

        @pl.when(z != d)
        def _():
            z_copy(d, z).start()

    result = sums[z, 0, 0]
    for k in range(1, n_z):
        z_copy(z_at(k), z_at(k)).wait_recv()
        result += z_in[z_at(k)].astype(F32)
    out_ref[...] = result

    for copy in sent:
        copy.wait_send()
    for d in range(n_z):
        @pl.when(z != d)
        def _():
            z_copy(d, z).wait_send()


PLAN = (0, 0, 0, 2)


def field_program(n_tm, n_cell, sensitivity, duals, time_cov, cell_coords, obs_time, obs_owner):
    obs, _, cells = sensitivity.shape
    rows, reals = duals.shape
    n_hi = n_tm // 2
    devices = n_tm * n_cell
    blocks = cells // LANES
    grid_rows = n_cell * cells // LANES
    duos = grid_rows // 2
    n_z = n_cell // 2

    def pair(count):
        return [pltpu.SemaphoreType.DMA((count,)), pltpu.SemaphoreType.DMA((count,))]

    return pl.pallas_call(
        functools.partial(field_kernel, (n_hi, n_cell)),
        out_shape=jax.ShapeDtypeStruct((rows, reals), F32),
        in_specs=[pl.BlockSpec(memory_space=pl.ANY)] * 6,
        out_specs=pl.BlockSpec(memory_space=pltpu.VMEM),
        scratch_shapes=[
            pltpu.VMEM((obs, cells), BF16),
            pltpu.VMEM((rows, reals), BF16),
            pltpu.SMEM((n_tm, n_tm), F32),
            pltpu.VMEM((2, cells), jnp.int32),
            pltpu.VMEM((1, obs), jnp.int32),
            pltpu.VMEM((1, obs), jnp.int32),
            pltpu.VMEM((devices, rows, reals), BF16),
            pltpu.VMEM((n_cell, 2, cells), jnp.int32),
            pltpu.VMEM((cells, obs), BF16),
            pltpu.VMEM((obs, cells), BF16),
            pltpu.VMEM((obs, LANES), F32),
            pltpu.VMEM((1, obs), F32),
            pltpu.VMEM((2 * grid_rows - 1, LANES, LANES), BF16),
            pltpu.VMEM((n_cell, 2 * LANES, cells), BF16),
            pltpu.VMEM((n_cell, cells, 2 * LANES), BF16),
            pltpu.VMEM((n_cell, 1, cells), jnp.int32),
            pltpu.VMEM((reals * blocks, LANES), F32),
            pltpu.VMEM((devices, TILE, LANES), BF16),
            pltpu.VMEM((devices, TILE, LANES), BF16),
            pltpu.VMEM((n_cell, n_tm * TILE, LANES), F32),
            pltpu.VMEM((n_cell, duos * TILE, cells), BF16),
            pltpu.VMEM(((duos + 2 * PAD) * TILE, 2 * LANES), BF16),
            pltpu.VMEM((duos * TILE, 2 * LANES), F32),
            pltpu.VMEM((n_cell, n_tm * TILE, LANES), F32),
            pltpu.VMEM((devices, TILE, LANES), BF16),
            pltpu.VMEM((devices, TILE, LANES), BF16),
            pltpu.VMEM((cells, reals), BF16),
            pltpu.VMEM((n_z, n_hi, 2, rows, reals), BF16),
            pltpu.VMEM((n_z, n_hi, 2, rows, reals), BF16),
            pltpu.VMEM((n_z, n_hi, 2, rows, reals), BF16),
            pltpu.VMEM((n_z, 2 * n_hi, rows, reals), BF16),
            pltpu.VMEM((n_z, n_hi, 2, rows, reals), F32),
            pltpu.VMEM((n_z, rows, reals), BF16),
            pltpu.VMEM((n_z, rows, reals), BF16),
            pltpu.SemaphoreType.DMA((6,)),
            *pair(n_z), *pair(n_z), *pair(n_z), *pair(2 * n_hi * n_z), *pair(2 * n_hi * n_z),
            *pair(devices), *pair(devices),
            *pair(n_z), *pair(2 * n_hi * n_z), *pair(n_z),
        ],
        compiler_params=pltpu.CompilerParams(
            collective_id=0, has_side_effects=True, vmem_limit_bytes=62 * 1024 * 1024
        ),
    )(
        sensitivity.reshape(obs, cells), duals, time_cov, cell_coords,
        obs_time.reshape(1, obs), obs_owner.reshape(1, obs),
    )


def per_device(n_tm, n_cell, sensitivity, duals, *rest):
    cells = sensitivity.shape[2]
    rows, reals = duals.shape
    devices = n_tm * n_cell
    per = reals // devices
    fits = (
        n_tm == 4 and n_cell % 2 == 0 and rows % TILE == 0 and reals == LANES and cells % LANES == 0 and reals % devices == 0
        and per * (cells // LANES) == TILE and per * n_tm == TILE and (n_cell * cells) % (2 * LANES) == 0
    )
    program = field_program if fits else ring_program
    return program(n_tm, n_cell, sensitivity, duals, *rest)


def solution(mesh):
    in_specs = (P(None, "tm", "cell"), P(("tm", "cell"), None), P(), P(None, "cell"), P(), P())
    out_specs = P(("tm", "cell"), None)
    return jax.shard_map(
        functools.partial(per_device, mesh.shape["tm"], mesh.shape["cell"]),
        mesh=mesh, in_specs=in_specs, out_specs=out_specs, check_vma=False,
    )
```

```python
import functools

import jax
import jax.numpy as jnp
from jax import lax
from jax.experimental import pallas as pl
from jax.experimental.pallas import tpu as pltpu
from jax.sharding import PartitionSpec as P

LSCALE = 4
LANES = 128
HALVES = 2
PICK_ROWS = 256
QUARTERS = 4
FILL = (0, 3, 3, 1, 1)
MESH = pl.DeviceIdType.MESH
BF16 = jnp.bfloat16
F32 = jnp.float32


def remote(src, dst, sems, index, device):
    send, recv = sems
    return pltpu.make_async_remote_copy(
        src_ref=src, dst_ref=dst, send_sem=send.at[index], recv_sem=recv.at[index],
        device_id=device, device_id_type=MESH,
    )


def column_of(row):
    return jnp.broadcast_to(row, (LANES, row.shape[1])).T


def ring_kernel(cfg, sens_hbm, duals_ref, cov_ref, coords_ref, time_ref, owner_ref, out_ref, *s):
    n_hi, n_cell, gather, scatter = cfg
    n_tm = 2 * n_hi
    (sens, full, coords_all, mask_t, picked, row_b, col_b, own_b, ids, cov_k, adj, held, acc,
     core_out, core_in, x_out, x_in, total, cell_out, cell_in, local_sem, *pairs) = s
    co, ac, ax, ap, bx, bp, ring_r, ring_l, dp, dx, dc = zip(pairs[0::2], pairs[1::2])
    obs, cells = sens.shape
    rows = duals_ref.shape[0]
    half = cells // HALVES
    quarter = cells // QUARTERS

    tm = lax.axis_index("tm")
    cell = lax.axis_index("cell")
    hi, core = tm // 2, tm % 2
    partner = (hi * 2 + (1 - core), cell)

    def hi_at(q):
        return lax.rem(hi + q + n_hi, n_hi)

    def x_peer(q):
        return (hi_at(q) * 2 + core, cell)

    def cell_at(k):
        return lax.rem(cell + k + n_cell, n_cell)

    load = pltpu.make_async_copy(sens_hbm, sens, local_sem)
    load.start()

    barrier = pltpu.get_barrier_semaphore()
    peers = [(tm, cell_at(k)) for k in range(1, n_cell)] + [x_peer(q) for q in range(1, n_hi)] + [partner]
    for peer in peers:
        pl.semaphore_signal(barrier, inc=1, device_id=peer, device_id_type=MESH)
    coords_all[cell] = coords_ref[...]
    row_b[...] = column_of(coords_ref[0:1, :].astype(F32))
    col_b[...] = column_of(coords_ref[1:2, :].astype(F32))
    own_b[...] = column_of(owner_ref[...].astype(F32))
    live = tm <= time_ref[...]
    ids[...] = jnp.where(live, lax.broadcasted_iota(jnp.int32, (1, obs), 1), -1).astype(F32)

    def covariance_block(c):
        @pl.loop(0, cells // LANES)
        def _(j):
            lanes = pl.ds(pl.multiple_of(j * LANES, LANES), LANES)
            row_gap = row_b[...] - coords_all[c, 0:1, lanes].astype(F32)
            col_gap = col_b[...] - coords_all[c, 1:2, lanes].astype(F32)
            distance = jnp.sqrt(row_gap * row_gap + col_gap * col_gap)
            cov_k[c, :, lanes] = (jnp.exp(-distance / LSCALE) / (8.0 * LSCALE)).astype(BF16)

    def pick(i):
        at = slice(i * PICK_ROWS, (i + 1) * PICK_ROWS)
        owned = own_b[at, :]
        hot = [
            jnp.where(owned == ids[:, j * LANES:(j + 1) * LANES], 1.0, 0.0).astype(BF16)
            for j in range(obs // LANES)
        ]
        picked[at, :] = jnp.dot(
            jnp.concatenate(hot, axis=1), sens[...], preferred_element_type=F32
        ).astype(BF16)

    fillers = [functools.partial(pick, i) for i in range(obs // PICK_ROWS)]

    def fill(count):
        for _ in range(count):
            if fillers:
                fillers.pop(0)()

    covariance_block(cell)
    load.wait()

    @pl.loop(0, obs // PICK_ROWS)
    def _(i):
        at = pl.ds(pl.multiple_of(i * PICK_ROWS, PICK_ROWS), PICK_ROWS)
        alive = jnp.where(ids[:, at] >= 0.0, 1.0, 0.0).astype(BF16)
        mask_t[:, at] = sens[at, :].T * alive

    fill(FILL[0])
    pl.semaphore_wait(barrier, len(peers))

    sent = []

    def go(copy):
        copy.start()
        sent.append(copy)
        return copy

    co_copies = {}
    for k in range(1, n_cell):
        co_copies[k] = go(remote(coords_ref, coords_all.at[cell], co, k, (tm, cell_at(k))))

    def block(t, c):
        return full.at[t * n_cell + c]

    cell_copies, x_copies, core_copies = {}, {}, {}

    def forward_x(src, k):
        for q in range(1, n_hi):
            x_copies[q, k] = go(remote(src, block(tm, cell_at(-k)), ax, q * n_cell + k, x_peer(q)))

    def forward_core(src, q, k):
        dst = block(hi_at(-q) * 2 + core, cell_at(-k))
        core_copies[q, k] = go(remote(src, dst, ap, q * n_cell + k, partner))

    if gather:
        for k in range(1, n_cell):
            cell_copies[k] = go(remote(duals_ref, block(tm, cell), ac, k, (tm, cell_at(k))))
        forward_x(duals_ref, 0)
        forward_core(duals_ref, 0, 0)
        full[tm * n_cell + cell] = duals_ref[...]

    fill(FILL[1])
    for k in range(1, n_cell):
        if gather:
            cell_copies[k].wait_recv()
            src = block(tm, cell_at(-k))
            forward_x(src, k)
            forward_core(src, 0, k)
    fill(FILL[2])
    if gather:
        for k in range(n_cell):
            for q in range(1, n_hi):
                x_copies[q, k].wait_recv()
                forward_core(block(hi_at(-q) * 2 + core, cell_at(-k)), q, k)
    for k in range(1, n_cell):
        co_copies[k].wait_recv()
    if gather:
        for k in range(n_cell):
            for q in range(n_hi):
                core_copies[q, k].wait_recv()

    bx_copies, bp_copies = {}, {}
    for h in range(HALVES):
        at = slice(h * half, (h + 1) * half)
        everything = full[...].reshape(obs, LANES) if gather else duals_ref[...]
        adj[tm, at, :] = jnp.dot(mask_t[at, :], everything, preferred_element_type=F32).astype(BF16)
        here = adj.at[tm, at]
        for q in range(1, n_hi):
            bx_copies[q, h] = go(remote(here, here, bx, q * HALVES + h, x_peer(q)))
        bp_copies[0, h] = go(remote(here, here, bp, h, partner))

    fill(FILL[3])
    for h in range(HALVES):
        for q in range(1, n_hi):
            bx_copies[q, h].wait_recv()
            got = adj.at[hi_at(-q) * 2 + core, h * half:(h + 1) * half]
            bp_copies[q, h] = go(remote(got, got, bp, q * HALVES + h, partner))
    fill(FILL[4])

    major = cell // 2
    place = jnp.where(cell % 2 == 0, major, n_cell - 1 - major)

    def cell_on(k):
        p = lax.rem(place + k + n_cell, n_cell)
        return jnp.where(p < n_cell // 2, p * 2, (n_cell - 1 - p) * 2 + 1)

    steps = n_cell // 2
    ring = {}

    def carries(way, step, h):
        return step < steps or (step == steps and (h < QUARTERS // 2) == (way > 0))

    def ring_send(way, step, h):
        if carries(way, step, h):
            part = held.at[cell_on(-way * (step - 1)), h * quarter:(h + 1) * quarter]
            sems = ring_r if way > 0 else ring_l
            ring[way, step, h] = go(remote(part, part, sems, step * QUARTERS + h, (tm, cell_on(way))))

    per_half = QUARTERS // HALVES
    for h in range(HALVES):
        at = slice(h * half, (h + 1) * half)
        for q in range(n_hi):
            bp_copies[q, h].wait_recv()
        mixed = cov_ref[tm, 0] * adj[0, at, :].astype(F32)
        for t in range(1, n_tm):
            mixed += cov_ref[tm, t] * adj[t, at, :].astype(F32)
        held[cell, at, :] = mixed.astype(BF16)
        for piece in range(h * per_half, (h + 1) * per_half):
            ring_send(1, 1, piece)
            ring_send(-1, 1, piece)

    def spread(c):
        return jnp.dot(cov_k[c], held[c], preferred_element_type=F32)

    def blocks(step):
        return [cell_on(-step), cell_on(step)] if step < steps else [cell_on(step)]

    acc[...] = spread(cell)
    for c in blocks(1):
        covariance_block(c)
    for step in range(1, steps + 1):
        for h in range(QUARTERS):
            for way in (1, -1):
                if carries(way, step, h):
                    ring[way, step, h].wait_recv()
                    ring_send(way, step + 1, h)
            if step < steps and h < len(blocks(step + 1)):
                covariance_block(blocks(step + 1)[h])
        for c in blocks(step):
            acc[...] += spread(c)
    fill(len(fillers))

    weighted = acc[...].astype(BF16)
    if scatter:
        span = rows * n_cell

        def product(t):
            at = pl.ds(pl.multiple_of(t * span, span), span)
            return jnp.dot(picked[at, :], weighted, preferred_element_type=F32)

        dp_copies, dx_copies, dc_copies = {}, {}, {}
        order = [*range(1, n_hi), 0]
        for q in order:
            core_out[q] = product(hi_at(q) * 2 + (1 - core)).astype(BF16)
            dp_copies[q] = go(remote(core_out.at[q], core_in.at[q], dp, q, partner))
        far = sorted(range(n_cell), key=lambda k: -min(k, n_cell - k))
        for q in order:
            summed = product(hi_at(q) * 2 + core)
            dp_copies[q].wait_recv()
            total[...] = (summed + core_in[q].astype(F32)).reshape(n_cell, rows, LANES)
            if q:
                for k in far:
                    c = cell_at(k)
                    x_out[q, c] = total[c].astype(BF16)
                    dx_copies[q, k] = go(remote(x_out.at[q, c], x_in.at[q, c], dx, q * n_cell + k, x_peer(q)))
        for k in far:
            c = cell_at(k)
            block_sum = total[c]
            for q in range(1, n_hi):
                dx_copies[q, k].wait_recv()
                block_sum += x_in[q, c].astype(F32)
            if k:
                cell_out[c] = block_sum.astype(BF16)
                dc_copies[k] = go(remote(cell_out.at[c], cell_in.at[k], dc, k, (tm, c)))
        result = block_sum
        for k in range(1, n_cell):
            dc_copies[k].wait_recv()
            result += cell_in[k].astype(F32)
        out_ref[...] = result
    else:
        for i in range(obs // PICK_ROWS):
            at = slice(i * PICK_ROWS, (i + 1) * PICK_ROWS)
            out_ref[at, :] = jnp.dot(picked[at, :], weighted, preferred_element_type=F32)

    for copy in sent:
        copy.wait_send()


def ring_program(n_tm, n_cell, sensitivity, duals, time_cov, cell_coords, obs_time, obs_owner):
    obs, _, cells = sensitivity.shape
    rows, reals = duals.shape
    n_hi = n_tm // 2
    inside = rows % 16 == 0
    if not inside:
        duals = lax.all_gather(duals, ("tm", "cell"), axis=0, tiled=True)
    span = rows * n_cell if inside else 16
    part = rows if inside else 16
    vmem = pl.BlockSpec(memory_space=pltpu.VMEM)

    def pair(count):
        return [pltpu.SemaphoreType.DMA((count,)), pltpu.SemaphoreType.DMA((count,))]

    steps = n_cell // 2 + 1
    out_rows = rows if inside else obs
    out = pl.pallas_call(
        functools.partial(ring_kernel, (n_hi, n_cell, inside, inside)),
        out_shape=jax.ShapeDtypeStruct((out_rows, reals), F32),
        in_specs=[
            pl.BlockSpec(memory_space=pl.ANY), vmem, pl.BlockSpec(memory_space=pltpu.SMEM), vmem, vmem, vmem,
        ],
        out_specs=vmem,
        scratch_shapes=[
            pltpu.VMEM((obs, cells), BF16),
            pltpu.VMEM((n_tm * n_cell if inside else 1, part, reals), BF16),
            pltpu.VMEM((n_cell, 2, cells), jnp.int32),
            pltpu.VMEM((cells, obs), BF16),
            pltpu.VMEM((obs, cells), BF16),
            pltpu.VMEM((cells, LANES), F32),
            pltpu.VMEM((cells, LANES), F32),
            pltpu.VMEM((obs, LANES), F32),
            pltpu.VMEM((1, obs), F32),
            pltpu.VMEM((n_cell, cells, cells), BF16),
            pltpu.VMEM((n_tm, cells, reals), BF16),
            pltpu.VMEM((n_cell, cells, reals), BF16),
            pltpu.VMEM((cells, reals), F32),
            pltpu.VMEM((n_hi, span, reals), BF16),
            pltpu.VMEM((n_hi, span, reals), BF16),
            pltpu.VMEM((n_hi, n_cell, part, reals), BF16),
            pltpu.VMEM((n_hi, n_cell, part, reals), BF16),
            pltpu.VMEM((n_cell, part, reals), F32),
            pltpu.VMEM((n_cell, part, reals), BF16),
            pltpu.VMEM((n_cell, part, reals), BF16),
            pltpu.SemaphoreType.DMA,
            *pair(n_cell), *pair(n_cell), *pair(n_hi * n_cell), *pair(n_hi * n_cell),
            *pair(n_hi * HALVES), *pair(n_hi * HALVES),
            *pair(steps * QUARTERS), *pair(steps * QUARTERS),
            *pair(n_hi), *pair(n_hi * n_cell), *pair(n_cell),
        ],
        compiler_params=pltpu.CompilerParams(
            collective_id=0, has_side_effects=True, vmem_limit_bytes=62 * 1024 * 1024
        ),
    )(
        sensitivity.reshape(obs, cells), duals, time_cov, cell_coords,
        obs_time.reshape(1, obs), obs_owner.reshape(1, obs),
    )
    if inside:
        return out
    return lax.psum_scatter(out, ("tm", "cell"), scatter_dimension=0, tiled=True)


GROUP = 4
PAD = GROUP - 1
TILE = 16


def field_kernel(
    cfg, sens_hbm, duals_hbm, cov_hbm, coords_hbm, time_hbm, owner_hbm, out_ref, *s
):
    n_hi, n_cell = cfg
    n_tm, n_z = 2 * n_hi, n_cell // 2
    (sens, duals_ref, cov_ref, coords_ref, time_ref, owner_ref, full, coords_all, mask_t, picked, own_b, ids,
     toeplitz, hot_t, hot, halves, row_hot, stage, tiles, fields, mixed, grid, acc, back, outs, returned, weighted,
     core_out, core_in, plane_out, plane_in, sums, z_out, z_in, local_sems, *pairs) = s
    cz, cy, az, ap, ac, ea, eb, dp, dx, dz = zip(pairs[0::2], pairs[1::2])
    obs, cells = sens.shape
    rows, reals = duals_ref.shape
    blocks = cells // LANES
    grid_rows = n_cell * cells // LANES
    duos = grid_rows // 2
    wide = 2 * LANES

    tm = lax.axis_index("tm")
    cell = lax.axis_index("cell")
    hi, core = tm // 2, tm % 2
    z, y = cell // 2, cell % 2
    partner = (hi * 2 + (1 - core), cell)
    me = tm * n_cell + cell
    plane = [(dx_, dy_) for dx_ in range(n_hi) for dy_ in range(2)]

    def z_at(k):
        return lax.rem(z + k + n_z, n_z)

    def tm_in(shift):
        return lax.rem(hi + shift[0], n_hi) * 2 + core

    def y_in(shift):
        return lax.rem(y + shift[1], 2)

    def z_peer(k):
        return (tm, z_at(k) * 2 + y)

    def plane_peer(shift):
        return (tm_in(shift), z * 2 + y_in(shift))

    def far_z(i):
        skew = jnp.where(2 * z < n_z - 1, n_z - 1 - 2 * z, 2 * z - (n_z - 1))
        reach = jnp.where(2 * z < n_z - 1, z, n_z - 1 - z)
        aside = jnp.where(2 * z < n_z - 1, n_z - 1 - i, i)
        turn = jnp.where(i < skew, 0, i - skew)
        gap = reach - turn // 2
        return jnp.where(i < skew, aside, z + jnp.where(turn % 2 == 0, gap, -gap))

    far_cells = [far_z(i) * 2 + lax.rem(y + f, 2) for i in range(n_z) for f in (1, 0)]
    shifts = [(fx, fc) for fx in (1, 0) for fc in (1, 0)]

    def tm_flip(shift):
        return lax.rem(hi + shift[0], n_hi) * 2 + lax.rem(core + shift[1], 2)

    def swap(src, dst, sems, there, here, device):
        send, recv = sems
        return pltpu.make_async_remote_copy(
            src_ref=src, dst_ref=dst, send_sem=send.at[there], recv_sem=recv.at[here],
            device_id=device, device_id_type=MESH,
        )

    barrier = pltpu.get_barrier_semaphore()
    peers = [z_peer(k) for k in range(1, n_z)] + [plane_peer(shift) for shift in plane[1:]] + [partner]
    for peer in peers:
        pl.semaphore_signal(barrier, inc=1, device_id=peer, device_id_type=MESH)

    loads = [
        pltpu.make_async_copy(src, dst, local_sems.at[i])
        for i, (src, dst) in enumerate([
            (duals_hbm, duals_ref), (coords_hbm, coords_ref), (time_hbm, time_ref), (owner_hbm, owner_ref),
            (cov_hbm, cov_ref), (sens_hbm, sens),
        ])
    ]
    for load in loads:
        load.start()
    loads[0].wait()
    loads[1].wait()
    pl.semaphore_wait(barrier, len(peers))

    sent = []

    def go(copy):
        copy.start()
        sent.append(copy)
        return copy

    def block_of(shift, k):
        return full.at[tm_in(shift) * n_cell + z_at(-k) * 2 + y_in(shift)]

    az_copies, ap_copies, ac_copies, cz_copies, cy_copies = {}, {}, {}, {}, {}

    def forward_plane(src, k):
        for j, shift in enumerate(plane):
            if j:
                ap_copies[j, k] = go(remote(src, block_of((0, 0), k), ap, j * n_z + k, plane_peer(shift)))

    def forward_core(src, j, k):
        ac_copies[j, k] = go(remote(src, block_of(plane[j], k), ac, j * n_z + k, partner))

    for k in range(1, n_z):
        az_copies[k] = go(remote(duals_ref, block_of((0, 0), 0), az, k, z_peer(k)))
    forward_plane(duals_ref, 0)
    forward_core(duals_ref, 0, 0)
    for k in range(1, n_z):
        cz_copies[k] = go(remote(coords_ref, coords_all.at[cell], cz, k, z_peer(k)))
    cy_copies[0] = go(remote(coords_ref, coords_all.at[cell], cy, 0, plane_peer((0, 1))))
    full[me] = duals_ref[...]
    coords_all[cell] = coords_ref[...]

    loads[2].wait()
    loads[3].wait()
    own_b[...] = column_of(owner_ref[...].astype(F32))
    live = tm <= time_ref[...]
    ids[...] = jnp.where(live, lax.broadcasted_iota(jnp.int32, (1, obs), 1), -1).astype(F32)
    loads[4].wait()
    loads[5].wait()

    @pl.loop(0, obs // PICK_ROWS)
    def _(i):
        at = pl.ds(pl.multiple_of(i * PICK_ROWS, PICK_ROWS), PICK_ROWS)
        alive = jnp.where(ids[:, at] >= 0.0, 1.0, 0.0).astype(BF16)
        mask_t[:, at] = sens[at, :].T * alive

    def pick(i):
        at = slice(i * PICK_ROWS, (i + 1) * PICK_ROWS)
        owned = own_b[at, :]
        hits = [
            jnp.where(owned == ids[:, j * LANES:(j + 1) * LANES], 1.0, 0.0).astype(BF16)
            for j in range(obs // LANES)
        ]
        picked[at, :] = jnp.dot(
            jnp.concatenate(hits, axis=1), sens[...], preferred_element_type=F32
        ).astype(BF16)

    fillers = [functools.partial(pick, i) for i in range(obs // PICK_ROWS)]

    def fill(count):
        for _ in range(count):
            if fillers:
                fillers.pop(0)()

    fill(PLAN[0])
    for k in range(1, n_z):
        az_copies[k].wait_recv()
        src = block_of((0, 0), k)
        forward_plane(src, k)
        forward_core(src, 0, k)
    for k in range(1, n_z):
        cz_copies[k].wait_recv()
        got = coords_all.at[z_at(-k) * 2 + y]
        cy_copies[k] = go(remote(got, got, cy, k, plane_peer((0, 1))))

    fill(PLAN[1])
    for k in range(n_z):
        for j in range(1, len(plane)):
            ap_copies[j, k].wait_recv()
            forward_core(block_of(plane[j], k), j, k)
    fill(PLAN[2])
    for k in range(n_z):
        for j in range(len(plane)):
            ac_copies[j, k].wait_recv()

    adjoint = jnp.dot(mask_t[...], full[...].reshape(obs, reals), preferred_element_type=F32)
    for b in range(blocks):
        stage[pl.ds(b, reals, stride=blocks), :] = adjoint[b * LANES:(b + 1) * LANES, :].T
    tiles[...] = stage[...].astype(BF16).reshape(tiles.shape)

    last = len(far_cells) - 1
    for i, c in enumerate(far_cells):
        for shift in shifts:
            if i < last or shift != (0, 0):
                t = tm_flip(shift)
                there = t * n_cell + c
                go(swap(tiles.at[there], fields.at[me], ea, there, me, (t, c)))
    fields[me] = tiles[me]

    for k in range(n_z):
        cy_copies[k].wait_recv()
    for k in range(n_cell):
        code = (coords_all[k, 0:1, :] & 1) * LANES + coords_all[k, 1:2, :]
        spots = lax.broadcasted_iota(jnp.int32, (wide, cells), 0)
        ones = jnp.where(spots == code, 1.0, 0.0).astype(BF16)
        hot_t[k] = ones
        hot[k] = ones.T
        halves[k] = coords_all[k, 0:1, :] >> 1
        duo = lax.broadcasted_iota(jnp.int32, (duos * TILE, cells), 0) // TILE
        row_hot[k] = jnp.where(duo == halves[k], 1.0, 0.0).astype(BF16)
    col_gap = (
        lax.broadcasted_iota(jnp.int32, (LANES, LANES), 0) - lax.broadcasted_iota(jnp.int32, (LANES, LANES), 1)
    ).astype(F32)
    col_gap = col_gap * col_gap
    grid[...] = jnp.zeros_like(grid)

    @pl.loop(0, grid_rows)
    def _(gap):
        row_gap = gap.astype(F32)
        distance = jnp.sqrt(row_gap * row_gap + col_gap)
        block = (jnp.exp(-distance / LSCALE) / (8.0 * LSCALE)).astype(BF16)
        toeplitz[grid_rows - 1 - gap] = block
        toeplitz[grid_rows - 1 + gap] = block

    fill(PLAN[3])

    for i, c in reversed(list(enumerate(far_cells))):
        for shift in reversed(shifts):
            if i < last or shift != (0, 0):
                t = tm_flip(shift)
                there = t * n_cell + c
                swap(tiles.at[me], fields.at[there], ea, there, there, (t, c)).wait_recv()
        got = [fields[t * n_cell + c].astype(F32) for t in range(n_tm)]
        for t in range(n_tm):
            blend = cov_ref[t, 0] * got[0]
            for u in range(1, n_tm):
                blend += cov_ref[t, u] * got[u]
            mixed[i, t * TILE:(t + 1) * TILE, :] = blend
        x = jnp.concatenate(
            [mixed[i, pl.ds(b, TILE, stride=blocks), :].astype(BF16) for b in range(blocks)], axis=1
        )
        placed = (row_hot[c].reshape(duos, TILE, cells) * x[None]).reshape(duos * TILE, cells)
        term = jnp.dot(placed, hot[c], preferred_element_type=F32)
        if i == last:
            acc[...] = term
        else:
            acc[...] += term
    on_grid = acc[...]
    grid[PAD * TILE:(PAD + duos) * TILE, :] = on_grid.astype(BF16)

    def covariance(m):
        at = grid_rows - 1 - 2 * m
        left = toeplitz[at:at + 2].reshape(wide, LANES)
        right = toeplitz[at - 1:at + 1].reshape(wide, LANES)
        return jnp.concatenate([left, right], axis=1)

    spans = [list(range(m, min(m + GROUP, duos))) for m in range(1 - duos, duos, GROUP)]
    spans.sort(key=lambda span: 0 not in span)
    for span in spans:
        low, high = max(0, span[0]), min(duos, duos + span[-1])
        count = (high - low) * TILE
        lhs = jnp.concatenate(
            [grid[(PAD + low - m) * TILE:(PAD + low - m) * TILE + count, :] for m in span], axis=1
        )
        rhs = jnp.concatenate([covariance(m) for m in span], axis=0)
        term = jnp.dot(lhs, rhs, preferred_element_type=F32)
        at = slice(low * TILE, high * TILE)
        if 0 in span:
            acc[at, :] = term
        else:
            acc[at, :] += term

    smooth = acc[...].astype(BF16)
    for i, c in enumerate(far_cells):
        spread = jnp.dot(smooth, hot_t[c], preferred_element_type=F32)
        for b in range(blocks):
            lanes = slice(b * LANES, (b + 1) * LANES)
            half = halves[c, 0:1, lanes]
            found = spread[0:TILE, lanes]
            for d in range(1, duos):
                found = jnp.where(half == d, spread[d * TILE:(d + 1) * TILE, lanes], found)
            back[i, pl.ds(b, TILE, stride=blocks), :] = found
        for t in range(n_tm):
            outs[t * n_cell + c] = back[i, t * TILE:(t + 1) * TILE, :].astype(BF16)
        for shift in shifts:
            if i < last or shift != (0, 0):
                t = tm_flip(shift)
                there = t * n_cell + c
                go(swap(outs.at[there], returned.at[me], eb, there, me, (t, c)))
    returned[me] = outs[me]
    fill(len(fillers))
    for i, c in reversed(list(enumerate(far_cells))):
        for shift in shifts:
            if i < last or shift != (0, 0):
                t = tm_flip(shift)
                there = t * n_cell + c
                swap(outs.at[me], returned.at[there], eb, there, there, (t, c)).wait_recv()
    stage[...] = returned[...].reshape(stage.shape).astype(F32)
    for b in range(blocks):
        weighted[b * LANES:(b + 1) * LANES, :] = stage[pl.ds(b, reals, stride=blocks), :].T.astype(BF16)

    deep = 2 * rows

    def product(t, d):
        at = pl.ds(pl.multiple_of((t * n_cell + 2 * d) * rows, deep), deep)
        return jnp.dot(picked[at, :], weighted[...], preferred_element_type=F32).reshape(2, rows, reals)

    dp_copies, dx_copies = {}, {}
    for d in range(n_z):
        for h in range(n_hi):
            core_out[d, h] = product(h * 2 + (1 - core), d).astype(BF16)
        dp_copies[d] = go(remote(core_out.at[d], core_in.at[d], dp, d, partner))
    for d in range(n_z):
        terms = [product(h * 2 + core, d) for h in range(n_hi)]
        dp_copies[d].wait_recv()
        for h in range(n_hi):
            total = terms[h] + core_in[d, h].astype(F32)
            plane_out[d, h] = total.astype(BF16)
            sums[d, h] = total
        if d == 1:
            @pl.when(core == 1)
            def _():
                for j in (1,):
                    dx_copies[j, 0].wait_recv()

        for j, shift in enumerate(plane):
            if j:
                src = plane_out.at[d, lax.rem(hi + shift[0], n_hi), y_in(shift)]
                dx_copies[j, d] = go(
                    remote(src, plane_in.at[d, j], dx, j * n_z + d, plane_peer(shift))
                )

    def z_copy(d, at):
        return remote(z_out.at[d], z_in.at[at], dz, at, (tm, d * 2 + y))

    for d in range(n_z):
        part = sums[d, hi, y]
        if d == 0:
            @pl.when(core == 0)
            def _():
                for j in (1,):
                    dx_copies[j, d].wait_recv()

        for j in range(1, len(plane)):
            if d != 0 or j not in (1,):
                dx_copies[j, d].wait_recv()
            part += plane_in[d, j].astype(F32)
        sums[d, 0, 0] = part
        z_out[d] = part.astype(BF16)

        @pl.when(z != d)
        def _():
            z_copy(d, z).start()

    result = sums[z, 0, 0]
    for k in range(1, n_z):
        z_copy(z_at(k), z_at(k)).wait_recv()
        result += z_in[z_at(k)].astype(F32)
    out_ref[...] = result

    for copy in sent:
        copy.wait_send()
    for d in range(n_z):
        @pl.when(z != d)
        def _():
            z_copy(d, z).wait_send()


PLAN = (0, 1, 0, 1)


def field_program(n_tm, n_cell, sensitivity, duals, time_cov, cell_coords, obs_time, obs_owner):
    obs, _, cells = sensitivity.shape
    rows, reals = duals.shape
    n_hi = n_tm // 2
    devices = n_tm * n_cell
    blocks = cells // LANES
    grid_rows = n_cell * cells // LANES
    duos = grid_rows // 2
    n_z = n_cell // 2

    def pair(count):
        return [pltpu.SemaphoreType.DMA((count,)), pltpu.SemaphoreType.DMA((count,))]

    return pl.pallas_call(
        functools.partial(field_kernel, (n_hi, n_cell)),
        out_shape=jax.ShapeDtypeStruct((rows, reals), F32),
        in_specs=[pl.BlockSpec(memory_space=pltpu.HBM)] * 6,
        out_specs=pl.BlockSpec(memory_space=pltpu.VMEM),
        scratch_shapes=[
            pltpu.VMEM((obs, cells), BF16),
            pltpu.VMEM((rows, reals), BF16),
            pltpu.SMEM((n_tm, n_tm), F32),
            pltpu.VMEM((2, cells), jnp.int32),
            pltpu.VMEM((1, obs), jnp.int32),
            pltpu.VMEM((1, obs), jnp.int32),
            pltpu.VMEM((devices, rows, reals), BF16),
            pltpu.VMEM((n_cell, 2, cells), jnp.int32),
            pltpu.VMEM((cells, obs), BF16),
            pltpu.VMEM((obs, cells), BF16),
            pltpu.VMEM((obs, LANES), F32),
            pltpu.VMEM((1, obs), F32),
            pltpu.VMEM((2 * grid_rows - 1, LANES, LANES), BF16),
            pltpu.VMEM((n_cell, 2 * LANES, cells), BF16),
            pltpu.VMEM((n_cell, cells, 2 * LANES), BF16),
            pltpu.VMEM((n_cell, 1, cells), jnp.int32),
            pltpu.VMEM((n_cell, duos * TILE, cells), BF16),
            pltpu.VMEM((reals * blocks, LANES), F32),
            pltpu.VMEM((devices, TILE, LANES), BF16),
            pltpu.VMEM((devices, TILE, LANES), BF16),
            pltpu.VMEM((n_cell, n_tm * TILE, LANES), F32),
            pltpu.VMEM(((duos + 2 * PAD) * TILE, 2 * LANES), BF16),
            pltpu.VMEM((duos * TILE, 2 * LANES), F32),
            pltpu.VMEM((n_cell, n_tm * TILE, LANES), F32),
            pltpu.VMEM((devices, TILE, LANES), BF16),
            pltpu.VMEM((devices, TILE, LANES), BF16),
            pltpu.VMEM((cells, reals), BF16),
            pltpu.VMEM((n_z, n_hi, 2, rows, reals), BF16),
            pltpu.VMEM((n_z, n_hi, 2, rows, reals), BF16),
            pltpu.VMEM((n_z, n_hi, 2, rows, reals), BF16),
            pltpu.VMEM((n_z, 2 * n_hi, rows, reals), BF16),
            pltpu.VMEM((n_z, n_hi, 2, rows, reals), F32),
            pltpu.VMEM((n_z, rows, reals), BF16),
            pltpu.VMEM((n_z, rows, reals), BF16),
            pltpu.SemaphoreType.DMA((6,)),
            *pair(n_z), *pair(n_z), *pair(n_z), *pair(2 * n_hi * n_z), *pair(2 * n_hi * n_z),
            *pair(devices), *pair(devices),
            *pair(n_z), *pair(2 * n_hi * n_z), *pair(n_z),
        ],
        compiler_params=pltpu.CompilerParams(
            collective_id=0, has_side_effects=True, vmem_limit_bytes=40 * 1024 * 1024
        ),
    )(*[
        pltpu.with_memory_space_constraint(x, pltpu.HBM) for x in (
            sensitivity.reshape(obs, cells), duals, time_cov, cell_coords,
            obs_time.reshape(1, obs), obs_owner.reshape(1, obs),
        )
    ])


def per_device(n_tm, n_cell, sensitivity, duals, *rest):
    cells = sensitivity.shape[2]
    rows, reals = duals.shape
    devices = n_tm * n_cell
    per = reals // devices
    fits = (
        n_tm == 4 and n_cell % 2 == 0 and rows % TILE == 0 and reals == LANES and cells % LANES == 0 and reals % devices == 0
        and per * (cells // LANES) == TILE and per * n_tm == TILE and (n_cell * cells) % (2 * LANES) == 0
    )
    program = field_program if fits else ring_program
    return program(n_tm, n_cell, sensitivity, duals, *rest)


def solution(mesh):
    in_specs = (P(None, "tm", "cell"), P(("tm", "cell"), None), P(), P(None, "cell"), P(), P())
    out_specs = P(("tm", "cell"), None)
    return jax.shard_map(
        functools.partial(per_device, mesh.shape["tm"], mesh.shape["cell"]),
        mesh=mesh, in_specs=in_specs, out_specs=out_specs, check_vma=False,
    )
```

```python
import functools

import jax
import jax.numpy as jnp
from jax import lax
from jax.experimental import pallas as pl
from jax.experimental.pallas import tpu as pltpu
from jax.sharding import PartitionSpec as P

LSCALE = 4
LANES = 128
HALVES = 2
PICK_ROWS = 256
QUARTERS = 4
FILL = (0, 3, 3, 1, 1)
MESH = pl.DeviceIdType.MESH
BF16 = jnp.bfloat16
F32 = jnp.float32


def remote(src, dst, sems, index, device):
    send, recv = sems
    return pltpu.make_async_remote_copy(
        src_ref=src, dst_ref=dst, send_sem=send.at[index], recv_sem=recv.at[index],
        device_id=device, device_id_type=MESH,
    )


def column_of(row):
    return jnp.broadcast_to(row, (LANES, row.shape[1])).T


def ring_kernel(cfg, sens_hbm, duals_ref, cov_ref, coords_ref, time_ref, owner_ref, out_ref, *s):
    n_hi, n_cell, gather, scatter = cfg
    n_tm = 2 * n_hi
    (sens, full, coords_all, mask_t, picked, row_b, col_b, own_b, ids, cov_k, adj, held, acc,
     core_out, core_in, x_out, x_in, total, cell_out, cell_in, local_sem, *pairs) = s
    co, ac, ax, ap, bx, bp, ring_r, ring_l, dp, dx, dc = zip(pairs[0::2], pairs[1::2])
    obs, cells = sens.shape
    rows = duals_ref.shape[0]
    half = cells // HALVES
    quarter = cells // QUARTERS

    tm = lax.axis_index("tm")
    cell = lax.axis_index("cell")
    hi, core = tm // 2, tm % 2
    partner = (hi * 2 + (1 - core), cell)

    def hi_at(q):
        return lax.rem(hi + q + n_hi, n_hi)

    def x_peer(q):
        return (hi_at(q) * 2 + core, cell)

    def cell_at(k):
        return lax.rem(cell + k + n_cell, n_cell)

    load = pltpu.make_async_copy(sens_hbm, sens, local_sem)
    load.start()

    barrier = pltpu.get_barrier_semaphore()
    peers = [(tm, cell_at(k)) for k in range(1, n_cell)] + [x_peer(q) for q in range(1, n_hi)] + [partner]
    for peer in peers:
        pl.semaphore_signal(barrier, inc=1, device_id=peer, device_id_type=MESH)
    coords_all[cell] = coords_ref[...]
    row_b[...] = column_of(coords_ref[0:1, :].astype(F32))
    col_b[...] = column_of(coords_ref[1:2, :].astype(F32))
    own_b[...] = column_of(owner_ref[...].astype(F32))
    live = tm <= time_ref[...]
    ids[...] = jnp.where(live, lax.broadcasted_iota(jnp.int32, (1, obs), 1), -1).astype(F32)

    def covariance_block(c):
        @pl.loop(0, cells // LANES)
        def _(j):
            lanes = pl.ds(pl.multiple_of(j * LANES, LANES), LANES)
            row_gap = row_b[...] - coords_all[c, 0:1, lanes].astype(F32)
            col_gap = col_b[...] - coords_all[c, 1:2, lanes].astype(F32)
            distance = jnp.sqrt(row_gap * row_gap + col_gap * col_gap)
            cov_k[c, :, lanes] = (jnp.exp(-distance / LSCALE) / (8.0 * LSCALE)).astype(BF16)

    def pick(i):
        at = slice(i * PICK_ROWS, (i + 1) * PICK_ROWS)
        owned = own_b[at, :]
        hot = [
            jnp.where(owned == ids[:, j * LANES:(j + 1) * LANES], 1.0, 0.0).astype(BF16)
            for j in range(obs // LANES)
        ]
        picked[at, :] = jnp.dot(
            jnp.concatenate(hot, axis=1), sens[...], preferred_element_type=F32
        ).astype(BF16)

    fillers = [functools.partial(pick, i) for i in range(obs // PICK_ROWS)]

    def fill(count):
        for _ in range(count):
            if fillers:
                fillers.pop(0)()

    covariance_block(cell)
    load.wait()

    @pl.loop(0, obs // PICK_ROWS)
    def _(i):
        at = pl.ds(pl.multiple_of(i * PICK_ROWS, PICK_ROWS), PICK_ROWS)
        alive = jnp.where(ids[:, at] >= 0.0, 1.0, 0.0).astype(BF16)
        mask_t[:, at] = sens[at, :].T * alive

    fill(FILL[0])
    pl.semaphore_wait(barrier, len(peers))

    sent = []

    def go(copy):
        copy.start()
        sent.append(copy)
        return copy

    co_copies = {}
    for k in range(1, n_cell):
        co_copies[k] = go(remote(coords_ref, coords_all.at[cell], co, k, (tm, cell_at(k))))

    def block(t, c):
        return full.at[t * n_cell + c]

    cell_copies, x_copies, core_copies = {}, {}, {}

    def forward_x(src, k):
        for q in range(1, n_hi):
            x_copies[q, k] = go(remote(src, block(tm, cell_at(-k)), ax, q * n_cell + k, x_peer(q)))

    def forward_core(src, q, k):
        dst = block(hi_at(-q) * 2 + core, cell_at(-k))
        core_copies[q, k] = go(remote(src, dst, ap, q * n_cell + k, partner))

    if gather:
        for k in range(1, n_cell):
            cell_copies[k] = go(remote(duals_ref, block(tm, cell), ac, k, (tm, cell_at(k))))
        forward_x(duals_ref, 0)
        forward_core(duals_ref, 0, 0)
        full[tm * n_cell + cell] = duals_ref[...]

    fill(FILL[1])
    for k in range(1, n_cell):
        if gather:
            cell_copies[k].wait_recv()
            src = block(tm, cell_at(-k))
            forward_x(src, k)
            forward_core(src, 0, k)
    fill(FILL[2])
    if gather:
        for k in range(n_cell):
            for q in range(1, n_hi):
                x_copies[q, k].wait_recv()
                forward_core(block(hi_at(-q) * 2 + core, cell_at(-k)), q, k)
    for k in range(1, n_cell):
        co_copies[k].wait_recv()
    if gather:
        for k in range(n_cell):
            for q in range(n_hi):
                core_copies[q, k].wait_recv()

    bx_copies, bp_copies = {}, {}
    for h in range(HALVES):
        at = slice(h * half, (h + 1) * half)
        everything = full[...].reshape(obs, LANES) if gather else duals_ref[...]
        adj[tm, at, :] = jnp.dot(mask_t[at, :], everything, preferred_element_type=F32).astype(BF16)
        here = adj.at[tm, at]
        for q in range(1, n_hi):
            bx_copies[q, h] = go(remote(here, here, bx, q * HALVES + h, x_peer(q)))
        bp_copies[0, h] = go(remote(here, here, bp, h, partner))

    fill(FILL[3])
    for h in range(HALVES):
        for q in range(1, n_hi):
            bx_copies[q, h].wait_recv()
            got = adj.at[hi_at(-q) * 2 + core, h * half:(h + 1) * half]
            bp_copies[q, h] = go(remote(got, got, bp, q * HALVES + h, partner))
    fill(FILL[4])

    major = cell // 2
    place = jnp.where(cell % 2 == 0, major, n_cell - 1 - major)

    def cell_on(k):
        p = lax.rem(place + k + n_cell, n_cell)
        return jnp.where(p < n_cell // 2, p * 2, (n_cell - 1 - p) * 2 + 1)

    steps = n_cell // 2
    ring = {}

    def carries(way, step, h):
        return step < steps or (step == steps and (h < QUARTERS // 2) == (way > 0))

    def ring_send(way, step, h):
        if carries(way, step, h):
            part = held.at[cell_on(-way * (step - 1)), h * quarter:(h + 1) * quarter]
            sems = ring_r if way > 0 else ring_l
            ring[way, step, h] = go(remote(part, part, sems, step * QUARTERS + h, (tm, cell_on(way))))

    per_half = QUARTERS // HALVES
    for h in range(HALVES):
        at = slice(h * half, (h + 1) * half)
        for q in range(n_hi):
            bp_copies[q, h].wait_recv()
        mixed = cov_ref[tm, 0] * adj[0, at, :].astype(F32)
        for t in range(1, n_tm):
            mixed += cov_ref[tm, t] * adj[t, at, :].astype(F32)
        held[cell, at, :] = mixed.astype(BF16)
        for piece in range(h * per_half, (h + 1) * per_half):
            ring_send(1, 1, piece)
            ring_send(-1, 1, piece)

    def spread(c):
        return jnp.dot(cov_k[c], held[c], preferred_element_type=F32)

    def blocks(step):
        return [cell_on(-step), cell_on(step)] if step < steps else [cell_on(step)]

    acc[...] = spread(cell)
    for c in blocks(1):
        covariance_block(c)
    for step in range(1, steps + 1):
        for h in range(QUARTERS):
            for way in (1, -1):
                if carries(way, step, h):
                    ring[way, step, h].wait_recv()
                    ring_send(way, step + 1, h)
            if step < steps and h < len(blocks(step + 1)):
                covariance_block(blocks(step + 1)[h])
        for c in blocks(step):
            acc[...] += spread(c)
    fill(len(fillers))

    weighted = acc[...].astype(BF16)
    if scatter:
        span = rows * n_cell

        def product(t):
            at = pl.ds(pl.multiple_of(t * span, span), span)
            return jnp.dot(picked[at, :], weighted, preferred_element_type=F32)

        dp_copies, dx_copies, dc_copies = {}, {}, {}
        order = [*range(1, n_hi), 0]
        for q in order:
            core_out[q] = product(hi_at(q) * 2 + (1 - core)).astype(BF16)
            dp_copies[q] = go(remote(core_out.at[q], core_in.at[q], dp, q, partner))
        far = sorted(range(n_cell), key=lambda k: -min(k, n_cell - k))
        for q in order:
            summed = product(hi_at(q) * 2 + core)
            dp_copies[q].wait_recv()
            total[...] = (summed + core_in[q].astype(F32)).reshape(n_cell, rows, LANES)
            if q:
                for k in far:
                    c = cell_at(k)
                    x_out[q, c] = total[c].astype(BF16)
                    dx_copies[q, k] = go(remote(x_out.at[q, c], x_in.at[q, c], dx, q * n_cell + k, x_peer(q)))
        for k in far:
            c = cell_at(k)
            block_sum = total[c]
            for q in range(1, n_hi):
                dx_copies[q, k].wait_recv()
                block_sum += x_in[q, c].astype(F32)
            if k:
                cell_out[c] = block_sum.astype(BF16)
                dc_copies[k] = go(remote(cell_out.at[c], cell_in.at[k], dc, k, (tm, c)))
        result = block_sum
        for k in range(1, n_cell):
            dc_copies[k].wait_recv()
            result += cell_in[k].astype(F32)
        out_ref[...] = result
    else:
        for i in range(obs // PICK_ROWS):
            at = slice(i * PICK_ROWS, (i + 1) * PICK_ROWS)
            out_ref[at, :] = jnp.dot(picked[at, :], weighted, preferred_element_type=F32)

    for copy in sent:
        copy.wait_send()


def ring_program(n_tm, n_cell, sensitivity, duals, time_cov, cell_coords, obs_time, obs_owner):
    obs, _, cells = sensitivity.shape
    rows, reals = duals.shape
    n_hi = n_tm // 2
    inside = rows % 16 == 0
    if not inside:
        duals = lax.all_gather(duals, ("tm", "cell"), axis=0, tiled=True)
    span = rows * n_cell if inside else 16
    part = rows if inside else 16
    vmem = pl.BlockSpec(memory_space=pltpu.VMEM)

    def pair(count):
        return [pltpu.SemaphoreType.DMA((count,)), pltpu.SemaphoreType.DMA((count,))]

    steps = n_cell // 2 + 1
    out_rows = rows if inside else obs
    out = pl.pallas_call(
        functools.partial(ring_kernel, (n_hi, n_cell, inside, inside)),
        out_shape=jax.ShapeDtypeStruct((out_rows, reals), F32),
        in_specs=[
            pl.BlockSpec(memory_space=pl.ANY), vmem, pl.BlockSpec(memory_space=pltpu.SMEM), vmem, vmem, vmem,
        ],
        out_specs=vmem,
        scratch_shapes=[
            pltpu.VMEM((obs, cells), BF16),
            pltpu.VMEM((n_tm * n_cell if inside else 1, part, reals), BF16),
            pltpu.VMEM((n_cell, 2, cells), jnp.int32),
            pltpu.VMEM((cells, obs), BF16),
            pltpu.VMEM((obs, cells), BF16),
            pltpu.VMEM((cells, LANES), F32),
            pltpu.VMEM((cells, LANES), F32),
            pltpu.VMEM((obs, LANES), F32),
            pltpu.VMEM((1, obs), F32),
            pltpu.VMEM((n_cell, cells, cells), BF16),
            pltpu.VMEM((n_tm, cells, reals), BF16),
            pltpu.VMEM((n_cell, cells, reals), BF16),
            pltpu.VMEM((cells, reals), F32),
            pltpu.VMEM((n_hi, span, reals), BF16),
            pltpu.VMEM((n_hi, span, reals), BF16),
            pltpu.VMEM((n_hi, n_cell, part, reals), BF16),
            pltpu.VMEM((n_hi, n_cell, part, reals), BF16),
            pltpu.VMEM((n_cell, part, reals), F32),
            pltpu.VMEM((n_cell, part, reals), BF16),
            pltpu.VMEM((n_cell, part, reals), BF16),
            pltpu.SemaphoreType.DMA,
            *pair(n_cell), *pair(n_cell), *pair(n_hi * n_cell), *pair(n_hi * n_cell),
            *pair(n_hi * HALVES), *pair(n_hi * HALVES),
            *pair(steps * QUARTERS), *pair(steps * QUARTERS),
            *pair(n_hi), *pair(n_hi * n_cell), *pair(n_cell),
        ],
        compiler_params=pltpu.CompilerParams(
            collective_id=0, has_side_effects=True, vmem_limit_bytes=62 * 1024 * 1024
        ),
    )(
        sensitivity.reshape(obs, cells), duals, time_cov, cell_coords,
        obs_time.reshape(1, obs), obs_owner.reshape(1, obs),
    )
    if inside:
        return out
    return lax.psum_scatter(out, ("tm", "cell"), scatter_dimension=0, tiled=True)


GROUP = 4
PAD = GROUP - 1
TILE = 16


def field_kernel(
    cfg, sens_hbm, duals_hbm, cov_hbm, coords_hbm, time_hbm, owner_hbm, out_ref, *s
):
    n_hi, n_cell = cfg
    n_tm, n_z = 2 * n_hi, n_cell // 2
    (sens, duals_ref, cov_ref, coords_ref, time_ref, owner_ref, full, coords_all, mask_t, picked, own_b, ids,
     toeplitz, hot_t, hot, halves, row_hot, stage, tiles, fields, mixed, grid, acc, back, outs, returned, weighted,
     core_out, core_in, plane_out, plane_in, sums, z_out, z_in, local_sems, *pairs) = s
    cz, cy, az, ap, ac, ea, eb, dp, dx, dz = zip(pairs[0::2], pairs[1::2])
    obs, cells = sens.shape
    rows, reals = duals_ref.shape
    blocks = cells // LANES
    grid_rows = n_cell * cells // LANES
    duos = grid_rows // 2
    wide = 2 * LANES

    tm = lax.axis_index("tm")
    cell = lax.axis_index("cell")
    hi, core = tm // 2, tm % 2
    z, y = cell // 2, cell % 2
    partner = (hi * 2 + (1 - core), cell)
    me = tm * n_cell + cell
    plane = [(dx_, dy_) for dx_ in range(n_hi) for dy_ in range(2)]

    def z_at(k):
        return lax.rem(z + k + n_z, n_z)

    def tm_in(shift):
        return lax.rem(hi + shift[0], n_hi) * 2 + core

    def y_in(shift):
        return lax.rem(y + shift[1], 2)

    def z_peer(k):
        return (tm, z_at(k) * 2 + y)

    def plane_peer(shift):
        return (tm_in(shift), z * 2 + y_in(shift))

    def far_z(i):
        skew = jnp.where(2 * z < n_z - 1, n_z - 1 - 2 * z, 2 * z - (n_z - 1))
        reach = jnp.where(2 * z < n_z - 1, z, n_z - 1 - z)
        aside = jnp.where(2 * z < n_z - 1, n_z - 1 - i, i)
        turn = jnp.where(i < skew, 0, i - skew)
        gap = reach - turn // 2
        return jnp.where(i < skew, aside, z + jnp.where(turn % 2 == 0, gap, -gap))

    far_cells = [far_z(i) * 2 + lax.rem(y + f, 2) for i in range(n_z) for f in (1, 0)]
    shifts = [(fx, fc) for fx in (1, 0) for fc in (1, 0)]

    def tm_flip(shift):
        return lax.rem(hi + shift[0], n_hi) * 2 + lax.rem(core + shift[1], 2)

    def swap(src, dst, sems, there, here, device):
        send, recv = sems
        return pltpu.make_async_remote_copy(
            src_ref=src, dst_ref=dst, send_sem=send.at[there], recv_sem=recv.at[here],
            device_id=device, device_id_type=MESH,
        )

    barrier = pltpu.get_barrier_semaphore()
    peers = [z_peer(k) for k in range(1, n_z)] + [plane_peer(shift) for shift in plane[1:3]] + [partner]
    for peer in peers:
        pl.semaphore_signal(barrier, inc=1, device_id=peer, device_id_type=MESH)

    loads = [
        pltpu.make_async_copy(src, dst, local_sems.at[i])
        for i, (src, dst) in enumerate([
            (duals_hbm, duals_ref), (coords_hbm, coords_ref), (time_hbm, time_ref), (owner_hbm, owner_ref),
            (cov_hbm, cov_ref), (sens_hbm, sens),
        ])
    ]
    for load in loads:
        load.start()
    loads[0].wait()
    loads[1].wait()
    col_gap = (
        lax.broadcasted_iota(jnp.int32, (LANES, LANES), 0) - lax.broadcasted_iota(jnp.int32, (LANES, LANES), 1)
    ).astype(F32)
    col_gap = col_gap * col_gap
    grid[...] = jnp.zeros_like(grid)

    @pl.loop(0, grid_rows)
    def _(gap):
        row_gap = gap.astype(F32)
        distance = jnp.sqrt(row_gap * row_gap + col_gap)
        block = (jnp.exp(-distance / LSCALE) / (8.0 * LSCALE)).astype(BF16)
        toeplitz[grid_rows - 1 - gap] = block
        toeplitz[grid_rows - 1 + gap] = block

    pl.semaphore_wait(barrier, len(peers))

    sent = []

    def go(copy):
        copy.start()
        sent.append(copy)
        return copy

    def block_of(shift, k):
        return full.at[tm_in(shift) * n_cell + z_at(-k) * 2 + y_in(shift)]

    az_copies, ap_copies, ac_copies, cz_copies, cy_copies = {}, {}, {}, {}, {}

    def forward_plane(src, k, ways):
        for j, shift in reversed(list(enumerate(plane))):
            if j in ways:
                ap_copies[j, k] = go(remote(src, block_of((0, 0), k), ap, j * n_z + k, plane_peer(shift)))

    def forward_core(src, j, k):
        ac_copies[j, k] = go(remote(src, block_of(plane[j], k), ac, j * n_z + k, partner))

    for k in range(1, n_z):
        az_copies[k] = go(remote(duals_ref, block_of((0, 0), 0), az, k, z_peer(k)))
    forward_plane(duals_ref, 0, (1, 2))
    forward_core(duals_ref, 0, 0)
    for k in range(1, n_z):
        cz_copies[k] = go(remote(coords_ref, coords_all.at[cell], cz, k, z_peer(k)))
    cy_copies[0] = go(remote(coords_ref, coords_all.at[cell], cy, 0, plane_peer((0, 1))))
    full[me] = duals_ref[...]
    coords_all[cell] = coords_ref[...]

    loads[2].wait()
    loads[3].wait()
    own_b[...] = column_of(owner_ref[...].astype(F32))
    live = tm <= time_ref[...]
    ids[...] = jnp.where(live, lax.broadcasted_iota(jnp.int32, (1, obs), 1), -1).astype(F32)
    loads[4].wait()
    loads[5].wait()

    @pl.loop(0, obs // PICK_ROWS)
    def _(i):
        at = pl.ds(pl.multiple_of(i * PICK_ROWS, PICK_ROWS), PICK_ROWS)
        alive = jnp.where(ids[:, at] >= 0.0, 1.0, 0.0).astype(BF16)
        mask_t[:, at] = sens[at, :].T * alive

    def pick(i):
        at = slice(i * PICK_ROWS, (i + 1) * PICK_ROWS)
        owned = own_b[at, :]
        hits = [
            jnp.where(owned == ids[:, j * LANES:(j + 1) * LANES], 1.0, 0.0).astype(BF16)
            for j in range(obs // LANES)
        ]
        picked[at, :] = jnp.dot(
            jnp.concatenate(hits, axis=1), sens[...], preferred_element_type=F32
        ).astype(BF16)

    fillers = [functools.partial(pick, i) for i in range(obs // PICK_ROWS)]

    def fill(count):
        for _ in range(count):
            if fillers:
                fillers.pop(0)()

    fill(PLAN[0])
    ap_copies[1, 0].wait_recv()
    forward_plane(duals_ref, 0, (3,))
    forward_core(block_of(plane[1], 0), 1, 0)
    for k in range(1, n_z):
        az_copies[k].wait_recv()
        src = block_of((0, 0), k)
        forward_plane(src, k, (1, 2, 3))
        forward_core(src, 0, k)
    for k in range(1, n_z):
        cz_copies[k].wait_recv()
        got = coords_all.at[z_at(-k) * 2 + y]
        cy_copies[k] = go(remote(got, got, cy, k, plane_peer((0, 1))))

    fill(PLAN[1])
    for k in range(n_z):
        for j in range(1, len(plane)):
            if (j, k) != (1, 0):
                ap_copies[j, k].wait_recv()
                forward_core(block_of(plane[j], k), j, k)
    fill(PLAN[2])
    for k in range(n_z):
        for j in range(len(plane)):
            ac_copies[j, k].wait_recv()

    adjoint = jnp.dot(mask_t[...], full[...].reshape(obs, reals), preferred_element_type=F32)
    for b in range(blocks):
        stage[pl.ds(b, reals, stride=blocks), :] = adjoint[b * LANES:(b + 1) * LANES, :].T
    tiles[...] = stage[...].astype(BF16).reshape(tiles.shape)

    last = len(far_cells) - 1
    for i, c in enumerate(far_cells):
        for shift in shifts:
            if i < last or shift != (0, 0):
                t = tm_flip(shift)
                there = t * n_cell + c
                go(swap(tiles.at[there], fields.at[me], ea, there, me, (t, c)))
    fields[me] = tiles[me]

    for k in range(n_z):
        cy_copies[k].wait_recv()
    for k in range(n_cell):
        code = (coords_all[k, 0:1, :] & 1) * LANES + coords_all[k, 1:2, :]
        spots = lax.broadcasted_iota(jnp.int32, (wide, cells), 0)
        ones = jnp.where(spots == code, 1.0, 0.0).astype(BF16)
        hot_t[k] = ones
        hot[k] = ones.T
        halves[k] = coords_all[k, 0:1, :] >> 1
        duo = lax.broadcasted_iota(jnp.int32, (duos * TILE, cells), 0) // TILE
        row_hot[k] = jnp.where(duo == halves[k], 1.0, 0.0).astype(BF16)
    fill(PLAN[3])

    for i, c in reversed(list(enumerate(far_cells))):
        for shift in reversed(shifts):
            if i < last or shift != (0, 0):
                t = tm_flip(shift)
                there = t * n_cell + c
                swap(tiles.at[me], fields.at[there], ea, there, there, (t, c)).wait_recv()
        got = [fields[t * n_cell + c].astype(F32) for t in range(n_tm)]
        for t in range(n_tm):
            blend = cov_ref[t, 0] * got[0]
            for u in range(1, n_tm):
                blend += cov_ref[t, u] * got[u]
            mixed[i, t * TILE:(t + 1) * TILE, :] = blend
        x = jnp.concatenate(
            [mixed[i, pl.ds(b, TILE, stride=blocks), :].astype(BF16) for b in range(blocks)], axis=1
        )
        placed = (row_hot[c].reshape(duos, TILE, cells) * x[None]).reshape(duos * TILE, cells)
        term = jnp.dot(placed, hot[c], preferred_element_type=F32)
        if i == last:
            acc[...] = term
        else:
            acc[...] += term
    on_grid = acc[...]
    grid[PAD * TILE:(PAD + duos) * TILE, :] = on_grid.astype(BF16)

    def covariance(m):
        at = grid_rows - 1 - 2 * m
        left = toeplitz[at:at + 2].reshape(wide, LANES)
        right = toeplitz[at - 1:at + 1].reshape(wide, LANES)
        return jnp.concatenate([left, right], axis=1)

    spans = [list(range(m, min(m + GROUP, duos))) for m in range(1 - duos, duos, GROUP)]
    spans.sort(key=lambda span: 0 not in span)
    for span in spans:
        low, high = max(0, span[0]), min(duos, duos + span[-1])
        count = (high - low) * TILE
        lhs = jnp.concatenate(
            [grid[(PAD + low - m) * TILE:(PAD + low - m) * TILE + count, :] for m in span], axis=1
        )
        rhs = jnp.concatenate([covariance(m) for m in span], axis=0)
        term = jnp.dot(lhs, rhs, preferred_element_type=F32)
        at = slice(low * TILE, high * TILE)
        if 0 in span:
            acc[at, :] = term
        else:
            acc[at, :] += term

    smooth = acc[...].astype(BF16)
    for i, c in enumerate(far_cells):
        spread = jnp.dot(smooth, hot_t[c], preferred_element_type=F32)
        for b in range(blocks):
            lanes = slice(b * LANES, (b + 1) * LANES)
            half = halves[c, 0:1, lanes]
            found = spread[0:TILE, lanes]
            for d in range(1, duos):
                found = jnp.where(half == d, spread[d * TILE:(d + 1) * TILE, lanes], found)
            back[i, pl.ds(b, TILE, stride=blocks), :] = found
        for t in range(n_tm):
            outs[t * n_cell + c] = back[i, t * TILE:(t + 1) * TILE, :].astype(BF16)
        for shift in shifts:
            if i < last or shift != (0, 0):
                t = tm_flip(shift)
                there = t * n_cell + c
                go(swap(outs.at[there], returned.at[me], eb, there, me, (t, c)))
    returned[me] = outs[me]
    fill(len(fillers))
    for i, c in reversed(list(enumerate(far_cells))):
        for shift in shifts:
            if i < last or shift != (0, 0):
                t = tm_flip(shift)
                there = t * n_cell + c
                swap(outs.at[me], returned.at[there], eb, there, there, (t, c)).wait_recv()
    stage[...] = returned[...].reshape(stage.shape).astype(F32)
    for b in range(blocks):
        weighted[b * LANES:(b + 1) * LANES, :] = stage[pl.ds(b, reals, stride=blocks), :].T.astype(BF16)

    deep = 2 * rows

    def product(t, d):
        at = pl.ds(pl.multiple_of((t * n_cell + 2 * d) * rows, deep), deep)
        return jnp.dot(picked[at, :], weighted[...], preferred_element_type=F32).reshape(2, rows, reals)

    def chunk_z(i):
        between = 0 if i == 0 else jnp.where(i < z, i, i + 1)
        return jnp.where(z == 0, n_z - 1 - i, z if i == n_z - 1 else between)

    dp_copies, dx_copies = {}, {}
    for d in range(n_z):
        for h in range(n_hi):
            core_out[d, h] = product(h * 2 + (1 - core), chunk_z(d)).astype(BF16)
        dp_copies[d] = go(remote(core_out.at[d], core_in.at[d], dp, d, partner))
    for d in range(n_z):
        terms = [product(h * 2 + core, chunk_z(d)) for h in range(n_hi)]
        dp_copies[d].wait_recv()
        for h in range(n_hi):
            total = terms[h] + core_in[d, h].astype(F32)
            plane_out[d, h] = total.astype(BF16)
            sums[d, h] = total
        if d == 1:
            @pl.when(core == 1)
            def _():
                for j in (1,):
                    dx_copies[j, 0].wait_recv()

        for j, shift in reversed(list(enumerate(plane))):
            if j:
                src = plane_out.at[d, lax.rem(hi + shift[0], n_hi), y_in(shift)]
                dx_copies[j, d] = go(
                    remote(src, plane_in.at[d, j], dx, j * n_z + d, plane_peer(shift))
                )

    for d in range(n_z):
        part = sums[d, hi, y]
        if d == 0:
            @pl.when(core == 0)
            def _():
                for j in (1,):
                    dx_copies[j, d].wait_recv()

        for j in range(1, len(plane)):
            if d != 0 or j not in (1,):
                dx_copies[j, d].wait_recv()
            part += plane_in[d, j].astype(F32)
        if d < n_z - 1:
            z_out[d] = part.astype(BF16)
            go(swap(z_out.at[d], z_in.at[z], dz, d, z, (tm, chunk_z(d) * 2 + y)))

    result = part
    for i in range(1, n_z):
        there = z_at(i)
        swap(z_out.at[0], z_in.at[there], dz, 0, there, (tm, there * 2 + y)).wait_recv()
        result += z_in[there].astype(F32)
    out_ref[...] = result

    for copy in sent:
        copy.wait_send()


PLAN = (0, 1, 0, 2)


def field_program(n_tm, n_cell, sensitivity, duals, time_cov, cell_coords, obs_time, obs_owner):
    obs, _, cells = sensitivity.shape
    rows, reals = duals.shape
    n_hi = n_tm // 2
    devices = n_tm * n_cell
    blocks = cells // LANES
    grid_rows = n_cell * cells // LANES
    duos = grid_rows // 2
    n_z = n_cell // 2

    def pair(count):
        return [pltpu.SemaphoreType.DMA((count,)), pltpu.SemaphoreType.DMA((count,))]

    return pl.pallas_call(
        functools.partial(field_kernel, (n_hi, n_cell)),
        out_shape=jax.ShapeDtypeStruct((rows, reals), F32),
        in_specs=[pl.BlockSpec(memory_space=pltpu.HBM)] * 6,
        out_specs=pl.BlockSpec(memory_space=pltpu.VMEM),
        scratch_shapes=[
            pltpu.VMEM((obs, cells), BF16),
            pltpu.VMEM((rows, reals), BF16),
            pltpu.SMEM((n_tm, n_tm), F32),
            pltpu.VMEM((2, cells), jnp.int32),
            pltpu.VMEM((1, obs), jnp.int32),
            pltpu.VMEM((1, obs), jnp.int32),
            pltpu.VMEM((devices, rows, reals), BF16),
            pltpu.VMEM((n_cell, 2, cells), jnp.int32),
            pltpu.VMEM((cells, obs), BF16),
            pltpu.VMEM((obs, cells), BF16),
            pltpu.VMEM((obs, LANES), F32),
            pltpu.VMEM((1, obs), F32),
            pltpu.VMEM((2 * grid_rows - 1, LANES, LANES), BF16),
            pltpu.VMEM((n_cell, 2 * LANES, cells), BF16),
            pltpu.VMEM((n_cell, cells, 2 * LANES), BF16),
            pltpu.VMEM((n_cell, 1, cells), jnp.int32),
            pltpu.VMEM((n_cell, duos * TILE, cells), BF16),
            pltpu.VMEM((reals * blocks, LANES), F32),
            pltpu.VMEM((devices, TILE, LANES), BF16),
            pltpu.VMEM((devices, TILE, LANES), BF16),
            pltpu.VMEM((n_cell, n_tm * TILE, LANES), F32),
            pltpu.VMEM(((duos + 2 * PAD) * TILE, 2 * LANES), BF16),
            pltpu.VMEM((duos * TILE, 2 * LANES), F32),
            pltpu.VMEM((n_cell, n_tm * TILE, LANES), F32),
            pltpu.VMEM((devices, TILE, LANES), BF16),
            pltpu.VMEM((devices, TILE, LANES), BF16),
            pltpu.VMEM((cells, reals), BF16),
            pltpu.VMEM((n_z, n_hi, 2, rows, reals), BF16),
            pltpu.VMEM((n_z, n_hi, 2, rows, reals), BF16),
            pltpu.VMEM((n_z, n_hi, 2, rows, reals), BF16),
            pltpu.VMEM((n_z, 2 * n_hi, rows, reals), BF16),
            pltpu.VMEM((n_z, n_hi, 2, rows, reals), F32),
            pltpu.VMEM((n_z, rows, reals), BF16),
            pltpu.VMEM((n_z, rows, reals), BF16),
            pltpu.SemaphoreType.DMA((6,)),
            *pair(n_z), *pair(n_z), *pair(n_z), *pair(2 * n_hi * n_z), *pair(2 * n_hi * n_z),
            *pair(devices), *pair(devices),
            *pair(n_z), *pair(2 * n_hi * n_z), *pair(n_z),
        ],
        compiler_params=pltpu.CompilerParams(
            collective_id=0, has_side_effects=True, vmem_limit_bytes=40 * 1024 * 1024
        ),
    )(*[
        pltpu.with_memory_space_constraint(x, pltpu.HBM) for x in (
            sensitivity.reshape(obs, cells), duals, time_cov, cell_coords,
            obs_time.reshape(1, obs), obs_owner.reshape(1, obs),
        )
    ])


def per_device(n_tm, n_cell, sensitivity, duals, *rest):
    cells = sensitivity.shape[2]
    rows, reals = duals.shape
    devices = n_tm * n_cell
    per = reals // devices
    fits = (
        n_tm == 4 and n_cell % 2 == 0 and rows % TILE == 0 and reals == LANES and cells % LANES == 0 and reals % devices == 0
        and per * (cells // LANES) == TILE and per * n_tm == TILE and (n_cell * cells) % (2 * LANES) == 0
    )
    program = field_program if fits else ring_program
    return program(n_tm, n_cell, sensitivity, duals, *rest)


def solution(mesh):
    in_specs = (P(None, "tm", "cell"), P(("tm", "cell"), None), P(), P(None, "cell"), P(), P())
    out_specs = P(("tm", "cell"), None)
    return jax.shard_map(
        functools.partial(per_device, mesh.shape["tm"], mesh.shape["cell"]),
        mesh=mesh, in_specs=in_specs, out_specs=out_specs, check_vma=False,
    )
```

```python
import functools

import jax
import jax.numpy as jnp
from jax import lax
from jax.experimental import pallas as pl
from jax.experimental.pallas import tpu as pltpu
from jax.sharding import PartitionSpec as P

LSCALE = 4
LANES = 128
HALVES = 2
PICK_ROWS = 256
QUARTERS = 4
FILL = (0, 3, 3, 1, 1)
MESH = pl.DeviceIdType.MESH
BF16 = jnp.bfloat16
F32 = jnp.float32


def remote(src, dst, sems, index, device):
    send, recv = sems
    return pltpu.make_async_remote_copy(
        src_ref=src, dst_ref=dst, send_sem=send.at[index], recv_sem=recv.at[index],
        device_id=device, device_id_type=MESH,
    )


def column_of(row):
    return jnp.broadcast_to(row, (LANES, row.shape[1])).T


def ring_kernel(cfg, sens_hbm, duals_ref, cov_ref, coords_ref, time_ref, owner_ref, out_ref, *s):
    n_hi, n_cell, gather, scatter = cfg
    n_tm = 2 * n_hi
    (sens, full, coords_all, mask_t, picked, row_b, col_b, own_b, ids, cov_k, adj, held, acc,
     core_out, core_in, x_out, x_in, total, cell_out, cell_in, local_sem, *pairs) = s
    co, ac, ax, ap, bx, bp, ring_r, ring_l, dp, dx, dc = zip(pairs[0::2], pairs[1::2])
    obs, cells = sens.shape
    rows = duals_ref.shape[0]
    half = cells // HALVES
    quarter = cells // QUARTERS

    tm = lax.axis_index("tm")
    cell = lax.axis_index("cell")
    hi, core = tm // 2, tm % 2
    partner = (hi * 2 + (1 - core), cell)

    def hi_at(q):
        return lax.rem(hi + q + n_hi, n_hi)

    def x_peer(q):
        return (hi_at(q) * 2 + core, cell)

    def cell_at(k):
        return lax.rem(cell + k + n_cell, n_cell)

    load = pltpu.make_async_copy(sens_hbm, sens, local_sem)
    load.start()

    barrier = pltpu.get_barrier_semaphore()
    peers = [(tm, cell_at(k)) for k in range(1, n_cell)] + [x_peer(q) for q in range(1, n_hi)] + [partner]
    for peer in peers:
        pl.semaphore_signal(barrier, inc=1, device_id=peer, device_id_type=MESH)
    coords_all[cell] = coords_ref[...]
    row_b[...] = column_of(coords_ref[0:1, :].astype(F32))
    col_b[...] = column_of(coords_ref[1:2, :].astype(F32))
    own_b[...] = column_of(owner_ref[...].astype(F32))
    live = tm <= time_ref[...]
    ids[...] = jnp.where(live, lax.broadcasted_iota(jnp.int32, (1, obs), 1), -1).astype(F32)

    def covariance_block(c):
        @pl.loop(0, cells // LANES)
        def _(j):
            lanes = pl.ds(pl.multiple_of(j * LANES, LANES), LANES)
            row_gap = row_b[...] - coords_all[c, 0:1, lanes].astype(F32)
            col_gap = col_b[...] - coords_all[c, 1:2, lanes].astype(F32)
            distance = jnp.sqrt(row_gap * row_gap + col_gap * col_gap)
            cov_k[c, :, lanes] = (jnp.exp(-distance / LSCALE) / (8.0 * LSCALE)).astype(BF16)

    def pick(i):
        at = slice(i * PICK_ROWS, (i + 1) * PICK_ROWS)
        owned = own_b[at, :]
        hot = [
            jnp.where(owned == ids[:, j * LANES:(j + 1) * LANES], 1.0, 0.0).astype(BF16)
            for j in range(obs // LANES)
        ]
        picked[at, :] = jnp.dot(
            jnp.concatenate(hot, axis=1), sens[...], preferred_element_type=F32
        ).astype(BF16)

    fillers = [functools.partial(pick, i) for i in range(obs // PICK_ROWS)]

    def fill(count):
        for _ in range(count):
            if fillers:
                fillers.pop(0)()

    covariance_block(cell)
    load.wait()

    @pl.loop(0, obs // PICK_ROWS)
    def _(i):
        at = pl.ds(pl.multiple_of(i * PICK_ROWS, PICK_ROWS), PICK_ROWS)
        alive = jnp.where(ids[:, at] >= 0.0, 1.0, 0.0).astype(BF16)
        mask_t[:, at] = sens[at, :].T * alive

    fill(FILL[0])
    pl.semaphore_wait(barrier, len(peers))

    sent = []

    def go(copy):
        copy.start()
        sent.append(copy)
        return copy

    co_copies = {}
    for k in range(1, n_cell):
        co_copies[k] = go(remote(coords_ref, coords_all.at[cell], co, k, (tm, cell_at(k))))

    def block(t, c):
        return full.at[t * n_cell + c]

    cell_copies, x_copies, core_copies = {}, {}, {}

    def forward_x(src, k):
        for q in range(1, n_hi):
            x_copies[q, k] = go(remote(src, block(tm, cell_at(-k)), ax, q * n_cell + k, x_peer(q)))

    def forward_core(src, q, k):
        dst = block(hi_at(-q) * 2 + core, cell_at(-k))
        core_copies[q, k] = go(remote(src, dst, ap, q * n_cell + k, partner))

    if gather:
        for k in range(1, n_cell):
            cell_copies[k] = go(remote(duals_ref, block(tm, cell), ac, k, (tm, cell_at(k))))
        forward_x(duals_ref, 0)
        forward_core(duals_ref, 0, 0)
        full[tm * n_cell + cell] = duals_ref[...]

    fill(FILL[1])
    for k in range(1, n_cell):
        if gather:
            cell_copies[k].wait_recv()
            src = block(tm, cell_at(-k))
            forward_x(src, k)
            forward_core(src, 0, k)
    fill(FILL[2])
    if gather:
        for k in range(n_cell):
            for q in range(1, n_hi):
                x_copies[q, k].wait_recv()
                forward_core(block(hi_at(-q) * 2 + core, cell_at(-k)), q, k)
    for k in range(1, n_cell):
        co_copies[k].wait_recv()
    if gather:
        for k in range(n_cell):
            for q in range(n_hi):
                core_copies[q, k].wait_recv()

    bx_copies, bp_copies = {}, {}
    for h in range(HALVES):
        at = slice(h * half, (h + 1) * half)
        everything = full[...].reshape(obs, LANES) if gather else duals_ref[...]
        adj[tm, at, :] = jnp.dot(mask_t[at, :], everything, preferred_element_type=F32).astype(BF16)
        here = adj.at[tm, at]
        for q in range(1, n_hi):
            bx_copies[q, h] = go(remote(here, here, bx, q * HALVES + h, x_peer(q)))
        bp_copies[0, h] = go(remote(here, here, bp, h, partner))

    fill(FILL[3])
    for h in range(HALVES):
        for q in range(1, n_hi):
            bx_copies[q, h].wait_recv()
            got = adj.at[hi_at(-q) * 2 + core, h * half:(h + 1) * half]
            bp_copies[q, h] = go(remote(got, got, bp, q * HALVES + h, partner))
    fill(FILL[4])

    major = cell // 2
    place = jnp.where(cell % 2 == 0, major, n_cell - 1 - major)

    def cell_on(k):
        p = lax.rem(place + k + n_cell, n_cell)
        return jnp.where(p < n_cell // 2, p * 2, (n_cell - 1 - p) * 2 + 1)

    steps = n_cell // 2
    ring = {}

    def carries(way, step, h):
        return step < steps or (step == steps and (h < QUARTERS // 2) == (way > 0))

    def ring_send(way, step, h):
        if carries(way, step, h):
            part = held.at[cell_on(-way * (step - 1)), h * quarter:(h + 1) * quarter]
            sems = ring_r if way > 0 else ring_l
            ring[way, step, h] = go(remote(part, part, sems, step * QUARTERS + h, (tm, cell_on(way))))

    per_half = QUARTERS // HALVES
    for h in range(HALVES):
        at = slice(h * half, (h + 1) * half)
        for q in range(n_hi):
            bp_copies[q, h].wait_recv()
        mixed = cov_ref[tm, 0] * adj[0, at, :].astype(F32)
        for t in range(1, n_tm):
            mixed += cov_ref[tm, t] * adj[t, at, :].astype(F32)
        held[cell, at, :] = mixed.astype(BF16)
        for piece in range(h * per_half, (h + 1) * per_half):
            ring_send(1, 1, piece)
            ring_send(-1, 1, piece)

    def spread(c):
        return jnp.dot(cov_k[c], held[c], preferred_element_type=F32)

    def blocks(step):
        return [cell_on(-step), cell_on(step)] if step < steps else [cell_on(step)]

    acc[...] = spread(cell)
    for c in blocks(1):
        covariance_block(c)
    for step in range(1, steps + 1):
        for h in range(QUARTERS):
            for way in (1, -1):
                if carries(way, step, h):
                    ring[way, step, h].wait_recv()
                    ring_send(way, step + 1, h)
            if step < steps and h < len(blocks(step + 1)):
                covariance_block(blocks(step + 1)[h])
        for c in blocks(step):
            acc[...] += spread(c)
    fill(len(fillers))

    weighted = acc[...].astype(BF16)
    if scatter:
        span = rows * n_cell

        def product(t):
            at = pl.ds(pl.multiple_of(t * span, span), span)
            return jnp.dot(picked[at, :], weighted, preferred_element_type=F32)

        dp_copies, dx_copies, dc_copies = {}, {}, {}
        order = [*range(1, n_hi), 0]
        for q in order:
            core_out[q] = product(hi_at(q) * 2 + (1 - core)).astype(BF16)
            dp_copies[q] = go(remote(core_out.at[q], core_in.at[q], dp, q, partner))
        far = sorted(range(n_cell), key=lambda k: -min(k, n_cell - k))
        for q in order:
            summed = product(hi_at(q) * 2 + core)
            dp_copies[q].wait_recv()
            total[...] = (summed + core_in[q].astype(F32)).reshape(n_cell, rows, LANES)
            if q:
                for k in far:
                    c = cell_at(k)
                    x_out[q, c] = total[c].astype(BF16)
                    dx_copies[q, k] = go(remote(x_out.at[q, c], x_in.at[q, c], dx, q * n_cell + k, x_peer(q)))
        for k in far:
            c = cell_at(k)
            block_sum = total[c]
            for q in range(1, n_hi):
                dx_copies[q, k].wait_recv()
                block_sum += x_in[q, c].astype(F32)
            if k:
                cell_out[c] = block_sum.astype(BF16)
                dc_copies[k] = go(remote(cell_out.at[c], cell_in.at[k], dc, k, (tm, c)))
        result = block_sum
        for k in range(1, n_cell):
            dc_copies[k].wait_recv()
            result += cell_in[k].astype(F32)
        out_ref[...] = result
    else:
        for i in range(obs // PICK_ROWS):
            at = slice(i * PICK_ROWS, (i + 1) * PICK_ROWS)
            out_ref[at, :] = jnp.dot(picked[at, :], weighted, preferred_element_type=F32)

    for copy in sent:
        copy.wait_send()


def ring_program(n_tm, n_cell, sensitivity, duals, time_cov, cell_coords, obs_time, obs_owner):
    obs, _, cells = sensitivity.shape
    rows, reals = duals.shape
    n_hi = n_tm // 2
    inside = rows % 16 == 0
    if not inside:
        duals = lax.all_gather(duals, ("tm", "cell"), axis=0, tiled=True)
    span = rows * n_cell if inside else 16
    part = rows if inside else 16
    vmem = pl.BlockSpec(memory_space=pltpu.VMEM)

    def pair(count):
        return [pltpu.SemaphoreType.DMA((count,)), pltpu.SemaphoreType.DMA((count,))]

    steps = n_cell // 2 + 1
    out_rows = rows if inside else obs
    out = pl.pallas_call(
        functools.partial(ring_kernel, (n_hi, n_cell, inside, inside)),
        out_shape=jax.ShapeDtypeStruct((out_rows, reals), F32),
        in_specs=[
            pl.BlockSpec(memory_space=pl.ANY), vmem, pl.BlockSpec(memory_space=pltpu.SMEM), vmem, vmem, vmem,
        ],
        out_specs=vmem,
        scratch_shapes=[
            pltpu.VMEM((obs, cells), BF16),
            pltpu.VMEM((n_tm * n_cell if inside else 1, part, reals), BF16),
            pltpu.VMEM((n_cell, 2, cells), jnp.int32),
            pltpu.VMEM((cells, obs), BF16),
            pltpu.VMEM((obs, cells), BF16),
            pltpu.VMEM((cells, LANES), F32),
            pltpu.VMEM((cells, LANES), F32),
            pltpu.VMEM((obs, LANES), F32),
            pltpu.VMEM((1, obs), F32),
            pltpu.VMEM((n_cell, cells, cells), BF16),
            pltpu.VMEM((n_tm, cells, reals), BF16),
            pltpu.VMEM((n_cell, cells, reals), BF16),
            pltpu.VMEM((cells, reals), F32),
            pltpu.VMEM((n_hi, span, reals), BF16),
            pltpu.VMEM((n_hi, span, reals), BF16),
            pltpu.VMEM((n_hi, n_cell, part, reals), BF16),
            pltpu.VMEM((n_hi, n_cell, part, reals), BF16),
            pltpu.VMEM((n_cell, part, reals), F32),
            pltpu.VMEM((n_cell, part, reals), BF16),
            pltpu.VMEM((n_cell, part, reals), BF16),
            pltpu.SemaphoreType.DMA,
            *pair(n_cell), *pair(n_cell), *pair(n_hi * n_cell), *pair(n_hi * n_cell),
            *pair(n_hi * HALVES), *pair(n_hi * HALVES),
            *pair(steps * QUARTERS), *pair(steps * QUARTERS),
            *pair(n_hi), *pair(n_hi * n_cell), *pair(n_cell),
        ],
        compiler_params=pltpu.CompilerParams(
            collective_id=0, has_side_effects=True, vmem_limit_bytes=62 * 1024 * 1024
        ),
    )(
        sensitivity.reshape(obs, cells), duals, time_cov, cell_coords,
        obs_time.reshape(1, obs), obs_owner.reshape(1, obs),
    )
    if inside:
        return out
    return lax.psum_scatter(out, ("tm", "cell"), scatter_dimension=0, tiled=True)


GROUP = 4
PAD = GROUP - 1
TILE = 16


def field_kernel(
    cfg, sens_hbm, duals_hbm, cov_hbm, coords_hbm, time_hbm, owner_hbm, out_ref, *s
):
    n_hi, n_cell = cfg
    n_tm, n_z = 2 * n_hi, n_cell // 2
    (sens, duals_ref, cov_ref, coords_ref, time_ref, owner_ref, full, coords_all, mask_t, picked, own_b, ids,
     toeplitz, hot_t, hot, halves, row_hot, stage, tiles, fields, mixed, grid, acc, back, outs, returned, weighted,
     core_out, core_in, plane_out, plane_in, sums, z_out, z_in, local_sems, *pairs) = s
    cz, cy, az, ap, ac, ea, eb, dp, dx, dz = zip(pairs[0::2], pairs[1::2])
    obs, cells = sens.shape
    rows, reals = duals_ref.shape
    blocks = cells // LANES
    grid_rows = n_cell * cells // LANES
    duos = grid_rows // 2
    wide = 2 * LANES

    tm = lax.axis_index("tm")
    cell = lax.axis_index("cell")
    hi, core = tm // 2, tm % 2
    z, y = cell // 2, cell % 2
    partner = (hi * 2 + (1 - core), cell)
    me = tm * n_cell + cell
    plane = [(dx_, dy_) for dx_ in range(n_hi) for dy_ in range(2)]

    def z_at(k):
        return lax.rem(z + k + n_z, n_z)

    def tm_in(shift):
        return lax.rem(hi + shift[0], n_hi) * 2 + core

    def y_in(shift):
        return lax.rem(y + shift[1], 2)

    def z_peer(k):
        return (tm, z_at(k) * 2 + y)

    def plane_peer(shift):
        return (tm_in(shift), z * 2 + y_in(shift))

    def far_z(i):
        skew = jnp.where(2 * z < n_z - 1, n_z - 1 - 2 * z, 2 * z - (n_z - 1))
        reach = jnp.where(2 * z < n_z - 1, z, n_z - 1 - z)
        aside = jnp.where(2 * z < n_z - 1, n_z - 1 - i, i)
        turn = jnp.where(i < skew, 0, i - skew)
        gap = reach - turn // 2
        return jnp.where(i < skew, aside, z + jnp.where(turn % 2 == 0, gap, -gap))

    far_cells = [far_z(i) * 2 + lax.rem(y + f, 2) for i in range(n_z) for f in (1, 0)]
    shifts = [(fx, fc) for fx in (1, 0) for fc in (1, 0)]

    def tm_flip(shift):
        return lax.rem(hi + shift[0], n_hi) * 2 + lax.rem(core + shift[1], 2)

    def swap(src, dst, sems, there, here, device):
        send, recv = sems
        return pltpu.make_async_remote_copy(
            src_ref=src, dst_ref=dst, send_sem=send.at[there], recv_sem=recv.at[here],
            device_id=device, device_id_type=MESH,
        )

    barrier = pltpu.get_barrier_semaphore()
    peers = [z_peer(k) for k in range(1, n_z)] + [plane_peer(shift) for shift in plane[1:3]] + [partner]
    for peer in peers:
        pl.semaphore_signal(barrier, inc=1, device_id=peer, device_id_type=MESH)

    loads = [
        pltpu.make_async_copy(src, dst, local_sems.at[i])
        for i, (src, dst) in enumerate([
            (duals_hbm, duals_ref), (coords_hbm, coords_ref), (time_hbm, time_ref), (owner_hbm, owner_ref),
            (cov_hbm, cov_ref), (sens_hbm, sens),
        ])
    ]
    for load in loads:
        load.start()
    loads[0].wait()
    loads[1].wait()
    col_gap = (
        lax.broadcasted_iota(jnp.int32, (LANES, LANES), 0) - lax.broadcasted_iota(jnp.int32, (LANES, LANES), 1)
    ).astype(F32)
    col_gap = col_gap * col_gap
    grid[...] = jnp.zeros_like(grid)

    @pl.loop(0, grid_rows)
    def _(gap):
        row_gap = gap.astype(F32)
        distance = jnp.sqrt(row_gap * row_gap + col_gap)
        block = (jnp.exp(-distance / LSCALE) / (8.0 * LSCALE)).astype(BF16)
        toeplitz[grid_rows - 1 - gap] = block
        toeplitz[grid_rows - 1 + gap] = block

    pl.semaphore_wait(barrier, len(peers))

    sent = []

    def go(copy):
        copy.start()
        sent.append(copy)
        return copy

    def block_of(shift, k):
        return full.at[tm_in(shift) * n_cell + z_at(-k) * 2 + y_in(shift)]

    az_copies, ap_copies, ac_copies, cz_copies, cy_copies = {}, {}, {}, {}, {}

    def forward_plane(src, k, ways):
        for j, shift in reversed(list(enumerate(plane))):
            if j in ways:
                ap_copies[j, k] = go(remote(src, block_of((0, 0), k), ap, j * n_z + k, plane_peer(shift)))

    def forward_core(src, j, k):
        ac_copies[j, k] = go(remote(src, block_of(plane[j], k), ac, j * n_z + k, partner))

    for k in range(1, n_z):
        az_copies[k] = go(remote(duals_ref, block_of((0, 0), 0), az, k, z_peer(k)))
    forward_plane(duals_ref, 0, (1, 2))
    forward_core(duals_ref, 0, 0)
    for k in range(1, n_z):
        cz_copies[k] = go(remote(coords_ref, coords_all.at[cell], cz, k, z_peer(k)))
    cy_copies[0] = go(remote(coords_ref, coords_all.at[cell], cy, 0, plane_peer((0, 1))))
    full[me] = duals_ref[...]
    coords_all[cell] = coords_ref[...]

    loads[2].wait()
    loads[3].wait()
    own_b[...] = column_of(owner_ref[...].astype(F32))
    live = tm <= time_ref[...]
    ids[...] = jnp.where(live, lax.broadcasted_iota(jnp.int32, (1, obs), 1), -1).astype(F32)
    loads[4].wait()
    loads[5].wait()

    @pl.loop(0, obs // PICK_ROWS)
    def _(i):
        at = pl.ds(pl.multiple_of(i * PICK_ROWS, PICK_ROWS), PICK_ROWS)
        alive = jnp.where(ids[:, at] >= 0.0, 1.0, 0.0).astype(BF16)
        mask_t[:, at] = sens[at, :].T * alive

    def pick(i):
        at = slice(i * PICK_ROWS, (i + 1) * PICK_ROWS)
        owned = own_b[at, :]
        hits = [
            jnp.where(owned == ids[:, j * LANES:(j + 1) * LANES], 1.0, 0.0).astype(BF16)
            for j in range(obs // LANES)
        ]
        picked[at, :] = jnp.dot(
            jnp.concatenate(hits, axis=1), sens[...], preferred_element_type=F32
        ).astype(BF16)

    fillers = [functools.partial(pick, i) for i in range(obs // PICK_ROWS)]

    def fill(count):
        for _ in range(count):
            if fillers:
                fillers.pop(0)()

    fill(PLAN[0])
    ap_copies[1, 0].wait_recv()
    forward_plane(duals_ref, 0, (3,))
    forward_core(block_of(plane[1], 0), 1, 0)
    for k in range(1, n_z):
        az_copies[k].wait_recv()
        src = block_of((0, 0), k)
        forward_plane(src, k, (1, 2, 3))
        forward_core(src, 0, k)
    for k in range(1, n_z):
        cz_copies[k].wait_recv()
        got = coords_all.at[z_at(-k) * 2 + y]
        cy_copies[k] = go(remote(got, got, cy, k, plane_peer((0, 1))))

    fill(PLAN[1])
    for k in range(n_z):
        for j in range(1, len(plane)):
            if (j, k) != (1, 0):
                ap_copies[j, k].wait_recv()
                forward_core(block_of(plane[j], k), j, k)
    fill(PLAN[2])
    for k in range(n_z):
        for j in range(len(plane)):
            ac_copies[j, k].wait_recv()

    everything = full[...].reshape(obs, reals)
    for b in range(0, blocks, 2):
        adjoint = jnp.dot(mask_t[b * LANES:(b + 2) * LANES, :], everything, preferred_element_type=F32)
        for i in range(2):
            stage[pl.ds(b + i, reals, stride=blocks), :] = adjoint[i * LANES:(i + 1) * LANES, :].T
    tiles[...] = stage[...].astype(BF16).reshape(tiles.shape)

    last = len(far_cells) - 1
    for i, c in enumerate(far_cells):
        for shift in shifts:
            if i < last or shift != (0, 0):
                t = tm_flip(shift)
                there = t * n_cell + c
                go(swap(tiles.at[there], fields.at[me], ea, there, me, (t, c)))
    fields[me] = tiles[me]

    for k in range(n_z):
        cy_copies[k].wait_recv()
    for k in range(n_cell):
        code = (coords_all[k, 0:1, :] & 1) * LANES + coords_all[k, 1:2, :]
        spots = lax.broadcasted_iota(jnp.int32, (wide, cells), 0)
        ones = jnp.where(spots == code, 1.0, 0.0).astype(BF16)
        hot_t[k] = ones
        hot[k] = ones.T
        halves[k] = coords_all[k, 0:1, :] >> 1
        duo = lax.broadcasted_iota(jnp.int32, (duos * TILE, cells), 0) // TILE
        row_hot[k] = jnp.where(duo == halves[k], 1.0, 0.0).astype(BF16)
    fill(PLAN[3])

    for i, c in reversed(list(enumerate(far_cells))):
        for shift in reversed(shifts):
            if i < last or shift != (0, 0):
                t = tm_flip(shift)
                there = t * n_cell + c
                swap(tiles.at[me], fields.at[there], ea, there, there, (t, c)).wait_recv()
        got = [fields[t * n_cell + c].astype(F32) for t in range(n_tm)]
        for t in range(n_tm):
            blend = cov_ref[t, 0] * got[0]
            for u in range(1, n_tm):
                blend += cov_ref[t, u] * got[u]
            mixed[i, t * TILE:(t + 1) * TILE, :] = blend
        x = jnp.concatenate(
            [mixed[i, pl.ds(b, TILE, stride=blocks), :].astype(BF16) for b in range(blocks)], axis=1
        )
        placed = (row_hot[c].reshape(duos, TILE, cells) * x[None]).reshape(duos * TILE, cells)
        term = jnp.dot(placed, hot[c], preferred_element_type=F32)
        if i == last:
            acc[...] = term
        else:
            acc[...] += term
    on_grid = acc[...]
    grid[PAD * TILE:(PAD + duos) * TILE, :] = on_grid.astype(BF16)

    def covariance(m):
        at = grid_rows - 1 - 2 * m
        left = toeplitz[at:at + 2].reshape(wide, LANES)
        right = toeplitz[at - 1:at + 1].reshape(wide, LANES)
        return jnp.concatenate([left, right], axis=1)

    spans = [list(range(m, min(m + GROUP, duos))) for m in range(1 - duos, duos, GROUP)]
    spans.sort(key=lambda span: 0 not in span)
    for span in spans:
        low, high = max(0, span[0]), min(duos, duos + span[-1])
        count = (high - low) * TILE
        lhs = jnp.concatenate(
            [grid[(PAD + low - m) * TILE:(PAD + low - m) * TILE + count, :] for m in span], axis=1
        )
        rhs = jnp.concatenate([covariance(m) for m in span], axis=0)
        term = jnp.dot(lhs, rhs, preferred_element_type=F32)
        at = slice(low * TILE, high * TILE)
        if 0 in span:
            acc[at, :] = term
        else:
            acc[at, :] += term

    smooth = acc[...].astype(BF16)
    for i, c in enumerate(far_cells):
        spread = jnp.dot(smooth, hot_t[c], preferred_element_type=F32)
        for b in range(blocks):
            lanes = slice(b * LANES, (b + 1) * LANES)
            half = halves[c, 0:1, lanes]
            found = spread[0:TILE, lanes]
            for d in range(1, duos):
                found = jnp.where(half == d, spread[d * TILE:(d + 1) * TILE, lanes], found)
            back[i, pl.ds(b, TILE, stride=blocks), :] = found
        for t in range(n_tm):
            outs[t * n_cell + c] = back[i, t * TILE:(t + 1) * TILE, :].astype(BF16)
        for shift in shifts:
            if i < last or shift != (0, 0):
                t = tm_flip(shift)
                there = t * n_cell + c
                go(swap(outs.at[there], returned.at[me], eb, there, me, (t, c)))
    returned[me] = outs[me]
    fill(len(fillers))
    for i, c in reversed(list(enumerate(far_cells))):
        for shift in shifts:
            if i < last or shift != (0, 0):
                t = tm_flip(shift)
                there = t * n_cell + c
                swap(outs.at[me], returned.at[there], eb, there, there, (t, c)).wait_recv()
    stage[...] = returned[...].reshape(stage.shape).astype(F32)
    for b in range(blocks):
        weighted[b * LANES:(b + 1) * LANES, :] = stage[pl.ds(b, reals, stride=blocks), :].T.astype(BF16)

    deep = 2 * rows

    def product(t, d):
        at = pl.ds(pl.multiple_of((t * n_cell + 2 * d) * rows, deep), deep)
        return jnp.dot(picked[at, :], weighted[...], preferred_element_type=F32).reshape(2, rows, reals)

    def chunk_z(i):
        between = 0 if i == 0 else jnp.where(i < z, i, i + 1)
        return jnp.where(z == 0, n_z - 1 - i, z if i == n_z - 1 else between)

    dp_copies, dx_copies = {}, {}
    for d in range(n_z):
        for h in range(n_hi):
            core_out[d, h] = product(h * 2 + (1 - core), chunk_z(d)).astype(BF16)
        dp_copies[d] = go(remote(core_out.at[d], core_in.at[d], dp, d, partner))
    for d in range(n_z):
        terms = [product(h * 2 + core, chunk_z(d)) for h in range(n_hi)]
        dp_copies[d].wait_recv()
        for h in range(n_hi):
            total = terms[h] + core_in[d, h].astype(F32)
            plane_out[d, h] = total.astype(BF16)
            sums[d, h] = total
        if d == 1:
            @pl.when(core == 1)
            def _():
                for j in (1,):
                    dx_copies[j, 0].wait_recv()

        for j, shift in reversed(list(enumerate(plane))):
            if j:
                src = plane_out.at[d, lax.rem(hi + shift[0], n_hi), y_in(shift)]
                dx_copies[j, d] = go(
                    remote(src, plane_in.at[d, j], dx, j * n_z + d, plane_peer(shift))
                )

    for d in range(n_z):
        part = sums[d, hi, y]
        if d == 0:
            @pl.when(core == 0)
            def _():
                for j in (1,):
                    dx_copies[j, d].wait_recv()

        for j in range(1, len(plane)):
            if d != 0 or j not in (1,):
                dx_copies[j, d].wait_recv()
            part += plane_in[d, j].astype(F32)
        if d < n_z - 1:
            z_out[d] = part.astype(BF16)
            go(swap(z_out.at[d], z_in.at[z], dz, d, z, (tm, chunk_z(d) * 2 + y)))

    result = part
    for i in range(1, n_z):
        there = z_at(i)
        swap(z_out.at[0], z_in.at[there], dz, 0, there, (tm, there * 2 + y)).wait_recv()
        result += z_in[there].astype(F32)
    out_ref[...] = result

    for copy in sent:
        copy.wait_send()


PLAN = (0, 1, 0, 2)


def field_program(n_tm, n_cell, sensitivity, duals, time_cov, cell_coords, obs_time, obs_owner):
    obs, _, cells = sensitivity.shape
    rows, reals = duals.shape
    n_hi = n_tm // 2
    devices = n_tm * n_cell
    blocks = cells // LANES
    grid_rows = n_cell * cells // LANES
    duos = grid_rows // 2
    n_z = n_cell // 2

    def pair(count):
        return [pltpu.SemaphoreType.DMA((count,)), pltpu.SemaphoreType.DMA((count,))]

    return pl.pallas_call(
        functools.partial(field_kernel, (n_hi, n_cell)),
        out_shape=jax.ShapeDtypeStruct((rows, reals), F32),
        in_specs=[pl.BlockSpec(memory_space=pltpu.HBM)] * 6,
        out_specs=pl.BlockSpec(memory_space=pltpu.VMEM),
        scratch_shapes=[
            pltpu.VMEM((obs, cells), BF16),
            pltpu.VMEM((rows, reals), BF16),
            pltpu.SMEM((n_tm, n_tm), F32),
            pltpu.VMEM((2, cells), jnp.int32),
            pltpu.VMEM((1, obs), jnp.int32),
            pltpu.VMEM((1, obs), jnp.int32),
            pltpu.VMEM((devices, rows, reals), BF16),
            pltpu.VMEM((n_cell, 2, cells), jnp.int32),
            pltpu.VMEM((cells, obs), BF16),
            pltpu.VMEM((obs, cells), BF16),
            pltpu.VMEM((obs, LANES), F32),
            pltpu.VMEM((1, obs), F32),
            pltpu.VMEM((2 * grid_rows - 1, LANES, LANES), BF16),
            pltpu.VMEM((n_cell, 2 * LANES, cells), BF16),
            pltpu.VMEM((n_cell, cells, 2 * LANES), BF16),
            pltpu.VMEM((n_cell, 1, cells), jnp.int32),
            pltpu.VMEM((n_cell, duos * TILE, cells), BF16),
            pltpu.VMEM((reals * blocks, LANES), F32),
            pltpu.VMEM((devices, TILE, LANES), BF16),
            pltpu.VMEM((devices, TILE, LANES), BF16),
            pltpu.VMEM((n_cell, n_tm * TILE, LANES), F32),
            pltpu.VMEM(((duos + 2 * PAD) * TILE, 2 * LANES), BF16),
            pltpu.VMEM((duos * TILE, 2 * LANES), F32),
            pltpu.VMEM((n_cell, n_tm * TILE, LANES), F32),
            pltpu.VMEM((devices, TILE, LANES), BF16),
            pltpu.VMEM((devices, TILE, LANES), BF16),
            pltpu.VMEM((cells, reals), BF16),
            pltpu.VMEM((n_z, n_hi, 2, rows, reals), BF16),
            pltpu.VMEM((n_z, n_hi, 2, rows, reals), BF16),
            pltpu.VMEM((n_z, n_hi, 2, rows, reals), BF16),
            pltpu.VMEM((n_z, 2 * n_hi, rows, reals), BF16),
            pltpu.VMEM((n_z, n_hi, 2, rows, reals), F32),
            pltpu.VMEM((n_z, rows, reals), BF16),
            pltpu.VMEM((n_z, rows, reals), BF16),
            pltpu.SemaphoreType.DMA((6,)),
            *pair(n_z), *pair(n_z), *pair(n_z), *pair(2 * n_hi * n_z), *pair(2 * n_hi * n_z),
            *pair(devices), *pair(devices),
            *pair(n_z), *pair(2 * n_hi * n_z), *pair(n_z),
        ],
        compiler_params=pltpu.CompilerParams(
            collective_id=0, has_side_effects=True, vmem_limit_bytes=40 * 1024 * 1024
        ),
    )(*[
        pltpu.with_memory_space_constraint(x, pltpu.HBM) for x in (
            sensitivity.reshape(obs, cells), duals, time_cov, cell_coords,
            obs_time.reshape(1, obs), obs_owner.reshape(1, obs),
        )
    ])


def per_device(n_tm, n_cell, sensitivity, duals, *rest):
    cells = sensitivity.shape[2]
    rows, reals = duals.shape
    devices = n_tm * n_cell
    per = reals // devices
    fits = (
        n_tm == 4 and n_cell % 2 == 0 and rows % TILE == 0 and reals == LANES and cells % LANES == 0 and reals % devices == 0
        and per * (cells // LANES) == TILE and per * n_tm == TILE and (n_cell * cells) % (2 * LANES) == 0
    )
    program = field_program if fits else ring_program
    return program(n_tm, n_cell, sensitivity, duals, *rest)


def solution(mesh):
    in_specs = (P(None, "tm", "cell"), P(("tm", "cell"), None), P(), P(None, "cell"), P(), P())
    out_specs = P(("tm", "cell"), None)
    return jax.shard_map(
        functools.partial(per_device, mesh.shape["tm"], mesh.shape["cell"]),
        mesh=mesh, in_specs=in_specs, out_specs=out_specs, check_vma=False,
    )
```

```python
import functools

import jax
import jax.numpy as jnp
from jax import lax
from jax.experimental import pallas as pl
from jax.experimental.pallas import tpu as pltpu
from jax.sharding import PartitionSpec as P

LSCALE = 4
LANES = 128
HALVES = 2
PICK_ROWS = 256
QUARTERS = 4
FILL = (0, 3, 3, 1, 1)
MESH = pl.DeviceIdType.MESH
BF16 = jnp.bfloat16
F32 = jnp.float32


def remote(src, dst, sems, index, device):
    send, recv = sems
    return pltpu.make_async_remote_copy(
        src_ref=src, dst_ref=dst, send_sem=send.at[index], recv_sem=recv.at[index],
        device_id=device, device_id_type=MESH,
    )


def column_of(row):
    return jnp.broadcast_to(row, (LANES, row.shape[1])).T


def ring_kernel(cfg, sens_hbm, duals_ref, cov_ref, coords_ref, time_ref, owner_ref, out_ref, *s):
    n_hi, n_cell, gather, scatter = cfg
    n_tm = 2 * n_hi
    (sens, full, coords_all, mask_t, picked, row_b, col_b, own_b, ids, cov_k, adj, held, acc,
     core_out, core_in, x_out, x_in, total, cell_out, cell_in, local_sem, *pairs) = s
    co, ac, ax, ap, bx, bp, ring_r, ring_l, dp, dx, dc = zip(pairs[0::2], pairs[1::2])
    obs, cells = sens.shape
    rows = duals_ref.shape[0]
    half = cells // HALVES
    quarter = cells // QUARTERS

    tm = lax.axis_index("tm")
    cell = lax.axis_index("cell")
    hi, core = tm // 2, tm % 2
    partner = (hi * 2 + (1 - core), cell)

    def hi_at(q):
        return lax.rem(hi + q + n_hi, n_hi)

    def x_peer(q):
        return (hi_at(q) * 2 + core, cell)

    def cell_at(k):
        return lax.rem(cell + k + n_cell, n_cell)

    load = pltpu.make_async_copy(sens_hbm, sens, local_sem)
    load.start()

    barrier = pltpu.get_barrier_semaphore()
    peers = [(tm, cell_at(k)) for k in range(1, n_cell)] + [x_peer(q) for q in range(1, n_hi)] + [partner]
    for peer in peers:
        pl.semaphore_signal(barrier, inc=1, device_id=peer, device_id_type=MESH)
    coords_all[cell] = coords_ref[...]
    row_b[...] = column_of(coords_ref[0:1, :].astype(F32))
    col_b[...] = column_of(coords_ref[1:2, :].astype(F32))
    own_b[...] = column_of(owner_ref[...].astype(F32))
    live = tm <= time_ref[...]
    ids[...] = jnp.where(live, lax.broadcasted_iota(jnp.int32, (1, obs), 1), -1).astype(F32)

    def covariance_block(c):
        @pl.loop(0, cells // LANES)
        def _(j):
            lanes = pl.ds(pl.multiple_of(j * LANES, LANES), LANES)
            row_gap = row_b[...] - coords_all[c, 0:1, lanes].astype(F32)
            col_gap = col_b[...] - coords_all[c, 1:2, lanes].astype(F32)
            distance = jnp.sqrt(row_gap * row_gap + col_gap * col_gap)
            cov_k[c, :, lanes] = (jnp.exp(-distance / LSCALE) / (8.0 * LSCALE)).astype(BF16)

    def pick(i):
        at = slice(i * PICK_ROWS, (i + 1) * PICK_ROWS)
        owned = own_b[at, :]
        hot = [
            jnp.where(owned == ids[:, j * LANES:(j + 1) * LANES], 1.0, 0.0).astype(BF16)
            for j in range(obs // LANES)
        ]
        picked[at, :] = jnp.dot(
            jnp.concatenate(hot, axis=1), sens[...], preferred_element_type=F32
        ).astype(BF16)

    fillers = [functools.partial(pick, i) for i in range(obs // PICK_ROWS)]

    def fill(count):
        for _ in range(count):
            if fillers:
                fillers.pop(0)()

    covariance_block(cell)
    load.wait()

    @pl.loop(0, obs // PICK_ROWS)
    def _(i):
        at = pl.ds(pl.multiple_of(i * PICK_ROWS, PICK_ROWS), PICK_ROWS)
        alive = jnp.where(ids[:, at] >= 0.0, 1.0, 0.0).astype(BF16)
        mask_t[:, at] = sens[at, :].T * alive

    fill(FILL[0])
    pl.semaphore_wait(barrier, len(peers))

    sent = []

    def go(copy):
        copy.start()
        sent.append(copy)
        return copy

    co_copies = {}
    for k in range(1, n_cell):
        co_copies[k] = go(remote(coords_ref, coords_all.at[cell], co, k, (tm, cell_at(k))))

    def block(t, c):
        return full.at[t * n_cell + c]

    cell_copies, x_copies, core_copies = {}, {}, {}

    def forward_x(src, k):
        for q in range(1, n_hi):
            x_copies[q, k] = go(remote(src, block(tm, cell_at(-k)), ax, q * n_cell + k, x_peer(q)))

    def forward_core(src, q, k):
        dst = block(hi_at(-q) * 2 + core, cell_at(-k))
        core_copies[q, k] = go(remote(src, dst, ap, q * n_cell + k, partner))

    if gather:
        for k in range(1, n_cell):
            cell_copies[k] = go(remote(duals_ref, block(tm, cell), ac, k, (tm, cell_at(k))))
        forward_x(duals_ref, 0)
        forward_core(duals_ref, 0, 0)
        full[tm * n_cell + cell] = duals_ref[...]

    fill(FILL[1])
    for k in range(1, n_cell):
        if gather:
            cell_copies[k].wait_recv()
            src = block(tm, cell_at(-k))
            forward_x(src, k)
            forward_core(src, 0, k)
    fill(FILL[2])
    if gather:
        for k in range(n_cell):
            for q in range(1, n_hi):
                x_copies[q, k].wait_recv()
                forward_core(block(hi_at(-q) * 2 + core, cell_at(-k)), q, k)
    for k in range(1, n_cell):
        co_copies[k].wait_recv()
    if gather:
        for k in range(n_cell):
            for q in range(n_hi):
                core_copies[q, k].wait_recv()

    bx_copies, bp_copies = {}, {}
    for h in range(HALVES):
        at = slice(h * half, (h + 1) * half)
        everything = full[...].reshape(obs, LANES) if gather else duals_ref[...]
        adj[tm, at, :] = jnp.dot(mask_t[at, :], everything, preferred_element_type=F32).astype(BF16)
        here = adj.at[tm, at]
        for q in range(1, n_hi):
            bx_copies[q, h] = go(remote(here, here, bx, q * HALVES + h, x_peer(q)))
        bp_copies[0, h] = go(remote(here, here, bp, h, partner))

    fill(FILL[3])
    for h in range(HALVES):
        for q in range(1, n_hi):
            bx_copies[q, h].wait_recv()
            got = adj.at[hi_at(-q) * 2 + core, h * half:(h + 1) * half]
            bp_copies[q, h] = go(remote(got, got, bp, q * HALVES + h, partner))
    fill(FILL[4])

    major = cell // 2
    place = jnp.where(cell % 2 == 0, major, n_cell - 1 - major)

    def cell_on(k):
        p = lax.rem(place + k + n_cell, n_cell)
        return jnp.where(p < n_cell // 2, p * 2, (n_cell - 1 - p) * 2 + 1)

    steps = n_cell // 2
    ring = {}

    def carries(way, step, h):
        return step < steps or (step == steps and (h < QUARTERS // 2) == (way > 0))

    def ring_send(way, step, h):
        if carries(way, step, h):
            part = held.at[cell_on(-way * (step - 1)), h * quarter:(h + 1) * quarter]
            sems = ring_r if way > 0 else ring_l
            ring[way, step, h] = go(remote(part, part, sems, step * QUARTERS + h, (tm, cell_on(way))))

    per_half = QUARTERS // HALVES
    for h in range(HALVES):
        at = slice(h * half, (h + 1) * half)
        for q in range(n_hi):
            bp_copies[q, h].wait_recv()
        mixed = cov_ref[tm, 0] * adj[0, at, :].astype(F32)
        for t in range(1, n_tm):
            mixed += cov_ref[tm, t] * adj[t, at, :].astype(F32)
        held[cell, at, :] = mixed.astype(BF16)
        for piece in range(h * per_half, (h + 1) * per_half):
            ring_send(1, 1, piece)
            ring_send(-1, 1, piece)

    def spread(c):
        return jnp.dot(cov_k[c], held[c], preferred_element_type=F32)

    def blocks(step):
        return [cell_on(-step), cell_on(step)] if step < steps else [cell_on(step)]

    acc[...] = spread(cell)
    for c in blocks(1):
        covariance_block(c)
    for step in range(1, steps + 1):
        for h in range(QUARTERS):
            for way in (1, -1):
                if carries(way, step, h):
                    ring[way, step, h].wait_recv()
                    ring_send(way, step + 1, h)
            if step < steps and h < len(blocks(step + 1)):
                covariance_block(blocks(step + 1)[h])
        for c in blocks(step):
            acc[...] += spread(c)
    fill(len(fillers))

    weighted = acc[...].astype(BF16)
    if scatter:
        span = rows * n_cell

        def product(t):
            at = pl.ds(pl.multiple_of(t * span, span), span)
            return jnp.dot(picked[at, :], weighted, preferred_element_type=F32)

        dp_copies, dx_copies, dc_copies = {}, {}, {}
        order = [*range(1, n_hi), 0]
        for q in order:
            core_out[q] = product(hi_at(q) * 2 + (1 - core)).astype(BF16)
            dp_copies[q] = go(remote(core_out.at[q], core_in.at[q], dp, q, partner))
        far = sorted(range(n_cell), key=lambda k: -min(k, n_cell - k))
        for q in order:
            summed = product(hi_at(q) * 2 + core)
            dp_copies[q].wait_recv()
            total[...] = (summed + core_in[q].astype(F32)).reshape(n_cell, rows, LANES)
            if q:
                for k in far:
                    c = cell_at(k)
                    x_out[q, c] = total[c].astype(BF16)
                    dx_copies[q, k] = go(remote(x_out.at[q, c], x_in.at[q, c], dx, q * n_cell + k, x_peer(q)))
        for k in far:
            c = cell_at(k)
            block_sum = total[c]
            for q in range(1, n_hi):
                dx_copies[q, k].wait_recv()
                block_sum += x_in[q, c].astype(F32)
            if k:
                cell_out[c] = block_sum.astype(BF16)
                dc_copies[k] = go(remote(cell_out.at[c], cell_in.at[k], dc, k, (tm, c)))
        result = block_sum
        for k in range(1, n_cell):
            dc_copies[k].wait_recv()
            result += cell_in[k].astype(F32)
        out_ref[...] = result
    else:
        for i in range(obs // PICK_ROWS):
            at = slice(i * PICK_ROWS, (i + 1) * PICK_ROWS)
            out_ref[at, :] = jnp.dot(picked[at, :], weighted, preferred_element_type=F32)

    for copy in sent:
        copy.wait_send()


def ring_program(n_tm, n_cell, sensitivity, duals, time_cov, cell_coords, obs_time, obs_owner):
    obs, _, cells = sensitivity.shape
    rows, reals = duals.shape
    n_hi = n_tm // 2
    inside = rows % 16 == 0
    if not inside:
        duals = lax.all_gather(duals, ("tm", "cell"), axis=0, tiled=True)
    span = rows * n_cell if inside else 16
    part = rows if inside else 16
    vmem = pl.BlockSpec(memory_space=pltpu.VMEM)

    def pair(count):
        return [pltpu.SemaphoreType.DMA((count,)), pltpu.SemaphoreType.DMA((count,))]

    steps = n_cell // 2 + 1
    out_rows = rows if inside else obs
    out = pl.pallas_call(
        functools.partial(ring_kernel, (n_hi, n_cell, inside, inside)),
        out_shape=jax.ShapeDtypeStruct((out_rows, reals), F32),
        in_specs=[
            pl.BlockSpec(memory_space=pl.ANY), vmem, pl.BlockSpec(memory_space=pltpu.SMEM), vmem, vmem, vmem,
        ],
        out_specs=vmem,
        scratch_shapes=[
            pltpu.VMEM((obs, cells), BF16),
            pltpu.VMEM((n_tm * n_cell if inside else 1, part, reals), BF16),
            pltpu.VMEM((n_cell, 2, cells), jnp.int32),
            pltpu.VMEM((cells, obs), BF16),
            pltpu.VMEM((obs, cells), BF16),
            pltpu.VMEM((cells, LANES), F32),
            pltpu.VMEM((cells, LANES), F32),
            pltpu.VMEM((obs, LANES), F32),
            pltpu.VMEM((1, obs), F32),
            pltpu.VMEM((n_cell, cells, cells), BF16),
            pltpu.VMEM((n_tm, cells, reals), BF16),
            pltpu.VMEM((n_cell, cells, reals), BF16),
            pltpu.VMEM((cells, reals), F32),
            pltpu.VMEM((n_hi, span, reals), BF16),
            pltpu.VMEM((n_hi, span, reals), BF16),
            pltpu.VMEM((n_hi, n_cell, part, reals), BF16),
            pltpu.VMEM((n_hi, n_cell, part, reals), BF16),
            pltpu.VMEM((n_cell, part, reals), F32),
            pltpu.VMEM((n_cell, part, reals), BF16),
            pltpu.VMEM((n_cell, part, reals), BF16),
            pltpu.SemaphoreType.DMA,
            *pair(n_cell), *pair(n_cell), *pair(n_hi * n_cell), *pair(n_hi * n_cell),
            *pair(n_hi * HALVES), *pair(n_hi * HALVES),
            *pair(steps * QUARTERS), *pair(steps * QUARTERS),
            *pair(n_hi), *pair(n_hi * n_cell), *pair(n_cell),
        ],
        compiler_params=pltpu.CompilerParams(
            collective_id=0, has_side_effects=True, vmem_limit_bytes=62 * 1024 * 1024
        ),
    )(
        sensitivity.reshape(obs, cells), duals, time_cov, cell_coords,
        obs_time.reshape(1, obs), obs_owner.reshape(1, obs),
    )
    if inside:
        return out
    return lax.psum_scatter(out, ("tm", "cell"), scatter_dimension=0, tiled=True)


GROUP = 4
PAD = GROUP - 1
TILE = 16


def field_kernel(
    cfg, sens_hbm, duals_hbm, cov_hbm, coords_hbm, time_hbm, owner_hbm, out_ref, *s
):
    n_hi, n_cell = cfg
    n_tm, n_z = 2 * n_hi, n_cell // 2
    (sens, duals_ref, cov_ref, coords_ref, time_ref, owner_ref, full, coords_all, mask_t, picked, own_b, ids,
     toeplitz, hot_t, hot, halves, row_hot, stage, tiles, fields, mixed, grid, acc, back, outs, returned, weighted,
     core_out, core_in, plane_out, plane_in, sums, z_out, z_in, local_sems, *pairs) = s
    cz, cy, az, ap, ac, ea, eb, dp, dx, dz = zip(pairs[0::2], pairs[1::2])
    obs, cells = sens.shape
    rows, reals = duals_ref.shape
    blocks = cells // LANES
    grid_rows = n_cell * cells // LANES
    duos = grid_rows // 2
    wide = 2 * LANES

    tm = lax.axis_index("tm")
    cell = lax.axis_index("cell")
    hi, core = tm // 2, tm % 2
    z, y = cell // 2, cell % 2
    partner = (hi * 2 + (1 - core), cell)
    me = tm * n_cell + cell
    plane = [(dx_, dy_) for dx_ in range(n_hi) for dy_ in range(2)]

    def z_at(k):
        return lax.rem(z + k + n_z, n_z)

    def tm_in(shift):
        return lax.rem(hi + shift[0], n_hi) * 2 + core

    def y_in(shift):
        return lax.rem(y + shift[1], 2)

    def z_peer(k):
        return (tm, z_at(k) * 2 + y)

    def plane_peer(shift):
        return (tm_in(shift), z * 2 + y_in(shift))

    def far_z(i):
        skew = jnp.where(2 * z < n_z - 1, n_z - 1 - 2 * z, 2 * z - (n_z - 1))
        reach = jnp.where(2 * z < n_z - 1, z, n_z - 1 - z)
        aside = jnp.where(2 * z < n_z - 1, n_z - 1 - i, i)
        turn = jnp.where(i < skew, 0, i - skew)
        gap = reach - turn // 2
        return jnp.where(i < skew, aside, z + jnp.where(turn % 2 == 0, gap, -gap))

    far_cells = [far_z(i) * 2 + lax.rem(y + f, 2) for i in range(n_z) for f in (1, 0)]
    shifts = [(fx, fc) for fx in (1, 0) for fc in (1, 0)]

    def tm_flip(shift):
        return lax.rem(hi + shift[0], n_hi) * 2 + lax.rem(core + shift[1], 2)

    def swap(src, dst, sems, there, here, device):
        send, recv = sems
        return pltpu.make_async_remote_copy(
            src_ref=src, dst_ref=dst, send_sem=send.at[there], recv_sem=recv.at[here],
            device_id=device, device_id_type=MESH,
        )

    barrier = pltpu.get_barrier_semaphore()
    peers = [z_peer(k) for k in range(1, n_z)] + [plane_peer(shift) for shift in plane[1:3]] + [partner]
    for peer in peers:
        pl.semaphore_signal(barrier, inc=1, device_id=peer, device_id_type=MESH)

    loads = [
        pltpu.make_async_copy(src, dst, local_sems.at[i])
        for i, (src, dst) in enumerate([
            (duals_hbm, duals_ref), (coords_hbm, coords_ref), (time_hbm, time_ref), (owner_hbm, owner_ref),
            (cov_hbm, cov_ref), (sens_hbm, sens),
        ])
    ]
    for load in loads:
        load.start()
    loads[0].wait()
    loads[1].wait()
    col_gap = (
        lax.broadcasted_iota(jnp.int32, (LANES, LANES), 0) - lax.broadcasted_iota(jnp.int32, (LANES, LANES), 1)
    ).astype(F32)
    col_gap = col_gap * col_gap
    grid[...] = jnp.zeros_like(grid)

    @pl.loop(0, grid_rows)
    def _(gap):
        row_gap = gap.astype(F32)
        distance = jnp.sqrt(row_gap * row_gap + col_gap)
        block = (jnp.exp(-distance / LSCALE) / (8.0 * LSCALE)).astype(BF16)
        toeplitz[grid_rows - 1 - gap] = block
        toeplitz[grid_rows - 1 + gap] = block

    pl.semaphore_wait(barrier, len(peers))

    sent = []

    def go(copy):
        copy.start()
        sent.append(copy)
        return copy

    def block_of(shift, k):
        return full.at[tm_in(shift) * n_cell + z_at(-k) * 2 + y_in(shift)]

    az_copies, ap_copies, ac_copies, cz_copies, cy_copies = {}, {}, {}, {}, {}

    def forward_plane(src, k, ways):
        for j, shift in reversed(list(enumerate(plane))):
            if j in ways:
                ap_copies[j, k] = go(remote(src, block_of((0, 0), k), ap, j * n_z + k, plane_peer(shift)))

    def forward_core(src, j, k):
        ac_copies[j, k] = go(remote(src, block_of(plane[j], k), ac, j * n_z + k, partner))

    for k in range(1, n_z):
        az_copies[k] = go(remote(duals_ref, block_of((0, 0), 0), az, k, z_peer(k)))
    forward_plane(duals_ref, 0, (1, 2))
    forward_core(duals_ref, 0, 0)
    for k in range(1, n_z):
        cz_copies[k] = go(remote(coords_ref, coords_all.at[cell], cz, k, z_peer(k)))
    cy_copies[0] = go(remote(coords_ref, coords_all.at[cell], cy, 0, plane_peer((0, 1))))
    full[me] = duals_ref[...]
    coords_all[cell] = coords_ref[...]

    loads[2].wait()
    loads[3].wait()
    own_b[...] = column_of(owner_ref[...].astype(F32))
    live = tm <= time_ref[...]
    ids[...] = jnp.where(live, lax.broadcasted_iota(jnp.int32, (1, obs), 1), -1).astype(F32)
    loads[4].wait()
    loads[5].wait()

    @pl.loop(0, obs // PICK_ROWS)
    def _(i):
        at = pl.ds(pl.multiple_of(i * PICK_ROWS, PICK_ROWS), PICK_ROWS)
        alive = jnp.where(ids[:, at] >= 0.0, 1.0, 0.0).astype(BF16)
        mask_t[:, at] = sens[at, :].T * alive

    def pick(i):
        at = slice(i * PICK_ROWS, (i + 1) * PICK_ROWS)
        owned = own_b[at, :]
        hits = [
            jnp.where(owned == ids[:, j * LANES:(j + 1) * LANES], 1.0, 0.0).astype(BF16)
            for j in range(obs // LANES)
        ]
        picked[at, :] = jnp.dot(
            jnp.concatenate(hits, axis=1), sens[...], preferred_element_type=F32
        ).astype(BF16)

    fillers = [functools.partial(pick, i) for i in range(obs // PICK_ROWS)]

    def fill(count):
        for _ in range(count):
            if fillers:
                fillers.pop(0)()

    fill(PLAN[0])
    ap_copies[1, 0].wait_recv()
    forward_plane(duals_ref, 0, (3,))
    forward_core(block_of(plane[1], 0), 1, 0)
    for k in range(1, n_z):
        az_copies[k].wait_recv()
        src = block_of((0, 0), k)
        forward_plane(src, k, (1, 2, 3))
        forward_core(src, 0, k)
    for k in range(1, n_z):
        cz_copies[k].wait_recv()
        got = coords_all.at[z_at(-k) * 2 + y]
        cy_copies[k] = go(remote(got, got, cy, k, plane_peer((0, 1))))

    fill(PLAN[1])
    for k in range(n_z):
        for j in range(1, len(plane)):
            if (j, k) != (1, 0):
                ap_copies[j, k].wait_recv()
                forward_core(block_of(plane[j], k), j, k)
    fill(PLAN[2])
    for k in range(n_z):
        for j in range(len(plane)):
            ac_copies[j, k].wait_recv()

    everything = full[...].reshape(obs, reals)
    for b in range(0, blocks, 2):
        adjoint = jnp.dot(mask_t[b * LANES:(b + 2) * LANES, :], everything, preferred_element_type=F32)
        for i in range(2):
            stage[pl.ds(b + i, reals, stride=blocks), :] = adjoint[i * LANES:(i + 1) * LANES, :].T
    tiles[...] = stage[...].astype(BF16).reshape(tiles.shape)

    last = len(far_cells) - 1
    for i, c in enumerate(far_cells):
        for shift in shifts:
            if i < last or shift != (0, 0):
                t = tm_flip(shift)
                there = t * n_cell + c
                go(swap(tiles.at[there], fields.at[me], ea, there, me, (t, c)))
    fields[me] = tiles[me]

    for k in range(n_z):
        cy_copies[k].wait_recv()
    for k in range(n_cell):
        code = (coords_all[k, 0:1, :] & 1) * LANES + coords_all[k, 1:2, :]
        spots = lax.broadcasted_iota(jnp.int32, (wide, cells), 0)
        ones = jnp.where(spots == code, 1.0, 0.0).astype(BF16)
        hot_t[k] = ones
        hot[k] = ones.T
        halves[k] = coords_all[k, 0:1, :] >> 1
        duo = lax.broadcasted_iota(jnp.int32, (duos * TILE, cells), 0) // TILE
        row_hot[k] = jnp.where(duo == halves[k], 1.0, 0.0).astype(BF16)
    fill(PLAN[3])

    for i, c in reversed(list(enumerate(far_cells))):
        for shift in reversed(shifts):
            if i < last or shift != (0, 0):
                t = tm_flip(shift)
                there = t * n_cell + c
                swap(tiles.at[me], fields.at[there], ea, there, there, (t, c)).wait_recv()
        got = [fields[t * n_cell + c].astype(F32) for t in range(n_tm)]
        for t in range(n_tm):
            blend = cov_ref[t, 0] * got[0]
            for u in range(1, n_tm):
                blend += cov_ref[t, u] * got[u]
            mixed[i, t * TILE:(t + 1) * TILE, :] = blend
        x = jnp.concatenate(
            [mixed[i, pl.ds(b, TILE, stride=blocks), :].astype(BF16) for b in range(blocks)], axis=1
        )
        placed = (row_hot[c].reshape(duos, TILE, cells) * x[None]).reshape(duos * TILE, cells)
        term = jnp.dot(placed, hot[c], preferred_element_type=F32)
        if i == last:
            acc[...] = term
        else:
            acc[...] += term
    on_grid = acc[...]
    grid[PAD * TILE:(PAD + duos) * TILE, :] = on_grid.astype(BF16)

    def covariance(m):
        at = grid_rows - 1 - 2 * m
        left = toeplitz[at:at + 2].reshape(wide, LANES)
        right = toeplitz[at - 1:at + 1].reshape(wide, LANES)
        return jnp.concatenate([left, right], axis=1)

    spans = [list(range(m, min(m + GROUP, duos))) for m in range(1 - duos, duos, GROUP)]
    spans.sort(key=lambda span: 0 not in span)
    for span in spans:
        low, high = max(0, span[0]), min(duos, duos + span[-1])
        count = (high - low) * TILE
        lhs = jnp.concatenate(
            [grid[(PAD + low - m) * TILE:(PAD + low - m) * TILE + count, :] for m in span], axis=1
        )
        rhs = jnp.concatenate([covariance(m) for m in span], axis=0)
        term = jnp.dot(lhs, rhs, preferred_element_type=F32)
        at = slice(low * TILE, high * TILE)
        if 0 in span:
            acc[at, :] = term
        else:
            acc[at, :] += term

    smooth = acc[...].astype(BF16)
    for i, c in enumerate(far_cells):
        spread = jnp.dot(smooth, hot_t[c], preferred_element_type=F32)
        for b in range(blocks):
            lanes = slice(b * LANES, (b + 1) * LANES)
            half = halves[c, 0:1, lanes]
            found = spread[0:TILE, lanes]
            for d in range(1, duos):
                found = jnp.where(half == d, spread[d * TILE:(d + 1) * TILE, lanes], found)
            back[i, pl.ds(b, TILE, stride=blocks), :] = found
        for t in range(n_tm):
            outs[t * n_cell + c] = back[i, t * TILE:(t + 1) * TILE, :].astype(BF16)
        for shift in shifts:
            if i < last or shift != (0, 0):
                t = tm_flip(shift)
                there = t * n_cell + c
                go(swap(outs.at[there], returned.at[me], eb, there, me, (t, c)))
    returned[me] = outs[me]
    fill(len(fillers))
    for i, c in reversed(list(enumerate(far_cells))):
        for shift in shifts:
            if i < last or shift != (0, 0):
                t = tm_flip(shift)
                there = t * n_cell + c
                swap(outs.at[me], returned.at[there], eb, there, there, (t, c)).wait_recv()
    stage[...] = returned[...].reshape(stage.shape).astype(F32)
    for b in range(blocks):
        weighted[b * LANES:(b + 1) * LANES, :] = stage[pl.ds(b, reals, stride=blocks), :].T.astype(BF16)

    deep = 2 * rows

    def product(c, d):
        picks = []
        for h in range(n_hi):
            at = pl.ds(pl.multiple_of(((h * 2 + c) * n_cell + 2 * d) * rows, deep), deep)
            picks.append(picked[at, :])
        out = jnp.dot(jnp.concatenate(picks, axis=0), weighted[...], preferred_element_type=F32)
        return out.reshape(n_hi, 2, rows, reals)

    def chunk_z(i):
        between = 0 if i == 0 else jnp.where(i < z, i, i + 1)
        return jnp.where(z == 0, n_z - 1 - i, z if i == n_z - 1 else between)

    dp_copies, dx_copies = {}, {}
    for d in range(n_z):
        core_out[d] = product(1 - core, chunk_z(d)).astype(BF16)
        dp_copies[d] = go(remote(core_out.at[d], core_in.at[d], dp, d, partner))
    for d in range(n_z):
        terms = product(core, chunk_z(d))
        dp_copies[d].wait_recv()
        for h in range(n_hi):
            total = terms[h] + core_in[d, h].astype(F32)
            plane_out[d, h] = total.astype(BF16)
            sums[d, h] = total
        if d == 1:
            @pl.when(core == 1)
            def _():
                for j in (1,):
                    dx_copies[j, 0].wait_recv()

        for j, shift in reversed(list(enumerate(plane))):
            if j:
                src = plane_out.at[d, lax.rem(hi + shift[0], n_hi), y_in(shift)]
                dx_copies[j, d] = go(
                    remote(src, plane_in.at[d, j], dx, j * n_z + d, plane_peer(shift))
                )

    for d in range(n_z):
        part = sums[d, hi, y]
        if d == 0:
            @pl.when(core == 0)
            def _():
                for j in (1,):
                    dx_copies[j, d].wait_recv()

        for j in range(1, len(plane)):
            if d != 0 or j not in (1,):
                dx_copies[j, d].wait_recv()
            part += plane_in[d, j].astype(F32)
        if d < n_z - 1:
            z_out[d] = part.astype(BF16)
            go(swap(z_out.at[d], z_in.at[z], dz, d, z, (tm, chunk_z(d) * 2 + y)))

    result = part
    for i in range(1, n_z):
        there = z_at(i)
        swap(z_out.at[0], z_in.at[there], dz, 0, there, (tm, there * 2 + y)).wait_recv()
        result += z_in[there].astype(F32)
    out_ref[...] = result

    for copy in sent:
        copy.wait_send()


PLAN = (0, 1, 0, 2)


def field_program(n_tm, n_cell, sensitivity, duals, time_cov, cell_coords, obs_time, obs_owner):
    obs, _, cells = sensitivity.shape
    rows, reals = duals.shape
    n_hi = n_tm // 2
    devices = n_tm * n_cell
    blocks = cells // LANES
    grid_rows = n_cell * cells // LANES
    duos = grid_rows // 2
    n_z = n_cell // 2

    def pair(count):
        return [pltpu.SemaphoreType.DMA((count,)), pltpu.SemaphoreType.DMA((count,))]

    return pl.pallas_call(
        functools.partial(field_kernel, (n_hi, n_cell)),
        out_shape=jax.ShapeDtypeStruct((rows, reals), F32),
        in_specs=[pl.BlockSpec(memory_space=pltpu.HBM)] * 6,
        out_specs=pl.BlockSpec(memory_space=pltpu.VMEM),
        scratch_shapes=[
            pltpu.VMEM((obs, cells), BF16),
            pltpu.VMEM((rows, reals), BF16),
            pltpu.SMEM((n_tm, n_tm), F32),
            pltpu.VMEM((2, cells), jnp.int32),
            pltpu.VMEM((1, obs), jnp.int32),
            pltpu.VMEM((1, obs), jnp.int32),
            pltpu.VMEM((devices, rows, reals), BF16),
            pltpu.VMEM((n_cell, 2, cells), jnp.int32),
            pltpu.VMEM((cells, obs), BF16),
            pltpu.VMEM((obs, cells), BF16),
            pltpu.VMEM((obs, LANES), F32),
            pltpu.VMEM((1, obs), F32),
            pltpu.VMEM((2 * grid_rows - 1, LANES, LANES), BF16),
            pltpu.VMEM((n_cell, 2 * LANES, cells), BF16),
            pltpu.VMEM((n_cell, cells, 2 * LANES), BF16),
            pltpu.VMEM((n_cell, 1, cells), jnp.int32),
            pltpu.VMEM((n_cell, duos * TILE, cells), BF16),
            pltpu.VMEM((reals * blocks, LANES), F32),
            pltpu.VMEM((devices, TILE, LANES), BF16),
            pltpu.VMEM((devices, TILE, LANES), BF16),
            pltpu.VMEM((n_cell, n_tm * TILE, LANES), F32),
            pltpu.VMEM(((duos + 2 * PAD) * TILE, 2 * LANES), BF16),
            pltpu.VMEM((duos * TILE, 2 * LANES), F32),
            pltpu.VMEM((n_cell, n_tm * TILE, LANES), F32),
            pltpu.VMEM((devices, TILE, LANES), BF16),
            pltpu.VMEM((devices, TILE, LANES), BF16),
            pltpu.VMEM((cells, reals), BF16),
            pltpu.VMEM((n_z, n_hi, 2, rows, reals), BF16),
            pltpu.VMEM((n_z, n_hi, 2, rows, reals), BF16),
            pltpu.VMEM((n_z, n_hi, 2, rows, reals), BF16),
            pltpu.VMEM((n_z, 2 * n_hi, rows, reals), BF16),
            pltpu.VMEM((n_z, n_hi, 2, rows, reals), F32),
            pltpu.VMEM((n_z, rows, reals), BF16),
            pltpu.VMEM((n_z, rows, reals), BF16),
            pltpu.SemaphoreType.DMA((6,)),
            *pair(n_z), *pair(n_z), *pair(n_z), *pair(2 * n_hi * n_z), *pair(2 * n_hi * n_z),
            *pair(devices), *pair(devices),
            *pair(n_z), *pair(2 * n_hi * n_z), *pair(n_z),
        ],
        compiler_params=pltpu.CompilerParams(
            collective_id=0, has_side_effects=True, vmem_limit_bytes=40 * 1024 * 1024
        ),
    )(*[
        pltpu.with_memory_space_constraint(x, pltpu.HBM) for x in (
            sensitivity.reshape(obs, cells), duals, time_cov, cell_coords,
            obs_time.reshape(1, obs), obs_owner.reshape(1, obs),
        )
    ])


def per_device(n_tm, n_cell, sensitivity, duals, *rest):
    cells = sensitivity.shape[2]
    rows, reals = duals.shape
    devices = n_tm * n_cell
    per = reals // devices
    fits = (
        n_tm == 4 and n_cell % 2 == 0 and rows % TILE == 0 and reals == LANES and cells % LANES == 0 and reals % devices == 0
        and per * (cells // LANES) == TILE and per * n_tm == TILE and (n_cell * cells) % (2 * LANES) == 0
    )
    program = field_program if fits else ring_program
    return program(n_tm, n_cell, sensitivity, duals, *rest)


def solution(mesh):
    in_specs = (P(None, "tm", "cell"), P(("tm", "cell"), None), P(), P(None, "cell"), P(), P())
    out_specs = P(("tm", "cell"), None)
    return jax.shard_map(
        functools.partial(per_device, mesh.shape["tm"], mesh.shape["cell"]),
        mesh=mesh, in_specs=in_specs, out_specs=out_specs, check_vma=False,
    )
```
